32 devices in a mesh: ctx: 8 (over z, x), tp: 4 (over y, core).
Axes of the slice: x: 2, y: 2, z: 4, core: 2. Of those that a mesh axis runs over, the one named last changes fastest.
Arguments:
- layer_input: bfloat16 [2048, 2048], P('ctx', 'tp'), may hold values from -6 to 6
- norm_gain: bfloat16 [2048], P('tp'), may hold values from 0.5 to 1.5
- norm_shift: bfloat16 [2048], P('tp'), may hold values from -3 to 3
- w_qkv: bfloat16 [2048, 3, 2048], P('ctx', None, 'tp'), may hold values from -1 to 1
- b_qkv: float32 [3, 2048], P(None, 'tp'), may hold values from -3 to 3
- w_out: bfloat16 [2048, 2048], P('tp', 'ctx'), may hold values from -0.125 to 0.125
- b_out: float32 [2048], P('tp'), may hold values from -3 to 3
- w_fc1: bfloat16 [2048, 8192], P('ctx', 'tp'), may hold values from -0.125 to 0.125
- b_fc1: float32 [8192], P('tp'), may hold values from -3 to 3
- w_fc2: bfloat16 [8192, 2048], P('tp', 'ctx'), may hold values from -0.0625 to 0.0625
- b_fc2: float32 [2048], P('tp'), may hold values from -3 to 3
- grad_output: bfloat16 [2048, 2048], P('ctx', 'tp'), may hold values from -6 to 6
- placement: int32 [16], replicated, may hold values from 0 to 15, as said below
- position_ids: int32 [2048], P('ctx'), may hold values from 0 to 4095
Outputs:
- layer_output: float32 [2048, 2048], P('ctx', 'tp')
- grad_input: float32 [2048, 2048], P('ctx', 'tp')
- grad_norm_gain: float32 [2048], P('tp')
- grad_norm_shift: float32 [2048], P('tp')
- grad_w_qkv: float32 [2048, 3, 2048], P('ctx', None, 'tp')
- grad_b_qkv: float32 [3, 2048], P(None, 'tp')
- grad_w_out: float32 [2048, 2048], P('tp', 'ctx')
- grad_b_out: float32 [2048], P('tp')
- grad_w_fc1: float32 [2048, 8192], P('ctx', 'tp')
- grad_b_fc1: float32 [8192], P('tp')
- grad_w_fc2: float32 [8192, 2048], P('tp', 'ctx')
- grad_b_fc2: float32 [2048], P('tp')
The draws below stay inside these ranges and needn't reach their ends.
Inputs may be any that keep to these rules, and one draw needn't show every extreme that they name: `placement`: stored blocks 2 c and 2 c + 1 sit on index c of ctx; entry 2 c is some block a and entry 2 c + 1 is 15 - a, with the values a over all c a permutation of 0 to 7.
All inputs are finite; a program needn't handle non-finite values.
Results may differ from the reference program's by a relative error of at most 0.019.
Values may be sent and summed in bfloat16 or wider, within the bound.
No kernel may reach another device: no remote copies, remote signals or barrier semaphores. Data moves between devices by JAX's collectives and lax.ppermute only.
A program may use at most 192 MiB of HBM per device.

```python
import math
import jax
import jax.numpy as jnp
from jax import lax

D = 2048
HEADS = 32
HD = 64
ROT = 32
FF = 8192
BLK = 128
SEQ = 2048
NBLOCKS = 16


def draw_w_qkv(key, part):
    base_key = jax.random.fold_in(key, 11)
    column_scale = jnp.array([1.7, 1.7, 1.0], dtype=jnp.float32) / math.sqrt(D)
    weights = jax.random.normal(base_key, (D, 3, D), jnp.float32) * column_scale[None, :, None]
    return jnp.clip(weights, -1.0, 1.0).astype(jnp.bfloat16)


def draw_placement(key, part):
    half = NBLOCKS // 2
    order = jax.random.permutation(key, jnp.arange(half, dtype=jnp.int32))
    index = jnp.arange(NBLOCKS, dtype=jnp.int32)
    device = index // 2
    first = order[device]
    return jnp.where(index % 2 == 0, first, NBLOCKS - 1 - first).astype(jnp.int32)


def with_ends(entries, key, smallest, high):
    shape = entries.shape
    place = [jax.random.randint(jax.random.fold_in(key, axis), (), 0, shape[axis]) for axis in range(len(shape))]
    entries = entries.at[tuple(place)].set(smallest)
    longest = shape.index(max(shape))
    place[longest] = (place[longest] + 1) % shape[longest]
    return entries.at[tuple(place)].set(high)


def level_of(rng, shape, shards, low, largest):
    def one(position, parts):
        steps = jax.random.uniform(jax.random.fold_in(jax.random.fold_in(rng, 6), position), (parts,), jnp.float32, low / len(shards), largest / len(shards))
        return jnp.repeat(jnp.exp(steps), shape[position] // parts).reshape((-1,) + (1,) * (len(shape) - position - 1))

    factor_of = one(*shards[0])
    for cut in shards[1:]:
        factor_of = factor_of * one(*cut)
    return factor_of


def noise(rng, dims, scale, limit, shards=(), kind=jnp.bfloat16):
    drawn = scale * jax.random.normal(rng, dims, jnp.float32)
    if shards:
        drawn = drawn * level_of(rng, dims, shards, -0.22, 0.18)
    return jnp.clip(drawn, -limit, limit).astype(kind)


def setup_inputs(seed: int = 0) -> dict:
    key_list = jax.random.split(jax.random.key(seed), 15)
    return {
        "layer_input": noise(key_list[0], (SEQ, D), 1.0, 6.0, ((0, 8), (1, 4))),
        "norm_gain": jnp.clip(1.0 + 0.1 * jax.random.normal(key_list[1], (D,), jnp.float32), 0.5, 1.5).astype(jnp.bfloat16),
        "norm_shift": noise(key_list[2], (D,), 0.5, 3.0, ((0, 4),)),
        "w_qkv": draw_w_qkv(jax.random.fold_in(key_list[14], 71), 0),
        "b_qkv": noise(key_list[4], (3, D), 0.5, 3.0, ((1, 4),), jnp.float32),
        "w_out": noise(key_list[5], (D, D), D ** -0.5, 0.125, ((0, 4), (1, 8))),
        "b_out": noise(key_list[6], (D,), 0.5, 3.0, ((0, 4),), jnp.float32),
        "w_fc1": noise(key_list[7], (D, FF), D ** -0.5, 0.125, ((0, 8), (1, 4))),
        "b_fc1": noise(key_list[8], (FF,), 0.5, 3.0, ((0, 4),), jnp.float32),
        "w_fc2": noise(key_list[9], (FF, D), FF ** -0.5, 0.0625, ((0, 4), (1, 8))),
        "b_fc2": noise(key_list[10], (D,), 0.5, 3.0, ((0, 4),), jnp.float32),
        "grad_output": noise(key_list[11], (SEQ, D), 1.0, 6.0, ((0, 8), (1, 4))),
        "placement": draw_placement(jax.random.fold_in(key_list[14], 71), 0),
        "position_ids": with_ends(jax.random.randint(key_list[13], (SEQ,), 0, 2 * SEQ), jax.random.fold_in(key_list[13], 1), 0, (2 * SEQ) - 1).astype(jnp.int32),
    }


epsilon = 1e-05
cubic_coef = 0.044715
neg_large = -1e+30

def rope_tables(positions):
    half_rot = ROT // 2
    frequency = 10000.0 ** (-2.0 * jnp.arange(half_rot, dtype=jnp.float32) / ROT)
    angles = positions.astype(jnp.float32)[:, None] * frequency[None, :]
    return (jnp.cos(angles), jnp.sin(angles))

def rotate(values, cosine, sine, direction):
    half_rot = ROT // 2
    first = values[..., :half_rot]
    second = values[..., half_rot:ROT]
    cos_wide = cosine[:, None, :]
    sin_wide = sine[:, None, :] * direction
    return jnp.concatenate([first * cos_wide - second * sin_wide, second * cos_wide + first * sin_wide, values[..., ROT:]], axis=-1)

def gelu_slope(pre):
    inner_coef = math.sqrt(2.0 / math.pi)
    tanh_value = jnp.tanh(inner_coef * (pre + cubic_coef * pre * pre * pre))
    return 0.5 * (1.0 + tanh_value) + 0.5 * pre * (1.0 - tanh_value * tanh_value) * inner_coef * (1.0 + 3.0 * cubic_coef * pre * pre)

def rounded(values):
    return lax.optimization_barrier(values.astype(jnp.bfloat16)).astype(jnp.float32)

def normalize(block, gain, shift):
    values = block.astype(jnp.float32)
    center = lax.optimization_barrier(jnp.mean(values, axis=-1, keepdims=True))
    spread = lax.optimization_barrier(jnp.mean(jnp.square(values - center), axis=-1, keepdims=True))
    inv_std = lax.rsqrt(spread + epsilon)
    normed = (values - center) * inv_std
    return (normed, inv_std, (normed * gain + shift).astype(jnp.bfloat16))

def reference(layer_input, norm_gain, norm_shift, w_qkv, b_qkv, w_out, b_out, w_fc1, b_fc1, w_fc2, b_fc2, grad_output, placement, position_ids):
    token_block = math.gcd(SEQ, 4096)
    block_count = SEQ // token_block
    query_block = math.gcd(SEQ, 512)
    query_count = SEQ // query_block
    key_block = math.gcd(SEQ, 2048)
    key_count = SEQ // key_block
    scale = 1.0 / math.sqrt(HD)
    gain = norm_gain.astype(jnp.float32)
    shift = norm_shift.astype(jnp.float32)
    joint_flat = w_qkv.reshape(D, 3 * D)
    indices = jnp.arange(SEQ, dtype=jnp.int32)
    logical = (placement[indices // BLK] * BLK + indices % BLK).astype(jnp.int32)
    input_blocks = layer_input.reshape(block_count, token_block, D)
    pos_blocks = position_ids.reshape(block_count, token_block)
    cot_blocks = grad_output.reshape(block_count, token_block, D)

    def front(carry, inputs):
        input_block, pos_block = inputs
        normed, inv_std, normed16 = normalize(input_block, gain, shift)
        joint = jnp.dot(normed16, joint_flat, preferred_element_type=jnp.float32).reshape(token_block, 3, D) + b_qkv[None]
        cosine, sine = rope_tables(pos_block)
        queries = rotate(joint[:, 0].reshape(token_block, HEADS, HD), cosine, sine, 1.0).astype(jnp.bfloat16)
        keys = rotate(joint[:, 1].reshape(token_block, HEADS, HD), cosine, sine, 1.0).astype(jnp.bfloat16)
        values = joint[:, 2].reshape(token_block, HEADS, HD).astype(jnp.bfloat16)
        return (carry, (queries, keys, values))
    _, (queries, keys, values) = lax.scan(front, None, (input_blocks, pos_blocks))
    queries = queries.reshape(SEQ, HEADS, HD)
    keys = keys.reshape(SEQ, HEADS, HD)
    values = values.reshape(SEQ, HEADS, HD)
    key_stack = keys.reshape(key_count, key_block, HEADS, HD)
    value_stack = values.reshape(key_count, key_block, HEADS, HD)
    keypos_stack = logical.reshape(key_count, key_block)

    def block_scores(query_rows, key_rows):
        return jnp.einsum('qhd,khd->hqk', query_rows.astype(jnp.float32), key_rows.astype(jnp.float32)) * scale

    def attend_forward(inputs):
        query_rows, query_pos = inputs

        def pass_one(carry, item):
            top, total = carry
            key_rows, key_pos = item
            scores = block_scores(query_rows, key_rows)
            allowed = key_pos[None, None, :] <= query_pos[None, :, None]
            masked = jnp.where(allowed, scores, neg_large)
            new_top = jnp.maximum(top, lax.optimization_barrier(jnp.max(masked, axis=-1)))
            weights = jnp.where(allowed, jnp.exp(scores - new_top[..., None]), 0.0)
            total = total * jnp.exp(top - new_top) + lax.optimization_barrier(jnp.sum(weights, axis=-1))
            return ((new_top, total), None)
        start_state = (jnp.full((HEADS, query_block), neg_large, jnp.float32), jnp.zeros((HEADS, query_block), jnp.float32))
        (top, total), _ = lax.scan(pass_one, start_state, (key_stack, keypos_stack))
        log_total = top + jnp.log(total)

        def pass_two(carry, item):
            key_rows, value_rows, key_pos = item
            scores = block_scores(query_rows, key_rows)
            allowed = key_pos[None, None, :] <= query_pos[None, :, None]
            probs = jnp.where(allowed, jnp.exp(scores - log_total[..., None]), 0.0)
            return (carry + jnp.einsum('hqk,khd->qhd', rounded(probs), value_rows.astype(jnp.float32)), None)
        mixed, _ = lax.scan(pass_two, jnp.zeros((query_block, HEADS, HD), jnp.float32), (key_stack, value_stack, keypos_stack))
        return (mixed.astype(jnp.bfloat16), log_total)
    attended, log_totals = lax.map(attend_forward, (queries.reshape(query_count, query_block, HEADS, HD), logical.reshape(query_count, query_block)))
    attended = attended.reshape(SEQ, D)

    def middle(carry, inputs):
        acc_fc2, acc_fc1, acc_out, acc_bias1, acc_biasout = carry
        input_block, attended_block, cot_block = inputs
        normed, inv_std, normed16 = normalize(input_block, gain, shift)
        pre = jnp.dot(normed16, w_fc1, preferred_element_type=jnp.float32) + b_fc1
        active16 = jax.nn.gelu(pre, approximate=True).astype(jnp.bfloat16)
        branch_mlp = jnp.dot(active16, w_fc2, preferred_element_type=jnp.float32)
        branch_attn = jnp.dot(attended_block, w_out, preferred_element_type=jnp.float32)
        result = input_block.astype(jnp.float32) + branch_attn + b_out + branch_mlp + b_fc2
        grad_active = jnp.dot(cot_block, w_fc2.T, preferred_element_type=jnp.float32)
        acc_fc2 = acc_fc2 + jnp.dot(active16.T, cot_block, preferred_element_type=jnp.float32)
        grad_pre = grad_active * gelu_slope(pre)
        acc_bias1 = acc_bias1 + lax.optimization_barrier(jnp.sum(grad_pre, axis=0))
        grad_pre16 = grad_pre.astype(jnp.bfloat16)
        acc_fc1 = acc_fc1 + jnp.dot(normed16.T, grad_pre16, preferred_element_type=jnp.float32)
        grad_attended = jnp.dot(cot_block, w_out.T, preferred_element_type=jnp.float32).astype(jnp.bfloat16)
        acc_out = acc_out + jnp.dot(attended_block.T, cot_block, preferred_element_type=jnp.float32)
        acc_biasout = acc_biasout + lax.optimization_barrier(jnp.sum(cot_block.astype(jnp.float32), axis=0))
        delta = lax.optimization_barrier(jnp.sum((grad_attended.astype(jnp.float32) * attended_block.astype(jnp.float32)).reshape(token_block, HEADS, HD), axis=-1))
        back_mlp = jnp.dot(grad_pre16, w_fc1.T, preferred_element_type=jnp.float32)
        return ((acc_fc2, acc_fc1, acc_out, acc_bias1, acc_biasout), (result, grad_attended, delta, back_mlp))
    start_acc = (jnp.zeros((FF, D), jnp.float32), jnp.zeros((D, FF), jnp.float32), jnp.zeros((D, D), jnp.float32), jnp.zeros((FF,), jnp.float32), jnp.zeros((D,), jnp.float32))
    (grad_w_fc2, grad_w_fc1, grad_w_out, grad_b_fc1, grad_b_out), (layer_output, grad_attended, delta, back_mlp) = lax.scan(middle, start_acc, (input_blocks, attended.reshape(block_count, token_block, D), cot_blocks))
    layer_output = layer_output.reshape(SEQ, D)
    grad_attended = grad_attended.reshape(SEQ, HEADS, HD)
    delta = delta.reshape(SEQ, HEADS)
    back_mlp = back_mlp.reshape(SEQ, D)

    def backward_block(carry, inputs):
        grad_keys, grad_values = carry
        query_rows, cot_rows, query_pos, log_total, delta_rows = inputs

        def over_keys(inner, number):
            grad_q, inner_keys, inner_values = inner
            start = number * key_block
            key_rows = lax.dynamic_slice_in_dim(keys, start, key_block, 0)
            value_rows = lax.dynamic_slice_in_dim(values, start, key_block, 0)
            key_pos = lax.dynamic_slice_in_dim(logical, start, key_block, 0)
            scores = block_scores(query_rows, key_rows)
            allowed = key_pos[None, None, :] <= query_pos[None, :, None]
            probs = jnp.where(allowed, jnp.exp(scores - log_total[..., None]), 0.0)
            grad_probs = jnp.einsum('qhd,khd->hqk', cot_rows.astype(jnp.float32), value_rows.astype(jnp.float32))
            grad_scores = rounded(probs * (grad_probs - delta_rows[..., None]))
            probs16 = rounded(probs)
            part_values = jnp.einsum('hqk,qhd->khd', probs16, cot_rows.astype(jnp.float32))
            part_keys = jnp.einsum('hqk,qhd->khd', grad_scores, query_rows.astype(jnp.float32)) * scale
            part_queries = jnp.einsum('hqk,khd->qhd', grad_scores, key_rows.astype(jnp.float32)) * scale
            old_keys = lax.dynamic_slice_in_dim(inner_keys, start, key_block, 0)
            old_values = lax.dynamic_slice_in_dim(inner_values, start, key_block, 0)
            inner_keys = lax.dynamic_update_slice_in_dim(inner_keys, old_keys + part_keys, start, 0)
            inner_values = lax.dynamic_update_slice_in_dim(inner_values, old_values + part_values, start, 0)
            return ((grad_q + part_queries, inner_keys, inner_values), None)
        start_inner = (jnp.zeros((query_block, HEADS, HD), jnp.float32), grad_keys, grad_values)
        (grad_q, grad_keys, grad_values), _ = lax.scan(over_keys, start_inner, jnp.arange(key_count, dtype=jnp.int32))
        return ((grad_keys, grad_values), grad_q)
    delta_blocks = delta.reshape(query_count, query_block, HEADS).transpose(0, 2, 1)
    start_grads = (jnp.zeros((SEQ, HEADS, HD), jnp.float32), jnp.zeros((SEQ, HEADS, HD), jnp.float32))
    (grad_keys, grad_values), grad_queries = lax.scan(backward_block, start_grads, (queries.reshape(query_count, query_block, HEADS, HD), grad_attended.reshape(query_count, query_block, HEADS, HD), logical.reshape(query_count, query_block), log_totals, delta_blocks))
    grad_queries = grad_queries.reshape(SEQ, HEADS, HD)

    def rear(carry, inputs):
        acc_joint, acc_bias, acc_gain, acc_shift = carry
        input_block, pos_block, grad_q, grad_k, grad_v, back_block, cot_block = inputs
        normed, inv_std, normed16 = normalize(input_block, gain, shift)
        cosine, sine = rope_tables(pos_block)
        grad_q = rotate(grad_q, cosine, sine, -1.0).reshape(token_block, D)
        grad_k = rotate(grad_k, cosine, sine, -1.0).reshape(token_block, D)
        grad_joint = jnp.stack([grad_q, grad_k, grad_v.reshape(token_block, D)], axis=1)
        acc_bias = acc_bias + lax.optimization_barrier(jnp.sum(grad_joint, axis=0))
        grad_joint16 = grad_joint.reshape(token_block, 3 * D).astype(jnp.bfloat16)
        acc_joint = acc_joint + jnp.dot(normed16.T, grad_joint16, preferred_element_type=jnp.float32)
        grad_normed = back_block + jnp.dot(grad_joint16, joint_flat.T, preferred_element_type=jnp.float32)
        acc_gain = acc_gain + lax.optimization_barrier(jnp.sum(grad_normed * normed, axis=0))
        acc_shift = acc_shift + lax.optimization_barrier(jnp.sum(grad_normed, axis=0))
        scaled = grad_normed * gain
        grad_x = inv_std * (scaled - lax.optimization_barrier(jnp.mean(scaled, axis=-1, keepdims=True)) - normed * lax.optimization_barrier(jnp.mean(scaled * normed, axis=-1, keepdims=True)))
        result = cot_block.astype(jnp.float32) + grad_x
        return ((acc_joint, acc_bias, acc_gain, acc_shift), result)
    start_rear = (jnp.zeros((D, 3 * D), jnp.float32), jnp.zeros((3, D), jnp.float32), jnp.zeros((D,), jnp.float32), jnp.zeros((D,), jnp.float32))
    (grad_w_qkv, grad_b_qkv, grad_norm_gain, grad_norm_shift), grad_input = lax.scan(rear, start_rear, (input_blocks, pos_blocks, grad_queries.reshape(block_count, token_block, HEADS, HD), grad_keys.reshape(block_count, token_block, HEADS, HD), grad_values.reshape(block_count, token_block, HEADS, HD), back_mlp.reshape(block_count, token_block, D), cot_blocks))
    grad_input = grad_input.reshape(SEQ, D)
    grad_w_qkv = grad_w_qkv.reshape(D, 3, D)
    return (layer_output, grad_input, grad_norm_gain, grad_norm_shift, grad_w_qkv, grad_b_qkv, grad_w_out, grad_b_out, grad_w_fc1, grad_b_fc1, grad_w_fc2, grad_b_out)
```

```python
import functools
import math

import jax
import jax.numpy as jnp
from jax import lax
from jax.experimental import pallas as pl
from jax.experimental.pallas import tpu as pltpu
from jax.sharding import Mesh, PartitionSpec as P

D = 2048
HD = 64
ROT = 32
BLK = 128
HALF = BLK // 2
LO = 8
UNIT = 1024

epsilon = 1e-05
cubic_coef = 0.044715
neg_large = -1e30
BF = jnp.bfloat16
F32 = jnp.float32
LOX = ("zh", "zl", "x")
CTX = ("hi",) + LOX
TP = ("y", "k")


def swap(values, axis):
    return lax.ppermute(values, axis, [(0, 1), (1, 0)])


def send_lo(values, step):
    return lax.ppermute(values, LOX, [(i, i ^ step) for i in range(LO)])


def full_spec(count):
    return [pl.BlockSpec(memory_space=pltpu.VMEM) for _ in range(count)]


def dot(left, right, left_dim, right_dim):
    return lax.dot_general(
        left, right, (((left_dim,), (right_dim,)), ((), ())), preferred_element_type=F32
    )


def gather_units(unit):
    pair = jnp.stack([unit, swap(unit, "zh")])
    quad = jnp.concatenate([pair, swap(pair, "zl")])
    first, second = quad[:, 0], quad[:, 1]
    first_x = swap(first, "x")
    second_y = swap(second, "y")
    firsts = jnp.stack([first, first_x])
    seconds = jnp.stack([second, second_y])
    firsts_y = swap(firsts, "y")
    seconds_x = swap(seconds, "x")
    return firsts, firsts_y, seconds, seconds_x


def scatter_units(first, second):
    def add(left, right):
        return left.astype(F32) + right.astype(F32)

    got_y = swap(first[:, :, UNIT:], "y")
    got_x = swap(second[4:], "x")
    first1 = add(first[:, :, :UNIT], got_y).astype(BF)
    second1 = add(second[:4], got_x).astype(BF)
    got_x = swap(first1[4:], "x")
    got_y = swap(second1[:, :, UNIT:], "y")
    first2 = add(first1[:4], got_x).astype(BF)
    second2 = add(second1[:, :, :UNIT], got_y).astype(BF)
    both = jnp.stack([first2, second2], axis=1)
    both = add(both[:2], swap(both[2:], "zl")).astype(BF)
    return add(both[0], swap(both[1], "zh"))


def exchange(pieces):
    return [pieces[0]] + [send_lo(pieces[s], s) for s in range(1, LO)]


def tokens_of(refs, slot, block):
    firsts, firsts_y, seconds, seconds_x = refs
    x, j = slot // 4, slot % 4
    if block == 0:
        return firsts[x, j], firsts_y[x, j]
    if x == 0:
        return seconds[0, j], seconds[1, j]
    return seconds_x[0, j], seconds_x[1, j]


def norm_kernel(a, b, c, d, gain, shift, normed, mean, inv):
    for slot in range(LO):
        for block in range(2):
            own, other = tokens_of((a, b, c, d), slot, block)
            own, other = own.astype(F32), other.astype(F32)
            center = (
                jnp.sum(own, axis=-1, keepdims=True) + jnp.sum(other, axis=-1, keepdims=True)
            ) / D
            own, other = own - center, other - center
            spread = (
                jnp.sum(own * own, axis=-1, keepdims=True)
                + jnp.sum(other * other, axis=-1, keepdims=True)
            ) / D
            inv_std = lax.rsqrt(spread + epsilon)
            rows = pl.ds((slot * 2 + block) * HALF, HALF)
            normed[rows, :UNIT] = (own * inv_std * gain[:, :UNIT] + shift[:, :UNIT]).astype(BF)
            normed[rows, UNIT:] = (other * inv_std * gain[:, UNIT:] + shift[:, UNIT:]).astype(BF)
            if slot == 0:
                mean[pl.ds(block * HALF, HALF), :] = jnp.broadcast_to(center, (HALF, 128))
                inv[pl.ds(block * HALF, HALF), :] = jnp.broadcast_to(inv_std, (HALF, 128))


def normalize(pieces, gain, shift):
    tokens = LO * BLK
    return pl.pallas_call(
        norm_kernel,
        out_shape=(
            jax.ShapeDtypeStruct((tokens, D), BF),
            jax.ShapeDtypeStruct((BLK, 128), F32),
            jax.ShapeDtypeStruct((BLK, 128), F32),
        ),
        in_specs=full_spec(6),
        out_specs=tuple(full_spec(3)),
        cost_estimate=pl.CostEstimate(
            flops=10 * tokens * D, bytes_accessed=4 * tokens * D, transcendentals=0
        ),
        name="norm",
    )(*pieces, gain, shift)


def collect_kernel(a, b, c, d, out):
    for slot in range(LO):
        for block in range(2):
            own, other = tokens_of((a, b, c, d), slot, block)
            rows = pl.ds((slot * 2 + block) * HALF, HALF)
            out[rows, :UNIT] = own
            out[rows, UNIT:] = other


def collect(pieces):
    tokens = LO * BLK
    return pl.pallas_call(
        collect_kernel,
        out_shape=jax.ShapeDtypeStruct((tokens, D), BF),
        in_specs=full_spec(4),
        out_specs=full_spec(1)[0],
        cost_estimate=pl.CostEstimate(
            flops=0, bytes_accessed=4 * tokens * D, transcendentals=0
        ),
        name="collect",
    )(*pieces)


def turn(values, cosine, sine_a, sine_b):
    return (
        values * cosine
        + pltpu.roll(values, 128 - ROT // 2, 1) * sine_a
        + pltpu.roll(values, ROT // 2, 1) * sine_b
    )


def joint_kernel(normed, weight, bias, cosine, sine_a, sine_b, queries, keys, values, sent):
    joint = (
        jnp.dot(normed[...], weight[...], preferred_element_type=F32) + bias[...]
    )
    tables = (cosine[...], sine_a[...], sine_b[...])
    queries[...] = turn(joint[:, :128], *tables).astype(BF)
    turned, value = turn(joint[:, 128:256], *tables), joint[:, 256:]
    keys[...] = turned.astype(BF)
    values[...] = value.astype(BF)
    sent[0] = pltpu.roll(turned, HD, 1).astype(BF)
    sent[1] = pltpu.roll(value, HD, 1).astype(BF)


def project(normed, weight, bias, cosine, sine_a, sine_b):
    tokens = normed.shape[0]
    step = 256
    row = lambda i: (i, 0)
    fixed = lambda i: (0, 0)
    wide = pl.BlockSpec((step, 128), row)
    return pl.pallas_call(
        joint_kernel,
        grid=(tokens // step,),
        out_shape=tuple(jax.ShapeDtypeStruct((tokens, 128), BF) for _ in range(3))
        + (jax.ShapeDtypeStruct((2, tokens, 128), BF),),
        in_specs=[
            pl.BlockSpec((step, D), row),
            pl.BlockSpec((D, 384), fixed),
            pl.BlockSpec((1, 384), fixed),
            wide,
            wide,
            wide,
        ],
        out_specs=(wide, wide, wide, pl.BlockSpec((2, step, 128), lambda i: (0, i, 0))),
        cost_estimate=pl.CostEstimate(
            flops=2 * tokens * D * 384, bytes_accessed=2 * tokens * D, transcendentals=0
        ),
        name="joint",
    )(normed, weight, bias, cosine, sine_a, sine_b)


def sort_in(table, own, other, target, blocks):
    core = table[0]
    for i in range(blocks):
        place = table[1 + i]
        rows = pl.ds(i * HALF, HALF)
        target[pl.ds(pl.multiple_of(place * BLK + core * HALF, HALF), HALF), :] = own[rows, :]
        target[pl.ds(pl.multiple_of(place * BLK + (1 - core) * HALF, HALF), HALF), :] = other[
            rows, :
        ]


def two_heads(tile):
    lane = lax.broadcasted_iota(jnp.int32, tile.shape, 1)
    zero = jnp.zeros_like(tile)
    return jnp.concatenate(
        [jnp.where(lane < HD, tile, zero), jnp.where(lane < HD, zero, tile)], axis=0
    )


def one_tile(pair):
    rows = pair.shape[0] // 2
    lane = lax.broadcasted_iota(jnp.int32, (rows, pair.shape[1]), 1)
    return jnp.where(lane < HD, pair[:rows], pair[rows:])


def attend_kernel(
    tiles, blocks, table, q, k_own, v_own, k_other, v_other, out, log_out, qs, ks, vs, os, ls
):
    core = table[0]
    sort_in(table, k_own, k_other, ks, blocks)
    sort_in(table, v_own, v_other, vs, blocks)
    for i in range(2 * LO):
        place = table[1 + blocks + i]
        qs[pl.ds(pl.multiple_of(place * HALF, HALF), HALF), :] = q[pl.ds(i * HALF, HALF), :]
    scale = 1.0 / math.sqrt(HD)
    full = len(tiles) > 0 and tiles[0] == tiles[-1] and len(tiles) > 1
    row = lax.broadcasted_iota(jnp.int32, (2 * BLK, 2 * BLK), 0) % BLK
    col = lax.broadcasted_iota(jnp.int32, (2 * BLK, 2 * BLK), 1)
    edge = col <= (row // HALF) * BLK + core * HALF + row % HALF

    def tile(m, extent):
        pair = two_heads(qs[pl.ds(pl.multiple_of(m * BLK, BLK), BLK), :])
        scores = dot(pair, ks[pl.ds(0, extent), :], 1, 1) * scale
        if full:
            wide_col = lax.broadcasted_iota(jnp.int32, scores.shape, 1)
            wide_row = lax.broadcasted_iota(jnp.int32, scores.shape, 0) % BLK
            begin = jnp.where(
                wide_row < HALF,
                table[1 + blocks + 2 * LO + 2 * m],
                table[2 + blocks + 2 * LO + 2 * m],
            )
            allowed = wide_col <= begin * BLK + core * HALF + wide_row % HALF
            scores = jnp.where(allowed, scores, neg_large)
        else:
            last = jnp.where(edge, scores[:, extent - 2 * BLK :], neg_large)
            if extent > 2 * BLK:
                scores = jnp.concatenate([scores[:, : extent - 2 * BLK], last], axis=1)
            else:
                scores = last
        top = jnp.max(scores, axis=-1, keepdims=True)
        weights = jnp.exp(scores - top)
        total = jnp.sum(weights, axis=-1, keepdims=True)
        probs = (weights * (1.0 / total)).astype(BF)
        mixed = dot(probs, vs[pl.ds(0, extent), :], 1, 0)
        os[pl.ds(pl.multiple_of(m * BLK, BLK), BLK), :] = one_tile(mixed)
        ls[pl.ds(pl.multiple_of(m * BLK, BLK), BLK), :] = one_tile(
            jnp.broadcast_to(top + jnp.log(total), (2 * BLK, 128))
        )

    if full:
        lax.fori_loop(0, len(tiles), lambda m, carry: (tile(m, tiles[0]), carry)[1], 0)
    else:
        for m, extent in enumerate(tiles):
            tile(m, extent)
    for i in range(2 * LO):
        place = table[1 + blocks + i]
        rows = pl.ds(pl.multiple_of(place * HALF, HALF), HALF)
        out[pl.ds(i * HALF, HALF), :] = os[rows, :].astype(BF)
        log_out[pl.ds(i * HALF, HALF), :] = ls[rows, :]


def attend(tiles, blocks, table, q, k_own, v_own, k_other, v_other):
    tokens = q.shape[0]
    keys = blocks * BLK
    return pl.pallas_call(
        functools.partial(attend_kernel, tiles, blocks),
        out_shape=(
            jax.ShapeDtypeStruct((tokens, 128), BF),
            jax.ShapeDtypeStruct((tokens, 128), F32),
        ),
        in_specs=[pl.BlockSpec(memory_space=pltpu.SMEM)] + full_spec(5),
        out_specs=tuple(full_spec(2)),
        scratch_shapes=[
            pltpu.VMEM((tokens, 128), BF),
            pltpu.VMEM((keys, 128), BF),
            pltpu.VMEM((keys, 128), BF),
            pltpu.VMEM((tokens, 128), F32),
            pltpu.VMEM((tokens, 128), F32),
        ],
        cost_estimate=pl.CostEstimate(
            flops=8 * 256 * 128 * sum(tiles),
            bytes_accessed=2000000,
            transcendentals=256 * sum(tiles),
        ),
        name="attend",
    )(table, q, k_own, v_own, k_other, v_other)


def attend_back_kernel(
    tiles,
    blocks,
    table,
    q,
    k_own,
    v_own,
    k_other,
    v_other,
    cot,
    att,
    log_in,
    dq,
    dk_own,
    dv_own,
    sent,
    qs,
    ks,
    vs,
    cs,
    ps,
    ls,
    dqs,
    dks,
    dvs,
):
    core = table[0]
    sort_in(table, k_own, k_other, ks, blocks)
    sort_in(table, v_own, v_other, vs, blocks)
    for i in range(2 * LO):
        place = table[1 + blocks + i]
        rows = pl.ds(i * HALF, HALF)
        target = pl.ds(pl.multiple_of(place * HALF, HALF), HALF)
        qs[target, :] = q[rows, :]
        cs[target, :] = cot[rows, :]
        ps[target, :] = cot[rows, :].astype(F32) * att[rows, :].astype(F32)
        ls[target, :] = log_in[rows, :]
    dks[...] = jnp.zeros_like(dks)
    dvs[...] = jnp.zeros_like(dvs)
    scale = 1.0 / math.sqrt(HD)
    full = len(tiles) > 0 and tiles[0] == tiles[-1] and len(tiles) > 1
    col = lax.broadcasted_iota(jnp.int32, (2 * BLK, 2 * BLK), 1) % BLK
    row = lax.broadcasted_iota(jnp.int32, (2 * BLK, 2 * BLK), 0)
    edge = row <= (col // HALF) * BLK + core * HALF + col % HALF

    def tile(m, extent):
        rows = pl.ds(pl.multiple_of(m * BLK, BLK), BLK)
        span = pl.ds(0, extent)
        pair = two_heads(qs[rows, :])
        cot_pair = two_heads(cs[rows, :])
        logs = jnp.transpose(ls[rows, :])
        log_row = jnp.concatenate([logs[0:1], logs[HD : HD + 1]], axis=1)
        products = jnp.transpose(ps[rows, :])
        delta = jnp.concatenate(
            [
                jnp.sum(products[:HD], axis=0, keepdims=True),
                jnp.sum(products[HD:], axis=0, keepdims=True),
            ],
            axis=1,
        )
        scores = dot(ks[span, :], pair, 1, 1) * scale
        probs = jnp.exp(scores - log_row)
        if full:
            wide_row = lax.broadcasted_iota(jnp.int32, scores.shape, 0)
            wide_col = lax.broadcasted_iota(jnp.int32, scores.shape, 1) % BLK
            begin = jnp.where(
                wide_col < HALF,
                table[1 + blocks + 2 * LO + 2 * m],
                table[2 + blocks + 2 * LO + 2 * m],
            )
            allowed = wide_row <= begin * BLK + core * HALF + wide_col % HALF
            probs = jnp.where(allowed, probs, 0.0)
        else:
            last = jnp.where(edge, probs[extent - 2 * BLK :], 0.0)
            if extent > 2 * BLK:
                probs = jnp.concatenate([probs[: extent - 2 * BLK], last], axis=0)
            else:
                probs = last
        grad_probs = dot(vs[span, :], cot_pair, 1, 1)
        grad_scores = (probs * (grad_probs - delta)).astype(BF)
        dvs[span, :] += dot(probs.astype(BF), cot_pair, 1, 0)
        dks[span, :] += dot(grad_scores, pair, 1, 0)
        dqs[rows, :] = one_tile(dot(grad_scores, ks[span, :], 0, 0)) * scale

    if full:
        lax.fori_loop(0, len(tiles), lambda m, carry: (tile(m, tiles[0]), carry)[1], 0)
    else:
        for m, extent in enumerate(tiles):
            tile(m, extent)
    for i in range(2 * LO):
        place = table[1 + blocks + i]
        dq[pl.ds(i * HALF, HALF), :] = dqs[
            pl.ds(pl.multiple_of(place * HALF, HALF), HALF), :
        ]
    for i in range(blocks):
        place = table[1 + i]
        rows = pl.ds(i * HALF, HALF)
        own = pl.ds(pl.multiple_of(place * BLK + core * HALF, HALF), HALF)
        other = pl.ds(pl.multiple_of(place * BLK + (1 - core) * HALF, HALF), HALF)
        dk_own[rows, :] = dks[own, :] * scale
        dv_own[rows, :] = dvs[own, :]
        sent[0, rows, :] = pltpu.roll(dks[other, :] * scale, HD, 1).astype(BF)
        sent[1, rows, :] = pltpu.roll(dvs[other, :], HD, 1).astype(BF)


def attend_back(tiles, blocks, table, q, k_own, v_own, k_other, v_other, cot, att, log_in):
    tokens = q.shape[0]
    keys = blocks * BLK
    return pl.pallas_call(
        functools.partial(attend_back_kernel, tiles, blocks),
        out_shape=(
            jax.ShapeDtypeStruct((tokens, 128), F32),
            jax.ShapeDtypeStruct((keys // 2, 128), F32),
            jax.ShapeDtypeStruct((keys // 2, 128), F32),
            jax.ShapeDtypeStruct((2, keys // 2, 128), BF),
        ),
        in_specs=[pl.BlockSpec(memory_space=pltpu.SMEM)] + full_spec(8),
        out_specs=tuple(full_spec(4)),
        scratch_shapes=[
            pltpu.VMEM((tokens, 128), BF),
            pltpu.VMEM((keys, 128), BF),
            pltpu.VMEM((keys, 128), BF),
            pltpu.VMEM((tokens, 128), BF),
            pltpu.VMEM((tokens, 128), F32),
            pltpu.VMEM((tokens, 128), F32),
            pltpu.VMEM((tokens, 128), F32),
            pltpu.VMEM((keys, 128), F32),
            pltpu.VMEM((keys, 128), F32),
        ],
        cost_estimate=pl.CostEstimate(
            flops=20 * 256 * 128 * sum(tiles),
            bytes_accessed=6000000,
            transcendentals=256 * sum(tiles),
        ),
        name="attend_back",
    )(table, q, k_own, v_own, k_other, v_other, cot, att, log_in)


def place_kernel(axis, count, index, *refs):
    out = refs[-1]
    for group in range(count):
        for s in range(LO):
            block = refs[group * LO + s]
            rows, columns = block.shape
            if axis == 0:
                target = pl.ds(pl.multiple_of(index[s] * rows, rows), rows)
                out[target, group * columns : (group + 1) * columns] = block[...].astype(out.dtype)
            else:
                target = pl.ds(pl.multiple_of(index[s] * columns, columns), columns)
                out[group * rows : (group + 1) * rows, target] = block[...].astype(out.dtype)


def place(groups, index, axis, dtype):
    parts, rows, columns = groups[0][0].shape
    count = len(groups)
    if parts == 1 and rows % 16 == 0 and columns % 128 == 0:
        shape = (LO * rows, count * columns) if axis == 0 else (count * rows, LO * columns)
        blocks = [block[0] for group in groups for block in group]
        size = shape[0] * shape[1]
        return pl.pallas_call(
            functools.partial(place_kernel, axis, count),
            out_shape=jax.ShapeDtypeStruct(shape, dtype),
            in_specs=[pl.BlockSpec(memory_space=pltpu.SMEM)] + full_spec(count * LO),
            out_specs=full_spec(1)[0],
            cost_estimate=pl.CostEstimate(
                flops=0, bytes_accessed=4 * size, transcendentals=0
            ),
            name="place",
        )(index[0], *blocks)
    order = jnp.argsort(index.reshape(-1))
    results = []
    for group in groups:
        stacked = jnp.stack(group, axis=1).reshape(parts * LO, rows, columns)[order]
        if axis == 0:
            results.append(stacked.reshape(parts * LO * rows, columns))
        else:
            results.append(stacked.transpose(1, 0, 2).reshape(rows, parts * LO * columns))
    return jnp.concatenate(results, axis=1 - axis).astype(dtype)


def gelu_slope(pre):
    inner_coef = math.sqrt(2.0 / math.pi)
    tanh_value = jnp.tanh(inner_coef * (pre + cubic_coef * pre * pre * pre))
    return 0.5 * (1.0 + tanh_value) + 0.5 * pre * (1.0 - tanh_value * tanh_value) * inner_coef * (
        1.0 + 3.0 * cubic_coef * pre * pre
    )


def on_device(
    n_hi,
    layer_input,
    norm_gain,
    norm_shift,
    w_qkv,
    b_qkv,
    w_out,
    b_out,
    w_fc1,
    b_fc1,
    w_fc2,
    b_fc2,
    grad_output,
    placement,
    position_ids,
):
    hi, y, k = (lax.axis_index(name) for name in ("hi", "y", "k"))
    lo = lax.axis_index(LOX)
    n_ctx = n_hi * LO
    depth = D // n_ctx
    width = w_qkv.shape[2]
    hidden = w_fc1.shape[1] // LO
    tokens = LO * BLK
    flip = (2 * y + k) * (n_ctx // 4)
    ctx_of = [lo ^ s for s in range(LO)]
    spots = jnp.stack(
        [jnp.stack([(h * LO + ctx_of[s]) ^ flip for s in range(LO)]) for h in range(n_hi)]
    ).astype(jnp.int32)
    slot_step = [((s & 1) << 2) | (s & 2) | (s >> 2) for s in range(LO)]
    slot_lo = [lo ^ step for step in slot_step]

    def half(values, which):
        split = values.reshape((2, 2, HALF) + values.shape[1:])
        return lax.dynamic_index_in_dim(split, which, 1, keepdims=False)

    def make_unit(values):
        got = swap(half(values, 1 - k), "k")
        return jnp.concatenate([half(values, k), got], axis=-1)

    own_head = lax.dynamic_slice_in_dim(b_qkv, lo * HD, HD, 1)
    own_bias1 = lax.dynamic_slice_in_dim(b_fc1, lo * hidden, hidden, 0)
    small = jnp.concatenate(
        [norm_gain.astype(F32), norm_shift.astype(F32), own_head.reshape(-1), own_bias1]
    )
    small_other = swap(small, "k")
    affine = jnp.stack([small[: 2 * width], small_other[: 2 * width]]).reshape(2, 2, width)
    affine = affine.transpose(1, 0, 2).reshape(2, 2 * width)
    affine = jnp.concatenate([affine, swap(affine, "y")], axis=1)
    gain, shift = affine[0:1], affine[1:2]
    heads_own = small[2 * width : 2 * width + 3 * HD].reshape(3, HD)
    heads_other = small_other[2 * width : 2 * width + 3 * HD].reshape(3, HD)
    bias_joint = jnp.concatenate([heads_own, heads_other], axis=1).reshape(1, 6 * HD)
    bias1 = jnp.concatenate([own_bias1, small_other[2 * width + 3 * HD :]])

    unit_in = make_unit(layer_input)
    pieces_in = gather_units(unit_in)
    unit_cot = make_unit(grad_output)
    pieces_cot = gather_units(unit_cot)

    def over_hi(values):
        if n_hi == 1:
            return values[None]
        return lax.all_gather(values, "hi", axis=0)

    def fetch(cut):
        own = exchange([over_hi(cut(ctx_of[s])) for s in range(LO)])
        return own, [swap(block, "k") for block in own]

    fc1_blocks = fetch(lambda c: lax.dynamic_slice_in_dim(w_fc1, c * hidden, hidden, 1))
    qkv_blocks = fetch(
        lambda c: lax.dynamic_slice_in_dim(w_qkv, c * HD, HD, 2).reshape(depth, 3 * HD)
    )
    fc2_blocks = fetch(lambda c: lax.dynamic_slice_in_dim(w_fc2, c * hidden, hidden, 0))
    out_blocks = fetch(lambda c: lax.dynamic_slice_in_dim(w_out, c * HD, HD, 0))
    fc1 = place(fc1_blocks, spots, 0, BF)
    fc2 = place(fc2_blocks, spots, 1, BF)
    out = place(out_blocks, spots, 1, BF)
    joined = [
        jnp.concatenate(
            [own.reshape(n_hi, depth, 3, HD), other.reshape(n_hi, depth, 3, HD)], axis=-1
        ).reshape(n_hi, depth, 6 * HD)
        for own, other in zip(*qkv_blocks)
    ]
    qkv = place([joined], spots, 0, BF)

    ids = half(position_ids, k)
    ids = jnp.stack([ids, swap(ids, "zh")])
    ids = jnp.stack([ids, swap(ids, "zl")])
    ids = jnp.stack([ids, swap(ids, "x")]).reshape(tokens)
    lane = jnp.arange(128, dtype=jnp.int32) % HD
    frequency = 10000.0 ** (-2.0 * (lane % (ROT // 2)).astype(F32) / ROT)
    angles = ids.astype(F32)[:, None] * frequency[None, :]
    cosine = jnp.where(lane < ROT, jnp.cos(angles), 1.0)
    sine = jnp.sin(angles)
    sine_a = jnp.where(lane < ROT // 2, -sine, 0.0)
    sine_b = jnp.where((lane >= ROT // 2) & (lane < ROT), sine, 0.0)

    blocks = n_hi * 2 * LO
    local = jnp.stack([placement[2 * (hi * LO + c) + b] for c in slot_lo for b in range(2)])
    key_table = jnp.stack(
        [placement[2 * (h * LO + c) + b] for h in range(n_hi) for c in slot_lo for b in range(2)]
    )
    ranks = jnp.sum((local[None, :] < local[:, None]).astype(jnp.int32), axis=1)
    sorted_local = jnp.sort(local) if n_hi > 1 else jnp.arange(2 * LO, dtype=jnp.int32)
    table = jnp.concatenate([k[None].astype(jnp.int32), key_table, ranks, sorted_local])
    if n_hi == 1:
        tiles = tuple(2 * BLK * (m + 1) for m in range(LO))
    else:
        tiles = (blocks * BLK,) * LO

    normed16, mean, inv = normalize(pieces_in, gain, shift)
    queries, keys, values, sent = project(normed16, qkv, bias_joint, cosine, sine_a, sine_b)
    other_kv = swap(sent, "k")

    def all_keys(rows):
        if n_hi == 1:
            return rows
        return lax.all_gather(rows, "hi", axis=0, tiled=True)

    k_own, v_own = all_keys(keys), all_keys(values)
    k_other, v_other = all_keys(other_kv[0]), all_keys(other_kv[1])
    attended, log_total = attend(tiles, blocks, table, queries, k_own, v_own, k_other, v_other)
    pre = jnp.dot(normed16, fc1, preferred_element_type=F32) + bias1
    active = jax.nn.gelu(pre, approximate=True).astype(BF)

    def halves(left_a, right_a, left_b, right_b, right_dim):
        results = []
        for b in range(2):
            total = 0.0
            for left, right in ((left_a, right_a), (left_b, right_b)):
                rows = left.reshape(LO, 2, HALF, -1)[:, b].reshape(LO * HALF, -1)
                total = total + dot(rows, right, 1, right_dim)
            results.append(total.astype(BF).reshape(LO, HALF, D))
        return results

    summed = scatter_units(*halves(attended, out, active, fc2, 0))

    cot = collect(pieces_cot)
    grad_active = dot(cot, fc2, 1, 1)
    grad_attended = dot(cot, out, 1, 1).astype(BF)
    term_fc2 = dot(active, cot, 0, 0)
    term_out = dot(attended, cot, 0, 0)
    grad_pre = grad_active * gelu_slope(pre)
    term_bias1 = jnp.sum(grad_pre, axis=0)
    grad_pre16 = grad_pre.astype(BF)
    term_fc1 = dot(normed16, grad_pre16, 0, 0)
    dq, dk, dv, grads_sent = attend_back(
        tiles,
        blocks,
        table,
        queries,
        k_own,
        v_own,
        k_other,
        v_other,
        grad_attended,
        attended,
        log_total,
    )

    def own_keys(rows):
        if n_hi == 1:
            return rows
        return lax.psum_scatter(rows, "hi", scatter_dimension=0, tiled=True)

    got = swap(grads_sent, "k")
    dk = own_keys(dk + got[0].astype(F32))
    dv = own_keys(dv + got[1].astype(F32))

    def turn_back(rows):
        return (
            rows * cosine
            - jnp.roll(rows, -(ROT // 2), 1) * sine_a
            - jnp.roll(rows, ROT // 2, 1) * sine_b
        )

    grad_joint = jnp.concatenate([turn_back(dq), turn_back(dk), dv], axis=1)
    term_joint_bias = jnp.sum(grad_joint, axis=0)
    grad_joint16 = grad_joint.astype(BF)
    term_qkv = dot(normed16, grad_joint16, 0, 0)
    first, second = halves(grad_joint16, qkv, grad_pre16, fc1, 1)
    grad_unit = scatter_units(first, second)

    def give(term, axis, own_first):
        sent, kept = [], []
        size = term.shape[1 - axis] // 2
        for s in range(LO):
            cut = jnp.stack(
                [
                    lax.dynamic_slice_in_dim(term, spots[h, s] * depth, depth, axis)
                    for h in range(n_hi)
                ]
            )
            mine, theirs = own_first(cut, size)
            kept.append(mine)
            sent.append(theirs.astype(BF))
        got = swap(jnp.stack(sent), "k")
        total = [kept[s] + got[s].astype(F32) for s in range(LO)]
        if n_hi > 1:
            total = exchange([t.astype(BF) for t in total])
            return [lax.psum_scatter(t.astype(F32), "hi", scatter_dimension=0) for t in total]
        return [t[0] for t in exchange([t.astype(BF) for t in total])]

    def columns(cut, size):
        return cut[:, :, :size], cut[:, :, size:]

    def rows_of(cut, size):
        return cut[:, :size], cut[:, size:]

    def head_columns(cut, size):
        split = cut.reshape(n_hi, depth, 3, 2, HD)
        return (
            split[:, :, :, 0].reshape(n_hi, depth, 3 * HD),
            split[:, :, :, 1].reshape(n_hi, depth, 3 * HD),
        )

    home = jnp.stack(ctx_of)[None].astype(jnp.int32)
    grad_fc2 = place([[t[None] for t in give(term_fc2, 1, rows_of)]], home, 0, F32)
    grad_fc1 = place([[t[None] for t in give(term_fc1, 0, columns)]], home, 1, F32)
    grad_out = place([[t[None] for t in give(term_out, 1, rows_of)]], home, 0, F32)
    back = give(term_qkv, 0, head_columns)
    grad_qkv = jnp.zeros((depth, 3, width), F32)
    for s in range(LO):
        grad_qkv = lax.dynamic_update_slice(
            grad_qkv,
            back[s].astype(F32).reshape(depth, 3, HD),
            (0, 0, ctx_of[s] * HD),
        )

    def to_rows(unit):
        got = swap(unit[:, :, width:], "k")
        own = unit[:, :, :width]
        return jnp.stack(
            [jnp.where(k == 0, own, got), jnp.where(k == 0, got, own)], axis=1
        ).reshape(2 * BLK, width)

    layer_output = (
        layer_input.astype(F32) + to_rows(summed) + b_out + b_fc2
    )
    unit_grad = grad_unit.reshape(BLK, UNIT)
    gain_own = gain[:, :UNIT]
    normed_unit = (unit_in.reshape(BLK, UNIT).astype(F32) - mean[:, :1]) * inv[:, :1]
    scaled = unit_grad * gain_own
    row_sums = jnp.stack(
        [jnp.sum(scaled, axis=-1), jnp.sum(scaled * normed_unit, axis=-1)]
    )
    row_sums = (row_sums + swap(row_sums, "y")) / D
    grad_x = inv[:, :1] * (
        scaled - row_sums[0][:, None] - normed_unit * row_sums[1][:, None]
    )
    grad_x = grad_x + unit_cot.reshape(BLK, UNIT).astype(F32)
    grad_input = to_rows(grad_x.reshape(2, HALF, UNIT))

    heads = jnp.zeros((2, 3, width), F32)
    heads = lax.dynamic_update_slice(
        heads, term_joint_bias.reshape(3, 2, HD).transpose(1, 0, 2), (0, 0, lo * HD)
    )
    bias_sum = jnp.zeros((2, LO * hidden), F32)
    bias_sum = lax.dynamic_update_slice(
        bias_sum, term_bias1.reshape(2, hidden), (0, lo * hidden)
    )
    gain_sum = jnp.sum(unit_grad * normed_unit, axis=0).reshape(2, width)
    shift_sum = jnp.sum(unit_grad, axis=0).reshape(2, width)
    flat = jnp.concatenate([heads.reshape(2, -1), bias_sum, gain_sum, shift_sum], axis=1)
    flat = flat[0] + swap(flat[1], "k")
    flat = jnp.concatenate([flat, jnp.sum(grad_output.astype(F32), axis=0)])
    for name in ("x", "zl", "zh"):
        flat = flat + swap(flat, name)
    if n_hi > 1:
        flat = lax.psum(flat, "hi")
    cuts = [3 * width, LO * hidden, width, width, width]
    ends = [sum(cuts[: i + 1]) for i in range(len(cuts))]
    grad_b_qkv = flat[: ends[0]].reshape(3, width)
    grad_b_fc1 = flat[ends[0] : ends[1]]
    grad_gain = flat[ends[1] : ends[2]]
    grad_shift = flat[ends[2] : ends[3]]
    grad_b_out = flat[ends[3] :]
    return (
        layer_output,
        grad_input,
        grad_gain,
        grad_shift,
        grad_qkv,
        grad_b_qkv,
        grad_out,
        grad_b_out,
        grad_fc1,
        grad_b_fc1,
        grad_fc2,
        grad_b_out,
    )


def solution(mesh):
    n_hi = mesh.shape["ctx"] // LO
    inner = Mesh(mesh.devices.reshape(n_hi, 2, 2, 2, 2, 2), CTX + TP)
    in_specs = (
        P(CTX, TP),
        P(TP),
        P(TP),
        P(CTX, None, TP),
        P(None, TP),
        P(TP, CTX),
        P(TP),
        P(CTX, TP),
        P(TP),
        P(TP, CTX),
        P(TP),
        P(CTX, TP),
        P(),
        P(CTX),
    )
    out_specs = (
        P(CTX, TP),
        P(CTX, TP),
        P(TP),
        P(TP),
        P(CTX, None, TP),
        P(None, TP),
        P(TP, CTX),
        P(TP),
        P(CTX, TP),
        P(TP),
        P(TP, CTX),
        P(TP),
    )
    return jax.shard_map(
        functools.partial(on_device, n_hi),
        mesh=inner,
        in_specs=in_specs,
        out_specs=out_specs,
        check_vma=False,
    )
```

```python
import functools
import math

import jax
import jax.numpy as jnp
from jax import lax
from jax.experimental import pallas as pl
from jax.experimental.pallas import tpu as pltpu
from jax.sharding import Mesh, PartitionSpec as P

D = 2048
HD = 64
ROT = 32
BLK = 128
HALF = BLK // 2
LO = 8
UNIT = 1024
STEP = 256

epsilon = 1e-05
cubic_coef = 0.044715
inner_coef = math.sqrt(2.0 / math.pi)
neg_large = -1e30
BF = jnp.bfloat16
F32 = jnp.float32
LOX = ("zh", "zl", "x")
CTX = ("hi",) + LOX
TP = ("y", "k")
CHIPS = LOX + ("y",)


def swap(values, axis):
    return lax.ppermute(values, axis, [(0, 1), (1, 0)])


def spread(pieces):
    return lax.all_to_all(pieces, LOX, 0, 0, tiled=True)


def full_spec(count):
    return [pl.BlockSpec(memory_space=pltpu.VMEM) for _ in range(count)]


def dot(left, right, left_dim, right_dim):
    return lax.dot_general(
        left, right, (((left_dim,), (right_dim,)), ((), ())), preferred_element_type=F32
    )


def cost(flops, size):
    return pl.CostEstimate(flops=flops, bytes_accessed=size, transcendentals=0)


def rows_spec(columns, step=STEP):
    return pl.BlockSpec((step, columns), lambda i: (i, 0))


def fixed_spec(*shape):
    return pl.BlockSpec(shape, lambda i: (0,) * len(shape))


def units_spec():
    return pl.BlockSpec((2, 2, BLK, UNIT), lambda i: (i, 0, 0, 0))


def whole_rows(units):
    return jnp.concatenate(
        [jnp.concatenate([units[s, 0], units[s, 1]], axis=1) for s in range(2)], axis=0
    )


def pack_kernel(weight, out):
    for c in range(LO):
        columns = slice(c * HD, (c + 1) * HD)
        for j in range(3):
            out[c, j] = jnp.concatenate(
                [weight[j, :BLK, columns], weight[j, BLK:, columns]], axis=1
            )


def pack_heads(weight):
    return pl.pallas_call(
        pack_kernel,
        out_shape=jax.ShapeDtypeStruct((LO, 3, BLK, BLK), BF),
        in_specs=full_spec(1),
        out_specs=full_spec(1)[0],
        cost_estimate=cost(0, 1600000),
        name="pack",
    )(weight)


def join_kernel(own, other, out):
    for c in range(LO):
        for u in range(2):
            columns = slice(u * HD, (u + 1) * HD)
            rows = pl.ds(c * 2 * BLK + u * BLK, BLK)
            for j in range(3):
                out[rows, j * BLK : (j + 1) * BLK] = jnp.concatenate(
                    [own[c, j, :, columns], other[c, j, :, columns]], axis=1
                )


def join_heads(own, other):
    return pl.pallas_call(
        join_kernel,
        out_shape=jax.ShapeDtypeStruct((D, 3 * BLK), BF),
        in_specs=full_spec(2),
        out_specs=full_spec(1)[0],
        cost_estimate=cost(0, 3200000),
        name="join",
    )(own, other)


def pack_grad_kernel(own, other, out):
    for c in range(LO):
        for j in range(3):
            columns = slice(j * HD, (j + 1) * HD)
            parts = []
            for u in range(2):
                rows = pl.ds(c * 2 * BLK + u * BLK, BLK)
                parts.append(own[rows, columns] + other[rows, columns].astype(F32))
            out[c, j] = jnp.concatenate(parts, axis=1).astype(BF)


def pack_grads(own, other):
    return pl.pallas_call(
        pack_grad_kernel,
        out_shape=jax.ShapeDtypeStruct((LO, 3, BLK, BLK), BF),
        in_specs=full_spec(2),
        out_specs=full_spec(1)[0],
        cost_estimate=cost(0, 4000000),
        name="pack_grad",
    )(own, other)


def home_kernel(pieces, out):
    for c in range(0, LO, 2):
        for u in range(2):
            columns = slice(u * HD, (u + 1) * HD)
            for j in range(3):
                out[j, u * BLK : (u + 1) * BLK, c * HD : (c + 2) * HD] = jnp.concatenate(
                    [pieces[c, j, :, columns], pieces[c + 1, j, :, columns]], axis=1
                ).astype(F32)


def home_heads(pieces):
    return pl.pallas_call(
        home_kernel,
        out_shape=jax.ShapeDtypeStruct((3, 2 * BLK, LO * HD), F32),
        in_specs=full_spec(1),
        out_specs=full_spec(1)[0],
        cost_estimate=cost(0, 2400000),
        name="home",
    )(pieces)


def turn(values, cosine, sine_a, sine_b):
    return (
        values * cosine
        + pltpu.roll(values, 128 - ROT // 2, 1) * sine_a
        + pltpu.roll(values, ROT // 2, 1) * sine_b
    )


def sort_in(table, own, other, target, blocks):
    core = table[0]
    for i in range(blocks):
        place = table[1 + i]
        rows = pl.ds(i * HALF, HALF)
        target[pl.ds(pl.multiple_of(place * BLK + core * HALF, HALF), HALF), :] = own[rows, :]
        target[pl.ds(pl.multiple_of(place * BLK + (1 - core) * HALF, HALF), HALF), :] = other[
            rows, :
        ]


def two_heads(tile):
    lane = lax.broadcasted_iota(jnp.int32, tile.shape, 1)
    zero = jnp.zeros_like(tile)
    return jnp.concatenate(
        [jnp.where(lane < HD, tile, zero), jnp.where(lane < HD, zero, tile)], axis=0
    )


def one_tile(pair):
    rows = pair.shape[0] // 2
    lane = lax.broadcasted_iota(jnp.int32, (rows, pair.shape[1]), 1)
    return jnp.where(lane < HD, pair[:rows], pair[rows:])


def attend_kernel(
    tiles, blocks, table, q, k_own, v_own, k_other, v_other, out, log_out, qs, ks, vs, os, ls
):
    core = table[0]
    sort_in(table, k_own, k_other, ks, blocks)
    sort_in(table, v_own, v_other, vs, blocks)
    for i in range(2 * LO):
        place = table[1 + blocks + i]
        qs[pl.ds(pl.multiple_of(place * HALF, HALF), HALF), :] = q[pl.ds(i * HALF, HALF), :]
    scale = 1.0 / math.sqrt(HD)
    full = len(tiles) > 0 and tiles[0] == tiles[-1] and len(tiles) > 1
    row = lax.broadcasted_iota(jnp.int32, (2 * BLK, 2 * BLK), 0) % BLK
    col = lax.broadcasted_iota(jnp.int32, (2 * BLK, 2 * BLK), 1)
    edge = col <= (row // HALF) * BLK + core * HALF + row % HALF

    def tile(m, extent):
        pair = two_heads(qs[pl.ds(pl.multiple_of(m * BLK, BLK), BLK), :])
        scores = dot(pair, ks[pl.ds(0, extent), :], 1, 1) * scale
        if full:
            wide_col = lax.broadcasted_iota(jnp.int32, scores.shape, 1)
            wide_row = lax.broadcasted_iota(jnp.int32, scores.shape, 0) % BLK
            begin = jnp.where(
                wide_row < HALF,
                table[1 + blocks + 2 * LO + 2 * m],
                table[2 + blocks + 2 * LO + 2 * m],
            )
            allowed = wide_col <= begin * BLK + core * HALF + wide_row % HALF
            scores = jnp.where(allowed, scores, neg_large)
        else:
            last = jnp.where(edge, scores[:, extent - 2 * BLK :], neg_large)
            if extent > 2 * BLK:
                scores = jnp.concatenate([scores[:, : extent - 2 * BLK], last], axis=1)
            else:
                scores = last
        top = jnp.max(scores, axis=-1, keepdims=True)
        weights = jnp.exp(scores - top)
        total = jnp.sum(weights, axis=-1, keepdims=True)
        probs = (weights * (1.0 / total)).astype(BF)
        mixed = dot(probs, vs[pl.ds(0, extent), :], 1, 0)
        os[pl.ds(pl.multiple_of(m * BLK, BLK), BLK), :] = one_tile(mixed)
        ls[pl.ds(pl.multiple_of(m * BLK, BLK), BLK), :] = one_tile(
            jnp.broadcast_to(top + jnp.log(total), (2 * BLK, 128))
        )

    if full:
        lax.fori_loop(0, len(tiles), lambda m, carry: (tile(m, tiles[0]), carry)[1], 0)
    else:
        for m, extent in enumerate(tiles):
            tile(m, extent)
    for i in range(2 * LO):
        place = table[1 + blocks + i]
        rows = pl.ds(pl.multiple_of(place * HALF, HALF), HALF)
        out[pl.ds(i * HALF, HALF), :] = os[rows, :].astype(BF)
        log_out[pl.ds(i * HALF, HALF), :] = ls[rows, :]


def attend(tiles, blocks, table, q, k_own, v_own, k_other, v_other):
    tokens = q.shape[0]
    keys = blocks * BLK
    return pl.pallas_call(
        functools.partial(attend_kernel, tiles, blocks),
        out_shape=(
            jax.ShapeDtypeStruct((tokens, 128), BF),
            jax.ShapeDtypeStruct((tokens, 128), F32),
        ),
        in_specs=[pl.BlockSpec(memory_space=pltpu.SMEM)] + full_spec(5),
        out_specs=tuple(full_spec(2)),
        scratch_shapes=[
            pltpu.VMEM((tokens, 128), BF),
            pltpu.VMEM((keys, 128), BF),
            pltpu.VMEM((keys, 128), BF),
            pltpu.VMEM((tokens, 128), F32),
            pltpu.VMEM((tokens, 128), F32),
        ],
        cost_estimate=pl.CostEstimate(
            flops=8 * 256 * 128 * sum(tiles),
            bytes_accessed=2000000,
            transcendentals=256 * sum(tiles),
        ),
        name="attend",
    )(table, q, k_own, v_own, k_other, v_other)


def attend_back_kernel(
    tiles,
    blocks,
    table,
    q,
    k_own,
    v_own,
    k_other,
    v_other,
    cot,
    att,
    log_in,
    dq,
    dk_own,
    dv_own,
    sent,
    qs,
    ks,
    vs,
    cs,
    ps,
    ls,
    dqs,
    dks,
    dvs,
):
    core = table[0]
    sort_in(table, k_own, k_other, ks, blocks)
    sort_in(table, v_own, v_other, vs, blocks)
    for i in range(2 * LO):
        place = table[1 + blocks + i]
        rows = pl.ds(i * HALF, HALF)
        target = pl.ds(pl.multiple_of(place * HALF, HALF), HALF)
        qs[target, :] = q[rows, :]
        cs[target, :] = cot[rows, :]
        ps[target, :] = cot[rows, :].astype(F32) * att[rows, :].astype(F32)
        ls[target, :] = log_in[rows, :]
    dks[...] = jnp.zeros_like(dks)
    dvs[...] = jnp.zeros_like(dvs)
    scale = 1.0 / math.sqrt(HD)
    full = len(tiles) > 0 and tiles[0] == tiles[-1] and len(tiles) > 1
    col = lax.broadcasted_iota(jnp.int32, (2 * BLK, 2 * BLK), 1) % BLK
    row = lax.broadcasted_iota(jnp.int32, (2 * BLK, 2 * BLK), 0)
    edge = row <= (col // HALF) * BLK + core * HALF + col % HALF

    def tile(m, extent):
        rows = pl.ds(pl.multiple_of(m * BLK, BLK), BLK)
        span = pl.ds(0, extent)
        pair = two_heads(qs[rows, :])
        cot_pair = two_heads(cs[rows, :])
        logs = jnp.transpose(ls[rows, :])
        log_row = jnp.concatenate([logs[0:1], logs[HD : HD + 1]], axis=1)
        products = jnp.transpose(ps[rows, :])
        delta = jnp.concatenate(
            [
                jnp.sum(products[:HD], axis=0, keepdims=True),
                jnp.sum(products[HD:], axis=0, keepdims=True),
            ],
            axis=1,
        )
        scores = dot(ks[span, :], pair, 1, 1) * scale
        probs = jnp.exp(scores - log_row)
        if full:
            wide_row = lax.broadcasted_iota(jnp.int32, scores.shape, 0)
            wide_col = lax.broadcasted_iota(jnp.int32, scores.shape, 1) % BLK
            begin = jnp.where(
                wide_col < HALF,
                table[1 + blocks + 2 * LO + 2 * m],
                table[2 + blocks + 2 * LO + 2 * m],
            )
            allowed = wide_row <= begin * BLK + core * HALF + wide_col % HALF
            probs = jnp.where(allowed, probs, 0.0)
        else:
            last = jnp.where(edge, probs[extent - 2 * BLK :], 0.0)
            if extent > 2 * BLK:
                probs = jnp.concatenate([probs[: extent - 2 * BLK], last], axis=0)
            else:
                probs = last
        grad_probs = dot(vs[span, :], cot_pair, 1, 1)
        grad_scores = (probs * (grad_probs - delta)).astype(BF)
        dvs[span, :] += dot(probs.astype(BF), cot_pair, 1, 0)
        dks[span, :] += dot(grad_scores, pair, 1, 0)
        dqs[rows, :] = one_tile(dot(grad_scores, ks[span, :], 0, 0)) * scale

    if full:
        lax.fori_loop(0, len(tiles), lambda m, carry: (tile(m, tiles[0]), carry)[1], 0)
    else:
        for m, extent in enumerate(tiles):
            tile(m, extent)
    for i in range(2 * LO):
        place = table[1 + blocks + i]
        dq[pl.ds(i * HALF, HALF), :] = dqs[
            pl.ds(pl.multiple_of(place * HALF, HALF), HALF), :
        ]
    for i in range(blocks):
        place = table[1 + i]
        rows = pl.ds(i * HALF, HALF)
        own = pl.ds(pl.multiple_of(place * BLK + core * HALF, HALF), HALF)
        other = pl.ds(pl.multiple_of(place * BLK + (1 - core) * HALF, HALF), HALF)
        dk_own[rows, :] = dks[own, :] * scale
        dv_own[rows, :] = dvs[own, :]
        sent[0, rows, :] = pltpu.roll(dks[other, :] * scale, HD, 1).astype(BF)
        sent[1, rows, :] = pltpu.roll(dvs[other, :], HD, 1).astype(BF)


def attend_back(tiles, blocks, table, q, k_own, v_own, k_other, v_other, cot, att, log_in):
    tokens = q.shape[0]
    keys = blocks * BLK
    return pl.pallas_call(
        functools.partial(attend_back_kernel, tiles, blocks),
        out_shape=(
            jax.ShapeDtypeStruct((tokens, 128), F32),
            jax.ShapeDtypeStruct((keys // 2, 128), F32),
            jax.ShapeDtypeStruct((keys // 2, 128), F32),
            jax.ShapeDtypeStruct((2, keys // 2, 128), BF),
        ),
        in_specs=[pl.BlockSpec(memory_space=pltpu.SMEM)] + full_spec(8),
        out_specs=tuple(full_spec(4)),
        scratch_shapes=[
            pltpu.VMEM((tokens, 128), BF),
            pltpu.VMEM((keys, 128), BF),
            pltpu.VMEM((keys, 128), BF),
            pltpu.VMEM((tokens, 128), BF),
            pltpu.VMEM((tokens, 128), F32),
            pltpu.VMEM((tokens, 128), F32),
            pltpu.VMEM((tokens, 128), F32),
            pltpu.VMEM((keys, 128), F32),
            pltpu.VMEM((keys, 128), F32),
        ],
        cost_estimate=pl.CostEstimate(
            flops=20 * 256 * 128 * sum(tiles),
            bytes_accessed=6000000,
            transcendentals=256 * sum(tiles),
        ),
        name="attend_back",
    )(table, q, k_own, v_own, k_other, v_other, cot, att, log_in)


def front_kernel(
    units,
    gain,
    shift,
    qkv,
    bias_joint,
    cosine,
    sine_a,
    sine_b,
    fc1_own,
    fc1_other,
    bias1,
    normed,
    mean,
    inv,
    queries,
    keys,
    values,
    sent,
    pre,
    active,
):
    rows = whole_rows(units[...]).astype(F32)
    center = jnp.mean(rows, axis=-1, keepdims=True)
    rows = rows - center
    inv_std = lax.rsqrt(jnp.mean(rows * rows, axis=-1, keepdims=True) + epsilon)
    mean[...] = jnp.broadcast_to(center, mean.shape)
    inv[...] = jnp.broadcast_to(inv_std, inv.shape)
    normed16 = (rows * inv_std * gain[...] + shift[...]).astype(BF)
    normed[...] = normed16
    joint = dot(normed16, qkv[...], 1, 0) + bias_joint[...]
    tables = (cosine[...], sine_a[...], sine_b[...])
    queries[...] = turn(joint[:, :BLK], *tables).astype(BF)
    turned, value = turn(joint[:, BLK : 2 * BLK], *tables), joint[:, 2 * BLK :]
    keys[...] = turned.astype(BF)
    values[...] = value.astype(BF)
    sent[0] = pltpu.roll(turned, HD, 1).astype(BF)
    sent[1] = pltpu.roll(value, HD, 1).astype(BF)
    hidden = fc1_own.shape[1]
    for part, weight in enumerate((fc1_own, fc1_other)):
        columns = slice(part * hidden, (part + 1) * hidden)
        result = dot(normed16, weight[...], 1, 0) + bias1[:, columns]
        pre[:, columns] = result
        inner = jnp.tanh(inner_coef * (result + cubic_coef * result * result * result))
        active[:, columns] = (0.5 * result * (1.0 + inner)).astype(BF)


def front(units, gain, shift, qkv, bias_joint, cosine, sine_a, sine_b, fc1_own, fc1_other, bias1):
    tokens = LO * BLK
    hidden = fc1_own.shape[1]

    def shape(columns, dtype):
        return jax.ShapeDtypeStruct((tokens, columns), dtype)

    narrow = rows_spec(BLK)
    return pl.pallas_call(
        front_kernel,
        grid=(tokens // STEP,),
        out_shape=(
            shape(D, BF),
            shape(BLK, F32),
            shape(BLK, F32),
            shape(BLK, BF),
            shape(BLK, BF),
            shape(BLK, BF),
            jax.ShapeDtypeStruct((2, tokens, BLK), BF),
            shape(2 * hidden, F32),
            shape(2 * hidden, BF),
        ),
        in_specs=[
            units_spec(),
            fixed_spec(1, D),
            fixed_spec(1, D),
            fixed_spec(D, 3 * BLK),
            fixed_spec(1, 3 * BLK),
            narrow,
            narrow,
            narrow,
            fixed_spec(D, hidden),
            fixed_spec(D, hidden),
            fixed_spec(1, 2 * hidden),
        ],
        out_specs=(
            rows_spec(D),
            narrow,
            narrow,
            narrow,
            narrow,
            narrow,
            pl.BlockSpec((2, STEP, BLK), lambda i: (0, i, 0)),
            rows_spec(2 * hidden),
            rows_spec(2 * hidden),
        ),
        cost_estimate=cost(2 * tokens * D * (384 + 2 * hidden), 12 * tokens * D // 2),
        name="front",
    )(units, gain, shift, qkv, bias_joint, cosine, sine_a, sine_b, fc1_own, fc1_other, bias1)


def mix_kernel(attended, active, out2, fc2_own, fc2_other, units):
    hidden = fc2_own.shape[1]
    for c in range(LO):
        total = (
            dot(active[:, :hidden], fc2_own[c], 1, 0)
            + dot(active[:, hidden:], fc2_other[c], 1, 0)
            + dot(attended[...], out2[c], 1, 0)
        ).astype(BF)
        columns = slice((c % 4) * 256, (c % 4 + 1) * 256)
        units[0, c // 4, :, columns] = total[:BLK]
        units[1, c // 4, :, columns] = total[BLK:]


def mix(attended, active, out2, fc2_own, fc2_other):
    tokens = LO * BLK
    hidden = fc2_own.shape[1]
    return pl.pallas_call(
        mix_kernel,
        grid=(tokens // STEP,),
        out_shape=jax.ShapeDtypeStruct((LO, 2, BLK, UNIT), BF),
        in_specs=[
            rows_spec(BLK),
            rows_spec(2 * hidden),
            fixed_spec(LO, BLK, 256),
            fixed_spec(LO, hidden, 256),
            fixed_spec(LO, hidden, 256),
        ],
        out_specs=units_spec(),
        cost_estimate=cost(2 * tokens * D * (128 + 2 * hidden), 8000000),
        name="mix",
    )(attended, active, out2, fc2_own, fc2_other)


def back_kernel(
    units, pre, out2, fc2_own, fc2_other, cot, grad_pre, grad_attended, bias_sum
):
    @pl.when(pl.program_id(0) == 0)
    def _():
        bias_sum[...] = jnp.zeros_like(bias_sum)

    rows = whole_rows(units[...])
    cot[...] = rows
    hidden = fc2_own.shape[1]

    def through(weight):
        total = 0.0
        for c in range(LO):
            total = total + dot(rows[:, c * 256 : (c + 1) * 256], weight[c], 1, 1)
        return total

    grad_attended[...] = through(out2).astype(BF)
    for part, weight in enumerate((fc2_own, fc2_other)):
        columns = slice(part * hidden, (part + 1) * hidden)
        value = pre[:, columns]
        inner = jnp.tanh(inner_coef * (value + cubic_coef * value * value * value))
        slope = 0.5 * (1.0 + inner) + 0.5 * value * (1.0 - inner * inner) * inner_coef * (
            1.0 + 3.0 * cubic_coef * value * value
        )
        grad = through(weight) * slope
        bias_sum[:, columns] += jnp.sum(grad, axis=0, keepdims=True)
        grad_pre[:, columns] = grad.astype(BF)


def back(units, pre, out2, fc2_own, fc2_other):
    tokens = LO * BLK
    hidden = fc2_own.shape[1]
    return pl.pallas_call(
        back_kernel,
        grid=(tokens // STEP,),
        out_shape=(
            jax.ShapeDtypeStruct((tokens, D), BF),
            jax.ShapeDtypeStruct((tokens, 2 * hidden), BF),
            jax.ShapeDtypeStruct((tokens, BLK), BF),
            jax.ShapeDtypeStruct((1, 2 * hidden), F32),
        ),
        in_specs=[
            units_spec(),
            rows_spec(2 * hidden),
            fixed_spec(LO, BLK, 256),
            fixed_spec(LO, hidden, 256),
            fixed_spec(LO, hidden, 256),
        ],
        out_specs=(
            rows_spec(D),
            rows_spec(2 * hidden),
            rows_spec(BLK),
            fixed_spec(1, 2 * hidden),
        ),
        cost_estimate=cost(2 * tokens * D * (128 + 2 * hidden), 14000000),
        name="back",
    )(units, pre, out2, fc2_own, fc2_other)


def unturn_kernel(dq, dk, dv, got, cosine, sine_a, sine_b, joint, own, other, bias):
    tables = (cosine[...], -sine_a[...], -sine_b[...])
    dk_all = dk[...] + got[0].astype(F32)
    dv_all = dv[...] + got[1].astype(F32)
    for j, grads in enumerate((turn(dq[...], *tables), turn(dk_all, *tables), dv_all)):
        columns = slice(j * BLK, (j + 1) * BLK)
        bias[:, columns] = jnp.sum(grads, axis=0, keepdims=True)
        grads = grads.astype(BF)
        joint[:, columns] = grads
        own[:, j * HD : (j + 1) * HD] = grads[:, :HD]
        other[:, j * HD : (j + 1) * HD] = grads[:, HD:]


def unturn(dq, dk, dv, got, cosine, sine_a, sine_b):
    tokens = dq.shape[0]
    return pl.pallas_call(
        unturn_kernel,
        out_shape=(
            jax.ShapeDtypeStruct((tokens, 3 * BLK), BF),
            jax.ShapeDtypeStruct((tokens, 3 * HD), BF),
            jax.ShapeDtypeStruct((tokens, 3 * HD), BF),
            jax.ShapeDtypeStruct((1, 3 * BLK), F32),
        ),
        in_specs=full_spec(7),
        out_specs=tuple(full_spec(4)),
        cost_estimate=cost(0, 6000000),
        name="unturn",
    )(dq, dk, dv, got, cosine, sine_a, sine_b)


def grad_kernel(
    units, mean, inv, gain, joint, grad_pre, qkv, fc1_own, fc1_other, out, sums, gain_sum, shift_sum
):
    @pl.when(pl.program_id(0) == 0)
    def _():
        gain_sum[...] = jnp.zeros_like(gain_sum)
        shift_sum[...] = jnp.zeros_like(shift_sum)

    hidden = fc1_own.shape[1]
    grads = (
        dot(joint[...], qkv[...], 1, 1)
        + dot(grad_pre[:, :hidden], fc1_own[...], 1, 1)
        + dot(grad_pre[:, hidden:], fc1_other[...], 1, 1)
    )
    for s in range(2):
        for y in range(2):
            out[s, y] = grads[
                s * BLK : (s + 1) * BLK, y * UNIT : (y + 1) * UNIT
            ].astype(BF)
    normed = (whole_rows(units[...]).astype(F32) - mean[:, :1]) * inv[:, :1]
    both = grads * normed
    shift_sum[...] += jnp.sum(grads, axis=0, keepdims=True)
    gain_sum[...] += jnp.sum(both, axis=0, keepdims=True)
    first = jnp.sum(grads * gain[...], axis=-1, keepdims=True)
    second = jnp.sum(both * gain[...], axis=-1, keepdims=True)
    lane = lax.broadcasted_iota(jnp.int32, sums.shape, 1)
    sums[...] = jnp.where(lane < HD, first, second)


def grad_units(units, mean, inv, gain, joint, grad_pre, qkv, fc1_own, fc1_other):
    tokens = LO * BLK
    hidden = fc1_own.shape[1]
    return pl.pallas_call(
        grad_kernel,
        grid=(tokens // STEP,),
        out_shape=(
            jax.ShapeDtypeStruct((LO, 2, BLK, UNIT), BF),
            jax.ShapeDtypeStruct((tokens, BLK), F32),
            jax.ShapeDtypeStruct((1, D), F32),
            jax.ShapeDtypeStruct((1, D), F32),
        ),
        in_specs=[
            units_spec(),
            rows_spec(BLK),
            rows_spec(BLK),
            fixed_spec(1, D),
            rows_spec(3 * BLK),
            rows_spec(2 * hidden),
            fixed_spec(D, 3 * BLK),
            fixed_spec(D, hidden),
            fixed_spec(D, hidden),
        ],
        out_specs=(units_spec(), rows_spec(BLK), fixed_spec(1, D), fixed_spec(1, D)),
        cost_estimate=cost(2 * tokens * D * (384 + 2 * hidden), 16000000),
        name="grad",
    )(units, mean, inv, gain, joint, grad_pre, qkv, fc1_own, fc1_other)


def on_device(
    n_hi,
    layer_input,
    norm_gain,
    norm_shift,
    w_qkv,
    b_qkv,
    w_out,
    b_out,
    w_fc1,
    b_fc1,
    w_fc2,
    b_fc2,
    grad_output,
    placement,
    position_ids,
):
    hi, y, k = (lax.axis_index(name) for name in ("hi", "y", "k"))
    lo = lax.axis_index(LOX)
    depth = D // (n_hi * LO)
    width = w_qkv.shape[2]
    hidden = w_fc1.shape[1] // LO
    tokens = LO * BLK

    def half(values, which):
        split = values.reshape((2, 2, HALF) + values.shape[1:])
        cut = lax.dynamic_index_in_dim(split, which, 1, keepdims=False)
        return cut.reshape((BLK,) + values.shape[1:])

    def in_order(index, own, got, axis):
        return jnp.where(
            index == 0,
            jnp.concatenate([own, got], axis=axis),
            jnp.concatenate([got, own], axis=axis),
        )

    def make_unit(values):
        got = swap(half(values, 1 - k), "k")
        return in_order(k, half(values, k), got, 1)

    def gather_units(unit):
        return lax.all_gather(unit, CHIPS, axis=0).reshape(LO, 2, BLK, UNIT)

    def scatter_units(units):
        flat = units.reshape(2 * LO * BLK, UNIT)
        return lax.psum_scatter(flat, CHIPS, scatter_dimension=0, tiled=True).astype(F32)

    unit_in = make_unit(layer_input)
    units_in = gather_units(unit_in)
    unit_cot = make_unit(grad_output)
    units_cot = gather_units(unit_cot)

    def over_hi(values):
        return values[None] if n_hi == 1 else lax.all_gather(values, "hi", axis=0)

    def ordered(got, shape):
        return got if n_hi == 1 else jnp.moveaxis(got, 1, 0).reshape(shape)

    fc1_own = spread(
        over_hi(w_fc1).reshape(n_hi, depth, LO, hidden).transpose(2, 0, 1, 3)
    )
    fc1_own = ordered(fc1_own, (D, hidden)).reshape(D, hidden)
    fc1_other = swap(fc1_own, "k")
    down = jnp.concatenate(
        [w_fc2.reshape(LO, hidden, depth), w_out.reshape(LO, HD, depth)], axis=1
    )
    down = spread(jnp.moveaxis(over_hi(down), 0, 1))
    if n_hi == 1:
        down_own = down.reshape(LO, hidden + HD, 256)
    else:
        down_own = down.transpose(2, 1, 0, 3).reshape(hidden + HD, LO, 256).transpose(1, 0, 2)
    down_other = swap(down_own, "k")
    fc2_own, fc2_other = down_own[:, :hidden], down_other[:, :hidden]
    out2 = jnp.concatenate([down_own[:, hidden:], down_other[:, hidden:]], axis=1)
    if n_hi == 1:
        heads_own = spread(pack_heads(w_qkv.transpose(1, 0, 2)))
        qkv = join_heads(heads_own, swap(heads_own, "k"))
    else:
        cut = over_hi(w_qkv).reshape(n_hi, depth, 3, LO, HD).transpose(3, 0, 1, 2, 4)
        heads_own = spread(cut.reshape(LO, n_hi, depth, 3 * HD))
        heads_own = ordered(heads_own, (D, 3, HD))
        qkv = jnp.concatenate([heads_own, swap(heads_own, "k")], axis=2).reshape(D, 6 * HD)

    own_head = lax.dynamic_slice_in_dim(b_qkv, lo * HD, HD, 1)
    own_bias1 = lax.dynamic_slice_in_dim(b_fc1, lo * hidden, hidden, 0)
    affine = jnp.stack([norm_gain.astype(F32), norm_shift.astype(F32)])
    small = jnp.concatenate([affine.reshape(-1), own_head.reshape(-1), own_bias1])
    small_other = swap(small, "k")
    affine = in_order(k, affine, small_other[: 2 * width].reshape(2, width), 1)
    affine = in_order(y, affine, swap(affine, "y"), 1)
    gain, shift = affine[0:1], affine[1:2]
    head_other = small_other[2 * width : 2 * width + 3 * HD].reshape(3, HD)
    bias_joint = jnp.concatenate([own_head, head_other], axis=1).reshape(1, 6 * HD)
    bias1 = jnp.concatenate([own_bias1, small_other[2 * width + 3 * HD :]])[None]

    ids = half(position_ids, k)[None]
    ids = in_order(lo & 1, ids, swap(ids, "x"), 0)
    ids = in_order((lo >> 1) & 1, ids, swap(ids, "zl"), 0)
    ids = in_order(lo >> 2, ids, swap(ids, "zh"), 0).reshape(tokens)
    lane = jnp.arange(BLK, dtype=jnp.int32) % HD
    frequency = 10000.0 ** (-2.0 * (lane % (ROT // 2)).astype(F32) / ROT)
    angles = ids.astype(F32)[:, None] * frequency[None, :]
    cosine = jnp.where(lane < ROT, jnp.cos(angles), 1.0)
    sine = jnp.sin(angles)
    sine_a = jnp.where(lane < ROT // 2, -sine, 0.0)
    sine_b = jnp.where((lane >= ROT // 2) & (lane < ROT), sine, 0.0)

    blocks = n_hi * 2 * LO
    local = lax.dynamic_slice_in_dim(placement, hi * 2 * LO, 2 * LO, 0)
    ranks = jnp.sum((local[None, :] < local[:, None]).astype(jnp.int32), axis=1)
    sorted_local = jnp.sort(local) if n_hi > 1 else jnp.arange(2 * LO, dtype=jnp.int32)
    table = jnp.concatenate([k[None].astype(jnp.int32), placement, ranks, sorted_local])
    if n_hi == 1:
        tiles = tuple(2 * BLK * (m + 1) for m in range(LO))
    else:
        tiles = (blocks * BLK,) * LO

    normed16, mean, inv, queries, keys, values, sent, pre, active = front(
        units_in,
        gain,
        shift,
        qkv,
        bias_joint,
        cosine,
        sine_a,
        sine_b,
        fc1_own,
        fc1_other,
        bias1,
    )
    other_kv = swap(sent, "k")

    def all_keys(rows):
        return rows if n_hi == 1 else lax.all_gather(rows, "hi", axis=0, tiled=True)

    key_set = tuple(all_keys(v) for v in (keys, values, other_kv[0], other_kv[1]))
    attended, log_total = attend(tiles, blocks, table, queries, *key_set)
    summed = scatter_units(mix(attended, active, out2, fc2_own, fc2_other))

    cot, grad_pre, grad_attended, term_bias1 = back(units_cot, pre, out2, fc2_own, fc2_other)
    dq, dk, dv, grads_sent = attend_back(
        tiles, blocks, table, queries, *key_set, grad_attended, attended, log_total
    )

    def own_keys(rows):
        if n_hi == 1:
            return rows
        return lax.psum_scatter(rows, "hi", scatter_dimension=0, tiled=True)

    got = swap(grads_sent, "k")
    if n_hi > 1:
        dk = own_keys(dk + got[0].astype(F32))
        dv = own_keys(dv + got[1].astype(F32))
        got = jnp.zeros((2,) + dk.shape, BF)
    joint, joint_own, joint_other, term_joint_bias = unturn(
        dq, dk, dv, got, cosine, sine_a, sine_b
    )
    partial, row_sums, gain_sum, shift_sum = grad_units(
        units_in, mean, inv, gain, joint, grad_pre, qkv, fc1_own, fc1_other
    )
    grad_unit = scatter_units(partial)

    def summed_dot(left, own, other, flip):
        def product(right):
            return dot(right, left, 0, 0) if flip else dot(left, right, 0, 0)

        return product(own), swap(product(other).astype(BF), "k")

    def home(total):
        got = spread(total)
        if n_hi == 1:
            return got[:, 0]
        return lax.psum_scatter(got.astype(F32), "hi", scatter_dimension=1)

    def add(own, got):
        return (own + got.astype(F32)).astype(BF)

    def cut_columns(values):
        rows = values.shape[0]
        return values.reshape(rows, n_hi, LO, depth).transpose(2, 1, 0, 3)

    fc2_sum = add(*summed_dot(cot, active[:, :hidden], active[:, hidden:], True))
    out_sum = add(*summed_dot(cot, attended[:, :HD], attended[:, HD:], True))
    down_home = home(cut_columns(jnp.concatenate([fc2_sum, out_sum], axis=0)))
    grad_fc2 = down_home[:, :hidden].reshape(LO * hidden, depth).astype(F32)
    grad_out = down_home[:, hidden:].reshape(LO * HD, depth).astype(F32)
    fc1_sum = add(*summed_dot(normed16, grad_pre[:, :hidden], grad_pre[:, hidden:], False))
    fc1_home = home(fc1_sum.reshape(n_hi, LO, depth, hidden).transpose(1, 0, 2, 3))
    grad_fc1 = fc1_home.transpose(1, 0, 2).reshape(depth, LO * hidden).astype(F32)
    own_term, got_term = summed_dot(normed16, joint_own, joint_other, False)
    if n_hi == 1:
        grad_qkv = home_heads(spread(pack_grads(own_term, got_term))).transpose(1, 0, 2)
    else:
        qkv_sum = add(own_term, got_term).reshape(n_hi, LO, depth, 3 * HD)
        qkv_home = home(qkv_sum.transpose(1, 0, 2, 3)).reshape(LO, depth, 3, HD)
        grad_qkv = qkv_home.transpose(1, 2, 0, 3).reshape(depth, 3, width).astype(F32)

    heads = lax.dynamic_update_slice(
        jnp.zeros((2, 3, width), F32),
        term_joint_bias.reshape(3, 2, HD).transpose(1, 0, 2),
        (0, 0, lo * HD),
    )
    bias_sum = lax.dynamic_update_slice(
        jnp.zeros((2, LO * hidden), F32), term_bias1.reshape(2, hidden), (0, lo * hidden)
    )
    affine_sum = jnp.concatenate([gain_sum, shift_sum]).reshape(2, 2, 2, width)
    affine_sum = affine_sum.transpose(1, 2, 0, 3)

    def pick(values, index):
        return lax.dynamic_index_in_dim(values, index, 0, keepdims=False)

    row_pair = row_sums[:, :: HD].reshape(-1)
    over_y = jnp.concatenate([pick(affine_sum, 1 - y).reshape(-1), row_pair])
    over_y = swap(over_y, "y")
    affine_sum = pick(affine_sum, y) + over_y[: 4 * width].reshape(2, 2, width)
    row_pair = row_pair + over_y[4 * width :]
    over_k = jnp.concatenate(
        [heads[1].reshape(-1), bias_sum[1], pick(affine_sum, 1 - k).reshape(-1)]
    )
    over_k = swap(over_k, "k") + jnp.concatenate(
        [heads[0].reshape(-1), bias_sum[0], pick(affine_sum, k).reshape(-1)]
    )
    local_bias = jnp.sum(grad_output.astype(F32), axis=0)
    flat = jnp.concatenate([over_k, local_bias, row_pair])
    for name in ("x", "zl", "zh"):
        flat = flat + swap(flat, name)
    row_pair = flat[-2 * tokens :].reshape(tokens, 2)
    flat = flat[: -2 * tokens]
    if n_hi > 1:
        flat = lax.psum(flat, "hi")
    cuts = [3 * width, LO * hidden, width, width, width]
    ends = [sum(cuts[: i + 1]) for i in range(len(cuts))]
    grad_b_qkv = flat[: ends[0]].reshape(3, width)
    grad_b_fc1 = flat[ends[0] : ends[1]]
    grad_gain = flat[ends[1] : ends[2]]
    grad_shift = flat[ends[2] : ends[3]]
    grad_b_out = flat[ends[3] :]

    def to_rows(unit):
        parts = unit.reshape(BLK, 2, width)
        own = lax.dynamic_index_in_dim(parts, k, 1, keepdims=False)
        got = swap(lax.dynamic_index_in_dim(parts, 1 - k, 1, keepdims=False), "k")
        own, got = own.reshape(2, 1, HALF, width), got.reshape(2, 1, HALF, width)
        return in_order(k, own, got, 1).reshape(2 * BLK, width)

    layer_output = layer_input.astype(F32) + to_rows(summed) + b_out + b_fc2

    def own_rows(values):
        return lax.dynamic_slice_in_dim(values, lo * BLK, BLK, 0)

    mean_own, inv_own = own_rows(mean)[:, :1], own_rows(inv)[:, :1]
    row_own = own_rows(row_pair) / D
    gain_own = lax.dynamic_slice_in_dim(gain, y * UNIT, UNIT, 1)
    normed_unit = (unit_in.astype(F32) - mean_own) * inv_own
    grad_x = inv_own * (
        grad_unit * gain_own - row_own[:, :1] - normed_unit * row_own[:, 1:]
    )
    grad_input = to_rows(grad_x + unit_cot.astype(F32))
    return (
        layer_output,
        grad_input,
        grad_gain,
        grad_shift,
        grad_qkv,
        grad_b_qkv,
        grad_out,
        grad_b_out,
        grad_fc1,
        grad_b_fc1,
        grad_fc2,
        grad_b_out,
    )


def solution(mesh):
    n_hi = mesh.shape["ctx"] // LO
    inner = Mesh(mesh.devices.reshape(n_hi, 2, 2, 2, 2, 2), CTX + TP)
    in_specs = (
        P(CTX, TP),
        P(TP),
        P(TP),
        P(CTX, None, TP),
        P(None, TP),
        P(TP, CTX),
        P(TP),
        P(CTX, TP),
        P(TP),
        P(TP, CTX),
        P(TP),
        P(CTX, TP),
        P(),
        P(CTX),
    )
    out_specs = (
        P(CTX, TP),
        P(CTX, TP),
        P(TP),
        P(TP),
        P(CTX, None, TP),
        P(None, TP),
        P(TP, CTX),
        P(TP),
        P(CTX, TP),
        P(TP),
        P(TP, CTX),
        P(TP),
    )
    return jax.shard_map(
        functools.partial(on_device, n_hi),
        mesh=inner,
        in_specs=in_specs,
        out_specs=out_specs,
        check_vma=False,
    )
```

```python
import functools
import math

import jax
import jax.numpy as jnp
from jax import lax
from jax.experimental import pallas as pl
from jax.experimental.pallas import tpu as pltpu
from jax.sharding import Mesh, PartitionSpec as P


D = 2048
HD = 64
ROT = 32
BLK = 128
HALF = BLK // 2
LO = 8
UNIT = 1024
STEP = 256

epsilon = 1e-05
cubic_coef = 0.044715
inner_coef = math.sqrt(2.0 / math.pi)
neg_large = -1e30
BF = jnp.bfloat16
F32 = jnp.float32
LOX = ("zh", "zl", "x")
CTX = ("hi",) + LOX
TP = ("y", "k")


def swap(values, axis):
    return lax.ppermute(values, axis, [(0, 1), (1, 0)])


def spread(pieces):
    return lax.all_to_all(pieces, LOX, 0, 0, tiled=True)


def gather_pieces(unit):
    unit = unit.reshape(2, HALF, UNIT)
    pair = jnp.stack([unit, swap(unit, "zh")])
    quad = jnp.concatenate([pair, swap(pair, "zl")])
    first, second = quad[:, 0], quad[:, 1]
    firsts = jnp.stack([first, swap(first, "x")])
    seconds = jnp.stack([second, swap(second, "y")])
    firsts_y = swap(firsts, "y")
    return firsts, firsts_y, seconds, swap(seconds, "x")


def scatter_pieces(a_own, a_other, b_near, b_far):
    def add(left, right):
        return left.astype(F32) + right.astype(F32)

    a_own = add(a_own, swap(a_other, "y")).astype(BF)
    b_near = add(b_near, swap(b_far, "x")).astype(BF)
    a_own = add(a_own[:4], swap(a_own[4:], "x")).astype(BF)
    b_near = add(b_near[:, 0], swap(b_near[:, 1], "y")).astype(BF)
    both = jnp.stack([a_own, b_near], axis=1)
    both = add(both[:2], swap(both[2:], "zl")).astype(BF)
    return add(both[0], swap(both[1], "zh")).reshape(BLK, UNIT)


def full_spec(count):
    return [pl.BlockSpec(memory_space=pltpu.VMEM) for _ in range(count)]


def dot(left, right, left_dim, right_dim):
    return lax.dot_general(
        left, right, (((left_dim,), (right_dim,)), ((), ())), preferred_element_type=F32
    )


def cost(flops, size):
    return pl.CostEstimate(flops=flops, bytes_accessed=size, transcendentals=0)


def rows_spec(columns, step=STEP):
    return pl.BlockSpec((step, columns), lambda i: (i, 0))


def fixed_spec(*shape):
    return pl.BlockSpec(shape, lambda i: (0,) * len(shape))


def scalar_spec():
    return pl.BlockSpec(memory_space=pltpu.SMEM)


def piece_specs():
    near = pl.BlockSpec((1, 2, HALF, UNIT), lambda i: (i // 2, i % 2, 0, 0))
    both = pl.BlockSpec((2, 2, HALF, UNIT), lambda i: (0, i % 2, 0, 0))
    return [near, near, both, both]


def piece_rows(step, firsts, firsts_y, seconds, seconds_x):
    later = jnp.where(step < 2, seconds[...], seconds_x[...])
    sides = []
    for side, first in enumerate((firsts, firsts_y)):
        parts = []
        for s in range(2):
            parts += [first[0, s], later[side, s]]
        sides.append(jnp.concatenate(parts, axis=0))
    return sides


def sides_of(place):
    y = place[0]
    return [
        pl.ds(pl.multiple_of(y * UNIT, UNIT), UNIT),
        pl.ds(pl.multiple_of((1 - y) * UNIT, UNIT), UNIT),
    ]


def pack_kernel(weight, out):
    for c in range(LO):
        columns = slice(c * HD, (c + 1) * HD)
        for j in range(3):
            out[c, j] = jnp.concatenate(
                [weight[j, :BLK, columns], weight[j, BLK:, columns]], axis=1
            )


def pack_heads(weight):
    return pl.pallas_call(
        pack_kernel,
        out_shape=jax.ShapeDtypeStruct((LO, 3, BLK, BLK), BF),
        in_specs=full_spec(1),
        out_specs=full_spec(1)[0],
        cost_estimate=cost(0, 1600000),
        name="pack",
    )(weight)


def join_kernel(own, other, out):
    for c in range(LO):
        for u in range(2):
            columns = slice(u * HD, (u + 1) * HD)
            rows = pl.ds(c * 2 * BLK + u * BLK, BLK)
            for j in range(3):
                out[rows, j * BLK : (j + 1) * BLK] = jnp.concatenate(
                    [own[c, j, :, columns], other[c, j, :, columns]], axis=1
                )


def join_heads(own, other):
    return pl.pallas_call(
        join_kernel,
        out_shape=jax.ShapeDtypeStruct((D, 3 * BLK), BF),
        in_specs=full_spec(2),
        out_specs=full_spec(1)[0],
        cost_estimate=cost(0, 3200000),
        name="join",
    )(own, other)


def pack_grad_kernel(fc1_own, fc1_other, own, other, out):
    for c in range(LO):
        rows = pl.ds(c * 2 * BLK, 2 * BLK)
        out[c, : 2 * BLK] = (fc1_own[rows, :] + fc1_other[rows, :].astype(F32)).astype(BF)
        tiles = []
        for j in range(3):
            columns = slice(j * HD, (j + 1) * HD)
            parts = []
            for u in range(2):
                rows = pl.ds(c * 2 * BLK + u * BLK, BLK)
                parts.append(own[rows, columns] + other[rows, columns].astype(F32))
            tiles.append(jnp.concatenate(parts, axis=1).astype(BF))
        out[c, 2 * BLK : 3 * BLK] = jnp.concatenate(tiles[:2], axis=1)
        out[c, 3 * BLK :] = jnp.concatenate([tiles[2][:HALF], tiles[2][HALF:]], axis=1)


def pack_grads(fc1_own, fc1_other, own, other):
    return pl.pallas_call(
        pack_grad_kernel,
        out_shape=jax.ShapeDtypeStruct((LO, 3 * BLK + HALF, 2 * BLK), BF),
        in_specs=full_spec(4),
        out_specs=full_spec(1)[0],
        cost_estimate=cost(0, 9000000),
        name="pack_grad",
    )(fc1_own, fc1_other, own, other)


def home_kernel(pieces, fc1, qkv):
    for c in range(LO):
        fc1[:, c * 256 : (c + 1) * 256] = pieces[c, : 2 * BLK].astype(F32)
    for c in range(0, LO, 2):
        for j in range(3):
            tiles = []
            for d in range(2):
                if j < 2:
                    tiles.append(pieces[c + d, 2 * BLK : 3 * BLK, j * BLK : (j + 1) * BLK])
                else:
                    tiles.append(
                        jnp.concatenate(
                            [pieces[c + d, 3 * BLK :, :BLK], pieces[c + d, 3 * BLK :, BLK:]],
                            axis=0,
                        )
                    )
            for u in range(2):
                columns = slice(u * HD, (u + 1) * HD)
                qkv[j, u * BLK : (u + 1) * BLK, c * HD : (c + 2) * HD] = jnp.concatenate(
                    [tile[:, columns] for tile in tiles], axis=1
                ).astype(F32)


def home_grads(pieces):
    return pl.pallas_call(
        home_kernel,
        out_shape=(
            jax.ShapeDtypeStruct((2 * BLK, LO * 256), F32),
            jax.ShapeDtypeStruct((3, 2 * BLK, LO * HD), F32),
        ),
        in_specs=full_spec(1),
        out_specs=tuple(full_spec(2)),
        cost_estimate=cost(0, 6000000),
        name="home",
    )(pieces)


def turn(values, cosine, sine_a, sine_b):
    return (
        values * cosine
        + pltpu.roll(values, 128 - ROT // 2, 1) * sine_a
        + pltpu.roll(values, ROT // 2, 1) * sine_b
    )


def sort_in(table, own, other, target, blocks):
    core = table[0]
    for i in range(blocks):
        place = table[1 + i]
        rows = pl.ds(i * HALF, HALF)
        target[pl.ds(pl.multiple_of(place * BLK + core * HALF, HALF), HALF), :] = own[rows, :]
        target[pl.ds(pl.multiple_of(place * BLK + (1 - core) * HALF, HALF), HALF), :] = other[
            rows, :
        ]


def two_heads(tile):
    lane = lax.broadcasted_iota(jnp.int32, tile.shape, 1)
    zero = jnp.zeros_like(tile)
    return jnp.concatenate(
        [jnp.where(lane < HD, tile, zero), jnp.where(lane < HD, zero, tile)], axis=0
    )


def one_tile(pair):
    rows = pair.shape[0] // 2
    lane = lax.broadcasted_iota(jnp.int32, (rows, pair.shape[1]), 1)
    return jnp.where(lane < HD, pair[:rows], pair[rows:])


def attend_kernel(
    tiles, blocks, table, q, k_own, v_own, k_other, v_other, out, log_out, qs, ks, vs, os, ls
):
    core = table[0]
    sort_in(table, k_own, k_other, ks, blocks)
    sort_in(table, v_own, v_other, vs, blocks)
    for i in range(2 * LO):
        place = table[1 + blocks + i]
        qs[pl.ds(pl.multiple_of(place * HALF, HALF), HALF), :] = q[pl.ds(i * HALF, HALF), :]
    scale = 1.0 / math.sqrt(HD)
    full = len(tiles) > 0 and tiles[0] == tiles[-1] and len(tiles) > 1
    row = lax.broadcasted_iota(jnp.int32, (2 * BLK, 4 * BLK), 0) % BLK
    col = lax.broadcasted_iota(jnp.int32, (2 * BLK, 4 * BLK), 1)
    edge = col - (row // HALF) * BLK - core * HALF - row % HALF

    def tile(m, extent):
        pair = two_heads(qs[pl.ds(pl.multiple_of(m * BLK, BLK), BLK), :])
        scores = dot(pair, ks[pl.ds(0, extent), :], 1, 1) * scale
        if full:
            wide_col = lax.broadcasted_iota(jnp.int32, scores.shape, 1)
            wide_row = lax.broadcasted_iota(jnp.int32, scores.shape, 0) % BLK
            begin = jnp.where(
                wide_row < HALF,
                table[1 + blocks + 2 * LO + 2 * m],
                table[2 + blocks + 2 * LO + 2 * m],
            )
            allowed = wide_col <= begin * BLK + core * HALF + wide_row % HALF
            scores = jnp.where(allowed, scores, neg_large)
        else:
            last = scores[:, extent - 4 * BLK :]
            last = jnp.where(edge <= (m % 2) * (2 * BLK), last, neg_large)
            if extent > 4 * BLK:
                scores = jnp.concatenate([scores[:, : extent - 4 * BLK], last], axis=1)
            else:
                scores = last
        top = jnp.max(scores, axis=-1, keepdims=True)
        weights = jnp.exp(scores - top)
        total = jnp.sum(weights, axis=-1, keepdims=True)
        probs = (weights * (1.0 / total)).astype(BF)
        mixed = dot(probs, vs[pl.ds(0, extent), :], 1, 0)
        os[pl.ds(pl.multiple_of(m * BLK, BLK), BLK), :] = one_tile(mixed)
        ls[pl.ds(pl.multiple_of(m * BLK, BLK), BLK), :] = one_tile(
            jnp.broadcast_to(top + jnp.log(total), (2 * BLK, 128))
        )

    if full:
        lax.fori_loop(0, len(tiles), lambda m, carry: (tile(m, tiles[0]), carry)[1], 0)
    else:
        for m in range(0, len(tiles), 2):
            lax.fori_loop(m, m + 2, lambda i, carry: (tile(i, tiles[m]), carry)[1], 0)
    for i in range(2 * LO):
        place = table[1 + blocks + i]
        rows = pl.ds(pl.multiple_of(place * HALF, HALF), HALF)
        out[pl.ds(i * HALF, HALF), :] = os[rows, :].astype(BF)
        log_out[pl.ds(i * HALF, HALF), :] = ls[rows, :]


def attend(tiles, blocks, table, q, k_own, v_own, k_other, v_other):
    tokens = q.shape[0]
    keys = blocks * BLK
    return pl.pallas_call(
        functools.partial(attend_kernel, tiles, blocks),
        out_shape=(
            jax.ShapeDtypeStruct((tokens, 128), BF),
            jax.ShapeDtypeStruct((tokens, 128), F32),
        ),
        in_specs=[pl.BlockSpec(memory_space=pltpu.SMEM)] + full_spec(5),
        out_specs=tuple(full_spec(2)),
        scratch_shapes=[
            pltpu.VMEM((tokens, 128), BF),
            pltpu.VMEM((keys, 128), BF),
            pltpu.VMEM((keys, 128), BF),
            pltpu.VMEM((tokens, 128), F32),
            pltpu.VMEM((tokens, 128), F32),
        ],
        cost_estimate=pl.CostEstimate(
            flops=8 * 256 * 128 * sum(tiles),
            bytes_accessed=2000000,
            transcendentals=256 * sum(tiles),
        ),
        name="attend",
    )(table, q, k_own, v_own, k_other, v_other)


def attend_back_kernel(
    tiles,
    blocks,
    table,
    q,
    k_own,
    v_own,
    k_other,
    v_other,
    cot,
    att,
    log_in,
    dq,
    dk_own,
    dv_own,
    sent,
    qs,
    ks,
    vs,
    cs,
    ps,
    ls,
    dqs,
    dks,
    dvs,
):
    core = table[0]
    sort_in(table, k_own, k_other, ks, blocks)
    sort_in(table, v_own, v_other, vs, blocks)
    for i in range(2 * LO):
        place = table[1 + blocks + i]
        rows = pl.ds(i * HALF, HALF)
        target = pl.ds(pl.multiple_of(place * HALF, HALF), HALF)
        qs[target, :] = q[rows, :]
        cs[target, :] = cot[rows, :]
        ps[target, :] = cot[rows, :].astype(F32) * att[rows, :].astype(F32)
        ls[target, :] = log_in[rows, :]
    dks[...] = jnp.zeros_like(dks)
    dvs[...] = jnp.zeros_like(dvs)
    scale = 1.0 / math.sqrt(HD)
    full = len(tiles) > 0 and tiles[0] == tiles[-1] and len(tiles) > 1
    col = lax.broadcasted_iota(jnp.int32, (4 * BLK, 2 * BLK), 1) % BLK
    row = lax.broadcasted_iota(jnp.int32, (4 * BLK, 2 * BLK), 0)
    edge = row - (col // HALF) * BLK - core * HALF - col % HALF

    def tile(m, extent):
        rows = pl.ds(pl.multiple_of(m * BLK, BLK), BLK)
        span = pl.ds(0, extent)
        pair = two_heads(qs[rows, :])
        cot_pair = two_heads(cs[rows, :])
        logs = jnp.transpose(ls[rows, :])
        log_row = jnp.concatenate([logs[0:1], logs[HD : HD + 1]], axis=1)
        products = jnp.transpose(ps[rows, :])
        delta = jnp.concatenate(
            [
                jnp.sum(products[:HD], axis=0, keepdims=True),
                jnp.sum(products[HD:], axis=0, keepdims=True),
            ],
            axis=1,
        )
        scores = dot(ks[span, :], pair, 1, 1) * scale
        probs = jnp.exp(scores - log_row)
        if full:
            wide_row = lax.broadcasted_iota(jnp.int32, scores.shape, 0)
            wide_col = lax.broadcasted_iota(jnp.int32, scores.shape, 1) % BLK
            begin = jnp.where(
                wide_col < HALF,
                table[1 + blocks + 2 * LO + 2 * m],
                table[2 + blocks + 2 * LO + 2 * m],
            )
            allowed = wide_row <= begin * BLK + core * HALF + wide_col % HALF
            probs = jnp.where(allowed, probs, 0.0)
        else:
            last = jnp.where(edge <= (m % 2) * (2 * BLK), probs[extent - 4 * BLK :], 0.0)
            if extent > 4 * BLK:
                probs = jnp.concatenate([probs[: extent - 4 * BLK], last], axis=0)
            else:
                probs = last
        grad_probs = dot(vs[span, :], cot_pair, 1, 1)
        grad_scores = (probs * (grad_probs - delta)).astype(BF)
        dvs[span, :] += dot(probs.astype(BF), cot_pair, 1, 0)
        dks[span, :] += dot(grad_scores, pair, 1, 0)
        dqs[rows, :] = one_tile(dot(grad_scores, ks[span, :], 0, 0)) * scale

    if full:
        lax.fori_loop(0, len(tiles), lambda m, carry: (tile(m, tiles[0]), carry)[1], 0)
    else:
        for m in range(0, len(tiles), 2):
            lax.fori_loop(m, m + 2, lambda i, carry: (tile(i, tiles[m]), carry)[1], 0)
    for i in range(2 * LO):
        place = table[1 + blocks + i]
        dq[pl.ds(i * HALF, HALF), :] = dqs[
            pl.ds(pl.multiple_of(place * HALF, HALF), HALF), :
        ]
    for i in range(blocks):
        place = table[1 + i]
        rows = pl.ds(i * HALF, HALF)
        own = pl.ds(pl.multiple_of(place * BLK + core * HALF, HALF), HALF)
        other = pl.ds(pl.multiple_of(place * BLK + (1 - core) * HALF, HALF), HALF)
        dk_own[rows, :] = dks[own, :] * scale
        dv_own[rows, :] = dvs[own, :]
        sent[0, rows, :] = pltpu.roll(dks[other, :] * scale, HD, 1).astype(BF)
        sent[1, rows, :] = pltpu.roll(dvs[other, :], HD, 1).astype(BF)


def attend_back(tiles, blocks, table, q, k_own, v_own, k_other, v_other, cot, att, log_in):
    tokens = q.shape[0]
    keys = blocks * BLK
    return pl.pallas_call(
        functools.partial(attend_back_kernel, tiles, blocks),
        out_shape=(
            jax.ShapeDtypeStruct((tokens, 128), F32),
            jax.ShapeDtypeStruct((keys // 2, 128), F32),
            jax.ShapeDtypeStruct((keys // 2, 128), F32),
            jax.ShapeDtypeStruct((2, keys // 2, 128), BF),
        ),
        in_specs=[pl.BlockSpec(memory_space=pltpu.SMEM)] + full_spec(8),
        out_specs=tuple(full_spec(4)),
        scratch_shapes=[
            pltpu.VMEM((tokens, 128), BF),
            pltpu.VMEM((keys, 128), BF),
            pltpu.VMEM((keys, 128), BF),
            pltpu.VMEM((tokens, 128), BF),
            pltpu.VMEM((tokens, 128), F32),
            pltpu.VMEM((tokens, 128), F32),
            pltpu.VMEM((tokens, 128), F32),
            pltpu.VMEM((keys, 128), F32),
            pltpu.VMEM((keys, 128), F32),
        ],
        cost_estimate=pl.CostEstimate(
            flops=20 * 256 * 128 * sum(tiles),
            bytes_accessed=6000000,
            transcendentals=256 * sum(tiles),
        ),
        name="attend_back",
    )(table, q, k_own, v_own, k_other, v_other, cot, att, log_in)


def front_kernel(
    place,
    firsts,
    firsts_y,
    seconds,
    seconds_x,
    gain,
    shift,
    qkv,
    bias_joint,
    cosine,
    sine_a,
    sine_b,
    fc1_own,
    fc1_other,
    bias1,
    normed,
    mean,
    inv,
    queries,
    keys,
    values,
    sent,
    pre,
    active,
):
    sides = sides_of(place)
    rows = [
        part.astype(F32)
        for part in piece_rows(pl.program_id(0), firsts, firsts_y, seconds, seconds_x)
    ]
    center = sum(jnp.sum(part, axis=-1, keepdims=True) for part in rows) / D
    rows = [part - center for part in rows]
    spread_ = sum(jnp.sum(part * part, axis=-1, keepdims=True) for part in rows) / D
    inv_std = lax.rsqrt(spread_ + epsilon)
    mean[...] = jnp.broadcast_to(center, mean.shape)
    inv[...] = jnp.broadcast_to(inv_std, inv.shape)
    for part, side in zip(rows, sides):
        normed[:, side] = (part * inv_std * gain[:, side] + shift[:, side]).astype(BF)
    normed16 = normed[...]
    joint = dot(normed16, qkv[...], 1, 0) + bias_joint[...]
    tables = (cosine[...], sine_a[...], sine_b[...])
    queries[...] = turn(joint[:, :BLK], *tables).astype(BF)
    turned, value = turn(joint[:, BLK : 2 * BLK], *tables), joint[:, 2 * BLK :]
    keys[...] = turned.astype(BF)
    values[...] = value.astype(BF)
    sent[0] = pltpu.roll(turned, HD, 1).astype(BF)
    sent[1] = pltpu.roll(value, HD, 1).astype(BF)
    hidden = fc1_own.shape[1]
    for part, weight in enumerate((fc1_own, fc1_other)):
        columns = slice(part * hidden, (part + 1) * hidden)
        result = dot(normed16, weight[...], 1, 0) + bias1[:, columns]
        pre[:, columns] = result
        inner = jnp.tanh(inner_coef * (result + cubic_coef * result * result * result))
        active[:, columns] = (0.5 * result * (1.0 + inner)).astype(BF)


def front(place, pieces, gain, shift, qkv, bias_joint, cosine, sine_a, sine_b, fc1_own, fc1_other, bias1):
    tokens = LO * BLK
    hidden = fc1_own.shape[1]

    def shape(columns, dtype):
        return jax.ShapeDtypeStruct((tokens, columns), dtype)

    narrow = rows_spec(BLK)
    return pl.pallas_call(
        front_kernel,
        grid=(tokens // STEP,),
        out_shape=(
            shape(D, BF),
            shape(BLK, F32),
            shape(BLK, F32),
            shape(BLK, BF),
            shape(BLK, BF),
            shape(BLK, BF),
            jax.ShapeDtypeStruct((2, tokens, BLK), BF),
            shape(2 * hidden, F32),
            shape(2 * hidden, BF),
        ),
        in_specs=[
            scalar_spec(),
            *piece_specs(),
            fixed_spec(1, D),
            fixed_spec(1, D),
            fixed_spec(D, 3 * BLK),
            fixed_spec(1, 3 * BLK),
            narrow,
            narrow,
            narrow,
            fixed_spec(D, hidden),
            fixed_spec(D, hidden),
            fixed_spec(1, 2 * hidden),
        ],
        out_specs=(
            rows_spec(D),
            narrow,
            narrow,
            narrow,
            narrow,
            narrow,
            pl.BlockSpec((2, STEP, BLK), lambda i: (0, i, 0)),
            rows_spec(2 * hidden),
            rows_spec(2 * hidden),
        ),
        cost_estimate=cost(2 * tokens * D * (384 + 2 * hidden), 12 * tokens * D // 2),
        name="front",
    )(
        place,
        *pieces,
        gain,
        shift,
        qkv,
        bias_joint,
        cosine,
        sine_a,
        sine_b,
        fc1_own,
        fc1_other,
        bias1,
    )


def store_pieces(step, index, rows, a_own, a_other, b_near, b_far):
    for s in range(2):
        (a_own, a_other)[index][s] = rows[s * BLK : s * BLK + HALF]
    for wanted, target in ((step < 2, b_near), (step >= 2, b_far)):

        @pl.when(wanted)
        def _(target=target):
            for s in range(2):
                target[s, index] = rows[s * BLK + HALF : (s + 1) * BLK]


def partial_shapes():
    return (
        jax.ShapeDtypeStruct((LO, HALF, UNIT), BF),
        jax.ShapeDtypeStruct((LO, HALF, UNIT), BF),
        jax.ShapeDtypeStruct((LO // 2, 2, HALF, UNIT), BF),
        jax.ShapeDtypeStruct((LO // 2, 2, HALF, UNIT), BF),
    )


def partial_specs():
    near = pl.BlockSpec((2, HALF, UNIT), lambda i: (i, 0, 0))
    return (
        near,
        near,
        pl.BlockSpec((2, 2, HALF, UNIT), lambda i: (jnp.minimum(i, 1), 0, 0, 0)),
        pl.BlockSpec((2, 2, HALF, UNIT), lambda i: (jnp.maximum(i - 2, 0), 0, 0, 0)),
    )


def mix_kernel(place, attended, active, out2, fc2_own, fc2_other, *partial):
    hidden = fc2_own.shape[1]
    for index, side in enumerate((place[0], 1 - place[0])):
        parts = []
        for quarter in range(4):
            c = 4 * side + quarter
            parts.append(
                (
                    dot(active[:, :hidden], fc2_own[c], 1, 0)
                    + dot(active[:, hidden:], fc2_other[c], 1, 0)
                    + dot(attended[...], out2[c], 1, 0)
                ).astype(BF)
            )
        store_pieces(pl.program_id(0), index, jnp.concatenate(parts, axis=1), *partial)


def mix(place, attended, active, out2, fc2_own, fc2_other):
    tokens = LO * BLK
    hidden = fc2_own.shape[1]
    return pl.pallas_call(
        mix_kernel,
        grid=(tokens // STEP,),
        out_shape=partial_shapes(),
        in_specs=[
            scalar_spec(),
            rows_spec(BLK),
            rows_spec(2 * hidden),
            fixed_spec(LO, BLK, 256),
            fixed_spec(LO, hidden, 256),
            fixed_spec(LO, hidden, 256),
        ],
        out_specs=partial_specs(),
        cost_estimate=cost(2 * tokens * D * (128 + 2 * hidden), 8000000),
        name="mix",
    )(place, attended, active, out2, fc2_own, fc2_other)


def back_kernel(
    place,
    firsts,
    firsts_y,
    seconds,
    seconds_x,
    pre,
    out2,
    fc2_own,
    fc2_other,
    cot,
    grad_pre,
    grad_attended,
    bias_sum,
):
    @pl.when(pl.program_id(0) == 0)
    def _():
        bias_sum[...] = jnp.zeros_like(bias_sum)

    parts = piece_rows(pl.program_id(0), firsts, firsts_y, seconds, seconds_x)
    for part, side in zip(parts, sides_of(place)):
        cot[:, side] = part
    rows = cot[...]
    hidden = fc2_own.shape[1]

    def through(weight):
        total = 0.0
        for c in range(LO):
            total = total + dot(rows[:, c * 256 : (c + 1) * 256], weight[c], 1, 1)
        return total

    grad_attended[...] = through(out2).astype(BF)
    for part, weight in enumerate((fc2_own, fc2_other)):
        columns = slice(part * hidden, (part + 1) * hidden)
        value = pre[:, columns]
        inner = jnp.tanh(inner_coef * (value + cubic_coef * value * value * value))
        slope = 0.5 * (1.0 + inner) + 0.5 * value * (1.0 - inner * inner) * inner_coef * (
            1.0 + 3.0 * cubic_coef * value * value
        )
        grad = through(weight) * slope
        bias_sum[:, columns] += jnp.sum(grad, axis=0, keepdims=True)
        grad_pre[:, columns] = grad.astype(BF)


def back(place, pieces, pre, out2, fc2_own, fc2_other):
    tokens = LO * BLK
    hidden = fc2_own.shape[1]
    return pl.pallas_call(
        back_kernel,
        grid=(tokens // STEP,),
        out_shape=(
            jax.ShapeDtypeStruct((tokens, D), BF),
            jax.ShapeDtypeStruct((tokens, 2 * hidden), BF),
            jax.ShapeDtypeStruct((tokens, BLK), BF),
            jax.ShapeDtypeStruct((1, 2 * hidden), F32),
        ),
        in_specs=[
            scalar_spec(),
            *piece_specs(),
            rows_spec(2 * hidden),
            fixed_spec(LO, BLK, 256),
            fixed_spec(LO, hidden, 256),
            fixed_spec(LO, hidden, 256),
        ],
        out_specs=(
            rows_spec(D),
            rows_spec(2 * hidden),
            rows_spec(BLK),
            fixed_spec(1, 2 * hidden),
        ),
        cost_estimate=cost(2 * tokens * D * (128 + 2 * hidden), 14000000),
        name="back",
    )(place, *pieces, pre, out2, fc2_own, fc2_other)


def unturn_kernel(dq, dk, dv, got, cosine, sine_a, sine_b, joint, own, other, bias):
    tables = (cosine[...], -sine_a[...], -sine_b[...])
    dk_all = dk[...] + got[0].astype(F32)
    dv_all = dv[...] + got[1].astype(F32)
    for j, grads in enumerate((turn(dq[...], *tables), turn(dk_all, *tables), dv_all)):
        columns = slice(j * BLK, (j + 1) * BLK)
        bias[:, columns] = jnp.sum(grads, axis=0, keepdims=True)
        grads = grads.astype(BF)
        joint[:, columns] = grads
        own[:, j * HD : (j + 1) * HD] = grads[:, :HD]
        other[:, j * HD : (j + 1) * HD] = grads[:, HD:]


def unturn(dq, dk, dv, got, cosine, sine_a, sine_b):
    tokens = dq.shape[0]
    return pl.pallas_call(
        unturn_kernel,
        out_shape=(
            jax.ShapeDtypeStruct((tokens, 3 * BLK), BF),
            jax.ShapeDtypeStruct((tokens, 3 * HD), BF),
            jax.ShapeDtypeStruct((tokens, 3 * HD), BF),
            jax.ShapeDtypeStruct((1, 3 * BLK), F32),
        ),
        in_specs=full_spec(7),
        out_specs=tuple(full_spec(4)),
        cost_estimate=cost(0, 6000000),
        name="unturn",
    )(dq, dk, dv, got, cosine, sine_a, sine_b)


def grad_kernel(
    place,
    firsts,
    firsts_y,
    seconds,
    seconds_x,
    mean,
    inv,
    gain,
    joint,
    grad_pre,
    qkv,
    fc1_own,
    fc1_other,
    a_own,
    a_other,
    b_near,
    b_far,
    sums,
    gain_sum,
    shift_sum,
):
    step = pl.program_id(0)

    @pl.when(step == 0)
    def _():
        gain_sum[...] = jnp.zeros_like(gain_sum)
        shift_sum[...] = jnp.zeros_like(shift_sum)

    hidden = fc1_own.shape[1]
    parts = piece_rows(step, firsts, firsts_y, seconds, seconds_x)
    first, second = 0.0, 0.0
    for index, (side, part) in enumerate(zip(sides_of(place), parts)):
        grads = (
            dot(joint[...], qkv[side, :], 1, 1)
            + dot(grad_pre[:, :hidden], fc1_own[side, :], 1, 1)
            + dot(grad_pre[:, hidden:], fc1_other[side, :], 1, 1)
        )
        store_pieces(step, index, grads.astype(BF), a_own, a_other, b_near, b_far)
        both = grads * ((part.astype(F32) - mean[:, :1]) * inv[:, :1])
        shift_sum[index : index + 1, :] += jnp.sum(grads, axis=0, keepdims=True)
        gain_sum[index : index + 1, :] += jnp.sum(both, axis=0, keepdims=True)
        first = first + jnp.sum(grads * gain[:, side], axis=-1, keepdims=True)
        second = second + jnp.sum(both * gain[:, side], axis=-1, keepdims=True)
    lane = lax.broadcasted_iota(jnp.int32, (STEP, BLK), 1)
    turned = jnp.transpose(jnp.where(lane < HD, first, second))
    sums[0:1, :] = turned[0:1]
    sums[1:2, :] = turned[HD : HD + 1]


def grad_units(place, pieces, mean, inv, gain, joint, grad_pre, qkv, fc1_own, fc1_other):
    tokens = LO * BLK
    hidden = fc1_own.shape[1]
    return pl.pallas_call(
        grad_kernel,
        grid=(tokens // STEP,),
        out_shape=(
            *partial_shapes(),
            jax.ShapeDtypeStruct((2, tokens), F32),
            jax.ShapeDtypeStruct((2, UNIT), F32),
            jax.ShapeDtypeStruct((2, UNIT), F32),
        ),
        in_specs=[
            scalar_spec(),
            *piece_specs(),
            rows_spec(BLK),
            rows_spec(BLK),
            fixed_spec(1, D),
            rows_spec(3 * BLK),
            rows_spec(2 * hidden),
            fixed_spec(D, 3 * BLK),
            fixed_spec(D, hidden),
            fixed_spec(D, hidden),
        ],
        out_specs=(
            *partial_specs(),
            pl.BlockSpec((2, STEP), lambda i: (0, i)),
            fixed_spec(2, UNIT),
            fixed_spec(2, UNIT),
        ),
        cost_estimate=cost(2 * tokens * D * (384 + 2 * hidden), 16000000),
        name="grad",
    )(place, *pieces, mean, inv, gain, joint, grad_pre, qkv, fc1_own, fc1_other)


def step_body(
    n_hi,
    layer_input,
    norm_gain,
    norm_shift,
    w_qkv,
    b_qkv,
    w_out,
    b_out,
    w_fc1,
    b_fc1,
    w_fc2,
    b_fc2,
    grad_output,
    placement,
    position_ids,
):
    hi, y, k = (lax.axis_index(name) for name in ("hi", "y", "k"))
    lo = lax.axis_index(LOX)
    depth = D // (n_hi * LO)
    width = w_qkv.shape[2]
    hidden = w_fc1.shape[1] // LO
    tokens = LO * BLK

    def half(values, which):
        split = values.reshape((2, 2, HALF) + values.shape[1:])
        cut = lax.dynamic_index_in_dim(split, which, 1, keepdims=False)
        return cut.reshape((BLK,) + values.shape[1:])

    def in_order(index, own, got, axis):
        return jnp.where(
            index == 0,
            jnp.concatenate([own, got], axis=axis),
            jnp.concatenate([got, own], axis=axis),
        )

    def make_unit(values):
        got = swap(half(values, 1 - k), "k")
        return in_order(k, half(values, k), got, 1)

    unit_in = make_unit(layer_input)
    pieces = gather_pieces(unit_in)
    unit_cot = make_unit(grad_output)
    pieces_cot = gather_pieces(unit_cot)
    ids = half(position_ids, k)
    for name in ("zh", "zl", "x"):
        ids = jnp.stack([ids, swap(ids, name)])
    ids, w_fc1, w_qkv, w_fc2, w_out = lax.optimization_barrier((ids, w_fc1, w_qkv, w_fc2, w_out))
    slot_lo = [lo ^ (((s & 1) << 2) | (s & 2) | (s >> 2)) for s in range(LO)]
    place = jnp.stack([y, k] + slot_lo).astype(jnp.int32)

    def over_hi(values):
        return values[None] if n_hi == 1 else lax.all_gather(values, "hi", axis=0)

    def ordered(got, shape):
        return got if n_hi == 1 else jnp.moveaxis(got, 1, 0).reshape(shape)

    fc1_own = spread(over_hi(w_fc1).reshape(n_hi, depth, LO, hidden).transpose(2, 0, 1, 3))
    fc1_own = ordered(fc1_own, (D, hidden)).reshape(D, hidden)
    fc1_other = swap(fc1_own, "k")
    down = jnp.concatenate(
        [w_fc2.reshape(LO, hidden, depth), w_out.reshape(LO, HD, depth)], axis=1
    )
    down = spread(jnp.moveaxis(over_hi(down), 0, 1))
    if n_hi == 1:
        down_own = down.reshape(LO, hidden + HD, 256)
    else:
        down_own = down.transpose(2, 1, 0, 3).reshape(hidden + HD, LO, 256).transpose(1, 0, 2)
    down_other = swap(down_own, "k")
    fc2_own, fc2_other = down_own[:, :hidden], down_other[:, :hidden]
    out2 = jnp.concatenate([down_own[:, hidden:], down_other[:, hidden:]], axis=1)
    if n_hi == 1:
        heads_own = spread(pack_heads(w_qkv.transpose(1, 0, 2)))
        qkv = join_heads(heads_own, swap(heads_own, "k"))
    else:
        cut = over_hi(w_qkv).reshape(n_hi, depth, 3, LO, HD).transpose(3, 0, 1, 2, 4)
        heads_own = spread(cut.reshape(LO, n_hi, depth, 3 * HD))
        heads_own = ordered(heads_own, (D, 3, HD))
        qkv = jnp.concatenate([heads_own, swap(heads_own, "k")], axis=2).reshape(D, 6 * HD)

    own_head = lax.dynamic_slice_in_dim(b_qkv, lo * HD, HD, 1)
    own_bias1 = lax.dynamic_slice_in_dim(b_fc1, lo * hidden, hidden, 0)
    affine = jnp.stack([norm_gain.astype(F32), norm_shift.astype(F32)])
    small = jnp.concatenate([affine.reshape(-1), own_head.reshape(-1), own_bias1])
    small_other = swap(small, "k")
    affine = in_order(k, affine, small_other[: 2 * width].reshape(2, width), 1)
    affine = in_order(y, affine, swap(affine, "y"), 1)
    gain, shift = affine[0:1], affine[1:2]
    head_other = small_other[2 * width : 2 * width + 3 * HD].reshape(3, HD)
    bias_joint = jnp.concatenate([own_head, head_other], axis=1).reshape(1, 6 * HD)
    bias1 = jnp.concatenate([own_bias1, small_other[2 * width + 3 * HD :]])[None]

    ids = ids.reshape(tokens)
    lane = jnp.arange(BLK, dtype=jnp.int32) % HD
    frequency = 10000.0 ** (-2.0 * (lane % (ROT // 2)).astype(F32) / ROT)
    angles = ids.astype(F32)[:, None] * frequency[None, :]
    cosine = jnp.where(lane < ROT, jnp.cos(angles), 1.0)
    sine = jnp.sin(angles)
    sine_a = jnp.where(lane < ROT // 2, -sine, 0.0)
    sine_b = jnp.where((lane >= ROT // 2) & (lane < ROT), sine, 0.0)

    blocks = n_hi * 2 * LO
    by_group = placement.reshape(n_hi, LO, 2)
    in_slots = jnp.stack(
        [lax.dynamic_index_in_dim(by_group, c, 1, keepdims=False) for c in slot_lo], axis=1
    ).reshape(n_hi, 2 * LO)
    local = lax.dynamic_index_in_dim(in_slots, hi, 0, keepdims=False)
    ranks = jnp.sum((local[None, :] < local[:, None]).astype(jnp.int32), axis=1)
    sorted_local = jnp.sort(local) if n_hi > 1 else jnp.arange(2 * LO, dtype=jnp.int32)
    table = jnp.concatenate(
        [k[None].astype(jnp.int32), in_slots.reshape(-1), ranks, sorted_local]
    )
    if n_hi == 1:
        tiles = tuple(4 * BLK * (m // 2 + 1) for m in range(LO))
    else:
        tiles = (blocks * BLK,) * LO

    normed16, mean, inv, queries, keys, values, sent, pre, active = front(
        place,
        pieces,
        gain,
        shift,
        qkv,
        bias_joint,
        cosine,
        sine_a,
        sine_b,
        fc1_own,
        fc1_other,
        bias1,
    )
    other_kv = swap(sent, "k")

    def all_keys(rows):
        return rows if n_hi == 1 else lax.all_gather(rows, "hi", axis=0, tiled=True)

    key_set = tuple(all_keys(v) for v in (keys, values, other_kv[0], other_kv[1]))
    attended, log_total = attend(tiles, blocks, table, queries, *key_set)
    summed = scatter_pieces(*mix(place, attended, active, out2, fc2_own, fc2_other))

    cot, grad_pre, grad_attended, term_bias1 = back(place, pieces_cot, pre, out2, fc2_own, fc2_other)

    def summed_dot(left, own, other, flip):
        def product(right):
            return dot(right, left, 0, 0) if flip else dot(left, right, 0, 0)

        return product(own), swap(product(other).astype(BF), "k")

    def home(total):
        got = spread(total)
        if n_hi == 1:
            return got[:, 0]
        return lax.psum_scatter(got.astype(F32), "hi", scatter_dimension=1)

    def add(own, got):
        return (own + got.astype(F32)).astype(BF)

    def cut_columns(values):
        rows = values.shape[0]
        return values.reshape(rows, n_hi, LO, depth).transpose(2, 1, 0, 3)

    fc2_sum = add(*summed_dot(cot, active[:, :hidden], active[:, hidden:], True))
    out_sum = add(*summed_dot(cot, attended[:, :HD], attended[:, HD:], True))
    down = jnp.concatenate([cut_columns(fc2_sum), cut_columns(out_sum)], axis=2)
    fc1_term, fc1_got = summed_dot(normed16, grad_pre[:, :hidden], grad_pre[:, hidden:], False)
    if n_hi == 1:
        grad_attended, down, fc1_term, fc1_got = lax.optimization_barrier(
            (grad_attended, down, fc1_term, fc1_got)
        )
    down_home = home(down)
    grad_fc2 = down_home[:, :hidden].reshape(LO * hidden, depth).astype(F32)
    grad_out = down_home[:, hidden:].reshape(LO * HD, depth).astype(F32)

    dq, dk, dv, grads_sent = attend_back(
        tiles, blocks, table, queries, *key_set, grad_attended, attended, log_total
    )

    def own_keys(rows):
        if n_hi == 1:
            return rows
        return lax.psum_scatter(rows, "hi", scatter_dimension=0, tiled=True)

    got = swap(grads_sent, "k")
    if n_hi > 1:
        dk = own_keys(dk + got[0].astype(F32))
        dv = own_keys(dv + got[1].astype(F32))
        got = jnp.zeros((2,) + dk.shape, BF)
    joint, joint_own, joint_other, term_joint_bias = unturn(
        dq, dk, dv, got, cosine, sine_a, sine_b
    )
    own_term, got_term = summed_dot(normed16, joint_own, joint_other, False)
    if n_hi == 1:
        packed = pack_grads(fc1_term, fc1_got, own_term, got_term)
        packed, joint = lax.optimization_barrier((packed, joint))
        grad_fc1, grad_qkv = home_grads(spread(packed))
        grad_qkv = grad_qkv.transpose(1, 0, 2)
    else:
        fc1_sum = add(fc1_term, fc1_got).reshape(n_hi, LO, depth, hidden)
        fc1_home = home(fc1_sum.transpose(1, 0, 2, 3))
        grad_fc1 = fc1_home.transpose(1, 0, 2).reshape(depth, LO * hidden).astype(F32)
        qkv_sum = add(own_term, got_term).reshape(n_hi, LO, depth, 3 * HD)
        qkv_home = home(qkv_sum.transpose(1, 0, 2, 3)).reshape(LO, depth, 3, HD)
        grad_qkv = qkv_home.transpose(1, 2, 0, 3).reshape(depth, 3, width).astype(F32)
    *partial, row_sums, gain_sum, shift_sum = grad_units(
        place, pieces, mean, inv, gain, joint, grad_pre, qkv, fc1_own, fc1_other
    )
    grad_unit = scatter_pieces(*partial)

    heads = lax.dynamic_update_slice(
        jnp.zeros((2, 3, width), F32),
        term_joint_bias.reshape(3, 2, HD).transpose(1, 0, 2),
        (0, 0, lo * HD),
    )
    bias_sum = lax.dynamic_update_slice(
        jnp.zeros((2, LO * hidden), F32), term_bias1.reshape(2, hidden), (0, lo * hidden)
    )
    affine_sum = jnp.stack([gain_sum, shift_sum]).reshape(2, 2, 2, width).transpose(1, 2, 0, 3)

    def pick(values, index):
        return lax.dynamic_index_in_dim(values, index, 0, keepdims=False)

    row_pair = row_sums.reshape(-1)
    over_y = jnp.concatenate([affine_sum[1].reshape(-1), row_pair])
    over_y = swap(over_y, "y")
    affine_sum = affine_sum[0] + over_y[: 4 * width].reshape(2, 2, width)
    row_pair = (row_pair + over_y[4 * width :]).reshape(2, tokens)
    over_k = jnp.concatenate(
        [heads[1].reshape(-1), bias_sum[1], pick(affine_sum, 1 - k).reshape(-1)]
    )
    over_k = swap(over_k, "k") + jnp.concatenate(
        [heads[0].reshape(-1), bias_sum[0], pick(affine_sum, k).reshape(-1)]
    )
    local_bias = jnp.sum(grad_output.astype(F32), axis=0)
    flat = jnp.concatenate([over_k, local_bias])
    length = flat.shape[0]
    for name in ("x", "zl", "zh"):
        left = row_pair.shape[1] // 2
        got = swap(jnp.concatenate([flat, row_pair[:, left:].reshape(-1)]), name)
        flat = flat + got[:length]
        row_pair = row_pair[:, :left] + got[length:].reshape(2, left)
    row_own = row_pair.T / D
    if n_hi > 1:
        flat = lax.psum(flat, "hi")
    cuts = [3 * width, LO * hidden, width, width, width]
    ends = [sum(cuts[: i + 1]) for i in range(len(cuts))]
    grad_b_qkv = flat[: ends[0]].reshape(3, width)
    grad_b_fc1 = flat[ends[0] : ends[1]]
    grad_gain = flat[ends[1] : ends[2]]
    grad_shift = flat[ends[2] : ends[3]]
    grad_b_out = flat[ends[3] :]

    def to_rows(unit):
        parts = unit.reshape(BLK, 2, width)
        own = lax.dynamic_index_in_dim(parts, k, 1, keepdims=False)
        got = swap(lax.dynamic_index_in_dim(parts, 1 - k, 1, keepdims=False), "k")
        own, got = own.reshape(2, 1, HALF, width), got.reshape(2, 1, HALF, width)
        return in_order(k, own, got, 1).reshape(2 * BLK, width)

    layer_output = layer_input.astype(F32) + to_rows(summed) + b_out + b_fc2

    mean_own, inv_own = mean[:BLK, :1], inv[:BLK, :1]
    gain_own = lax.dynamic_slice_in_dim(gain, y * UNIT, UNIT, 1)
    normed_unit = (unit_in.astype(F32) - mean_own) * inv_own
    grad_x = inv_own * (
        grad_unit * gain_own - row_own[:, :1] - normed_unit * row_own[:, 1:]
    )
    grad_input = to_rows(grad_x + unit_cot.astype(F32))
    return (
        layer_output,
        grad_input,
        grad_gain,
        grad_shift,
        grad_qkv,
        grad_b_qkv,
        grad_out,
        grad_b_out,
        grad_fc1,
        grad_b_fc1,
        grad_fc2,
        grad_b_out,
    )


def on_device(n_hi, *arguments):
    return step_body(n_hi, *arguments)


def solution(mesh):
    n_hi = mesh.shape["ctx"] // LO
    inner = Mesh(mesh.devices.reshape(n_hi, 2, 2, 2, 2, 2), CTX + TP)
    in_specs = (
        P(CTX, TP),
        P(TP),
        P(TP),
        P(CTX, None, TP),
        P(None, TP),
        P(TP, CTX),
        P(TP),
        P(CTX, TP),
        P(TP),
        P(TP, CTX),
        P(TP),
        P(CTX, TP),
        P(),
        P(CTX),
    )
    out_specs = (
        P(CTX, TP),
        P(CTX, TP),
        P(TP),
        P(TP),
        P(CTX, None, TP),
        P(None, TP),
        P(TP, CTX),
        P(TP),
        P(CTX, TP),
        P(TP),
        P(TP, CTX),
        P(TP),
    )
    return jax.shard_map(
        functools.partial(on_device, n_hi),
        mesh=inner,
        in_specs=in_specs,
        out_specs=out_specs,
        check_vma=False,
    )
```

```python
import functools
import math

import jax
import jax.numpy as jnp
from jax import lax
from jax.experimental import pallas as pl
from jax.experimental.pallas import tpu as pltpu
from jax.sharding import Mesh, PartitionSpec as P


D = 2048
HD = 64
ROT = 32
BLK = 128
HALF = BLK // 2
LO = 8
UNIT = 1024
STEP = 256
IDS = 16

epsilon = 1e-05
cubic_coef = 0.044715
inner_coef = math.sqrt(2.0 / math.pi)
neg_large = -1e30
BF = jnp.bfloat16
F32 = jnp.float32
LOX = ("zh", "zl", "x")
CTX = ("hi",) + LOX
TP = ("y", "k")


def swap(values, axis):
    return lax.ppermute(values, axis, [(0, 1), (1, 0)])


def spread(pieces):
    return lax.all_to_all(pieces, LOX, 0, 0, tiled=True)


def gather_pieces(unit):
    unit = unit.reshape(2, HALF, UNIT)
    pair = jnp.stack([unit, swap(unit, "zh")])
    quad = jnp.concatenate([pair, swap(pair, "zl")])
    first, second = quad[:, 0], quad[:, 1]
    first_x = swap(first, "x")
    second_y = swap(second, "y")
    first_y = swap(first, "y")
    second_x = swap(second, "x")
    first_xy = swap(first_x, "y")
    second_yx = swap(second_y, "x")
    return first, first_x, first_y, first_xy, second, second_x, second_y, second_yx


def scatter_pieces(a_own, a_other, b_near, b_far):
    def add(left, right):
        return left.astype(F32) + right.astype(F32)

    a_own = add(a_own, swap(a_other, "y")).astype(BF)
    b_near = add(b_near, swap(b_far, "x")).astype(BF)
    a_own = add(a_own[:4], swap(a_own[4:], "x")).astype(BF)
    b_near = add(b_near[:, 0], swap(b_near[:, 1], "y")).astype(BF)
    both = jnp.stack([a_own, b_near], axis=1)
    both = add(both[:2], swap(both[2:], "zl")).astype(BF)
    return add(both[0], swap(both[1], "zh")).reshape(BLK, UNIT)


def full_spec(count):
    return [pl.BlockSpec(memory_space=pltpu.VMEM) for _ in range(count)]


def dot(left, right, left_dim, right_dim):
    return lax.dot_general(
        left, right, (((left_dim,), (right_dim,)), ((), ())), preferred_element_type=F32
    )


def cost(flops, size):
    return pl.CostEstimate(flops=flops, bytes_accessed=size, transcendentals=0)


def rows_spec(columns, step=STEP):
    return pl.BlockSpec((step, columns), lambda i: (i, 0))


def fixed_spec(*shape):
    return pl.BlockSpec(shape, lambda i: (0,) * len(shape))


def scalar_spec():
    return pl.BlockSpec(memory_space=pltpu.SMEM)


PIECES = 8


def piece_specs():
    return [pl.BlockSpec((2, HALF, UNIT), lambda i: (i % 2, 0, 0)) for _ in range(PIECES)]


def piece_rows(step, pieces):
    near = step < 2
    chosen = [jnp.where(near, pieces[i][...], pieces[i + 1][...]) for i in (0, 2, 4, 6)]
    return [
        jnp.concatenate([first[0], second[0], first[1], second[1]], axis=0)
        for first, second in ((chosen[0], chosen[2]), (chosen[1], chosen[3]))
    ]


def sides_of(place):
    y = place[0]
    return [
        pl.ds(pl.multiple_of(y * UNIT, UNIT), UNIT),
        pl.ds(pl.multiple_of((1 - y) * UNIT, UNIT), UNIT),
    ]


def pack_kernel(weight, ids, out):
    for c in range(LO):
        out[c, 3 * BLK :] = ids[...]
        columns = slice(c * HD, (c + 1) * HD)
        for j in range(3):
            out[c, j * BLK : (j + 1) * BLK] = jnp.concatenate(
                [weight[j, :BLK, columns], weight[j, BLK:, columns]], axis=1
            )


def pack_heads(weight, ids):
    return pl.pallas_call(
        pack_kernel,
        out_shape=jax.ShapeDtypeStruct((LO, 3 * BLK + IDS, BLK), BF),
        in_specs=full_spec(2),
        out_specs=full_spec(1)[0],
        cost_estimate=cost(0, 1600000),
        name="pack",
    )(weight, ids)


def join_kernel(own, other, out):
    for c in range(LO):
        for u in range(2):
            columns = slice(u * HD, (u + 1) * HD)
            rows = pl.ds(c * 2 * BLK + u * BLK, BLK)
            for j in range(3):
                out[rows, j * BLK : (j + 1) * BLK] = jnp.concatenate(
                    [
                        half[c, j * BLK : (j + 1) * BLK, columns]
                        for half in (own, other)
                    ],
                    axis=1,
                )


def join_heads(own, other):
    return pl.pallas_call(
        join_kernel,
        out_shape=jax.ShapeDtypeStruct((D, 3 * BLK), BF),
        in_specs=full_spec(2),
        out_specs=full_spec(1)[0],
        cost_estimate=cost(0, 3200000),
        name="join",
    )(own, other)


def pack_grad_kernel(fc1_own, fc1_other, own, other, out):
    for c in range(LO):
        rows = pl.ds(c * 2 * BLK, 2 * BLK)
        out[c, : 2 * BLK] = (fc1_own[rows, :] + fc1_other[rows, :].astype(F32)).astype(BF)
        tiles = []
        for j in range(3):
            columns = slice(j * HD, (j + 1) * HD)
            parts = []
            for u in range(2):
                rows = pl.ds(c * 2 * BLK + u * BLK, BLK)
                parts.append(own[rows, columns] + other[rows, columns].astype(F32))
            tiles.append(jnp.concatenate(parts, axis=1).astype(BF))
        out[c, 2 * BLK : 3 * BLK] = jnp.concatenate(tiles[:2], axis=1)
        out[c, 3 * BLK :] = jnp.concatenate([tiles[2][:HALF], tiles[2][HALF:]], axis=1)


def pack_grads(fc1_own, fc1_other, own, other):
    return pl.pallas_call(
        pack_grad_kernel,
        out_shape=jax.ShapeDtypeStruct((LO, 3 * BLK + HALF, 2 * BLK), BF),
        in_specs=full_spec(4),
        out_specs=full_spec(1)[0],
        cost_estimate=cost(0, 9000000),
        name="pack_grad",
    )(fc1_own, fc1_other, own, other)


def home_kernel(pieces, fc1, qkv):
    for c in range(LO):
        fc1[:, c * 256 : (c + 1) * 256] = pieces[c, : 2 * BLK].astype(F32)
    for c in range(0, LO, 2):
        for j in range(3):
            tiles = []
            for d in range(2):
                if j < 2:
                    tiles.append(pieces[c + d, 2 * BLK : 3 * BLK, j * BLK : (j + 1) * BLK])
                else:
                    tiles.append(
                        jnp.concatenate(
                            [pieces[c + d, 3 * BLK :, :BLK], pieces[c + d, 3 * BLK :, BLK:]],
                            axis=0,
                        )
                    )
            for u in range(2):
                columns = slice(u * HD, (u + 1) * HD)
                qkv[j, u * BLK : (u + 1) * BLK, c * HD : (c + 2) * HD] = jnp.concatenate(
                    [tile[:, columns] for tile in tiles], axis=1
                ).astype(F32)


def home_grads(pieces):
    return pl.pallas_call(
        home_kernel,
        out_shape=(
            jax.ShapeDtypeStruct((2 * BLK, LO * 256), F32),
            jax.ShapeDtypeStruct((3, 2 * BLK, LO * HD), F32),
        ),
        in_specs=full_spec(1),
        out_specs=tuple(full_spec(2)),
        cost_estimate=cost(0, 6000000),
        name="home",
    )(pieces)


def turn(values, cosine, sine_a, sine_b):
    return (
        values * cosine
        + pltpu.roll(values, 128 - ROT // 2, 1) * sine_a
        + pltpu.roll(values, ROT // 2, 1) * sine_b
    )


def sort_in(table, own, other, target, blocks):
    core = table[0]
    for i in range(blocks):
        place = table[1 + i]
        rows = pl.ds(i * HALF, HALF)
        target[pl.ds(pl.multiple_of(place * BLK + core * HALF, HALF), HALF), :] = own[rows, :]
        target[pl.ds(pl.multiple_of(place * BLK + (1 - core) * HALF, HALF), HALF), :] = other[
            rows, :
        ]


def two_heads(tile):
    lane = lax.broadcasted_iota(jnp.int32, tile.shape, 1)
    zero = jnp.zeros_like(tile)
    return jnp.concatenate(
        [jnp.where(lane < HD, tile, zero), jnp.where(lane < HD, zero, tile)], axis=0
    )


def one_tile(pair):
    rows = pair.shape[0] // 2
    lane = lax.broadcasted_iota(jnp.int32, (rows, pair.shape[1]), 1)
    return jnp.where(lane < HD, pair[:rows], pair[rows:])


def attend_kernel(
    tiles, blocks, table, q, k_own, v_own, k_other, v_other, out, log_out, qs, ks, vs, os, ls
):
    core = table[0]
    sort_in(table, k_own, k_other, ks, blocks)
    sort_in(table, v_own, v_other, vs, blocks)
    for i in range(2 * LO):
        place = table[1 + blocks + i]
        qs[pl.ds(pl.multiple_of(place * HALF, HALF), HALF), :] = q[pl.ds(i * HALF, HALF), :]
    scale = 1.0 / math.sqrt(HD)
    full = len(tiles) > 0 and tiles[0] == tiles[-1] and len(tiles) > 1
    row = lax.broadcasted_iota(jnp.int32, (2 * BLK, 4 * BLK), 0) % BLK
    col = lax.broadcasted_iota(jnp.int32, (2 * BLK, 4 * BLK), 1)
    edge = col - (row // HALF) * BLK - core * HALF - row % HALF

    def tile(m, extent):
        pair = two_heads(qs[pl.ds(pl.multiple_of(m * BLK, BLK), BLK), :])
        scores = dot(pair, ks[pl.ds(0, extent), :], 1, 1) * scale
        if full:
            wide_col = lax.broadcasted_iota(jnp.int32, scores.shape, 1)
            wide_row = lax.broadcasted_iota(jnp.int32, scores.shape, 0) % BLK
            begin = jnp.where(
                wide_row < HALF,
                table[1 + blocks + 2 * LO + 2 * m],
                table[2 + blocks + 2 * LO + 2 * m],
            )
            allowed = wide_col <= begin * BLK + core * HALF + wide_row % HALF
            scores = jnp.where(allowed, scores, neg_large)
        else:
            last = scores[:, extent - 4 * BLK :]
            last = jnp.where(edge <= (m % 2) * (2 * BLK), last, neg_large)
            if extent > 4 * BLK:
                scores = jnp.concatenate([scores[:, : extent - 4 * BLK], last], axis=1)
            else:
                scores = last
        top = jnp.max(scores, axis=-1, keepdims=True)
        weights = jnp.exp(scores - top)
        total = jnp.sum(weights, axis=-1, keepdims=True)
        probs = (weights * (1.0 / total)).astype(BF)
        mixed = dot(probs, vs[pl.ds(0, extent), :], 1, 0)
        os[pl.ds(pl.multiple_of(m * BLK, BLK), BLK), :] = one_tile(mixed)
        ls[pl.ds(pl.multiple_of(m * BLK, BLK), BLK), :] = one_tile(
            jnp.broadcast_to(top + jnp.log(total), (2 * BLK, 128))
        )

    if full:
        lax.fori_loop(0, len(tiles), lambda m, carry: (tile(m, tiles[0]), carry)[1], 0)
    else:
        for m in range(0, len(tiles), 2):
            lax.fori_loop(m, m + 2, lambda i, carry: (tile(i, tiles[m]), carry)[1], 0)
    for i in range(2 * LO):
        place = table[1 + blocks + i]
        rows = pl.ds(pl.multiple_of(place * HALF, HALF), HALF)
        out[pl.ds(i * HALF, HALF), :] = os[rows, :].astype(BF)
        log_out[pl.ds(i * HALF, HALF), :] = ls[rows, :]


def attend(tiles, blocks, table, q, k_own, v_own, k_other, v_other):
    tokens = q.shape[0]
    keys = blocks * BLK
    return pl.pallas_call(
        functools.partial(attend_kernel, tiles, blocks),
        out_shape=(
            jax.ShapeDtypeStruct((tokens, 128), BF),
            jax.ShapeDtypeStruct((tokens, 128), F32),
        ),
        in_specs=[pl.BlockSpec(memory_space=pltpu.SMEM)] + full_spec(5),
        out_specs=tuple(full_spec(2)),
        scratch_shapes=[
            pltpu.VMEM((tokens, 128), BF),
            pltpu.VMEM((keys, 128), BF),
            pltpu.VMEM((keys, 128), BF),
            pltpu.VMEM((tokens, 128), F32),
            pltpu.VMEM((tokens, 128), F32),
        ],
        cost_estimate=pl.CostEstimate(
            flops=8 * 256 * 128 * sum(tiles),
            bytes_accessed=2000000,
            transcendentals=256 * sum(tiles),
        ),
        name="attend",
    )(table, q, k_own, v_own, k_other, v_other)


def attend_back_kernel(
    tiles,
    blocks,
    table,
    q,
    k_own,
    v_own,
    k_other,
    v_other,
    cot,
    att,
    log_in,
    dq,
    dk_own,
    dv_own,
    sent,
    qs,
    ks,
    vs,
    cs,
    ps,
    ls,
    dqs,
    dks,
    dvs,
):
    core = table[0]
    sort_in(table, k_own, k_other, ks, blocks)
    sort_in(table, v_own, v_other, vs, blocks)
    for i in range(2 * LO):
        place = table[1 + blocks + i]
        rows = pl.ds(i * HALF, HALF)
        target = pl.ds(pl.multiple_of(place * HALF, HALF), HALF)
        qs[target, :] = q[rows, :]
        cs[target, :] = cot[rows, :]
        ps[target, :] = cot[rows, :].astype(F32) * att[rows, :].astype(F32)
        ls[target, :] = log_in[rows, :]
    dks[...] = jnp.zeros_like(dks)
    dvs[...] = jnp.zeros_like(dvs)
    scale = 1.0 / math.sqrt(HD)
    full = len(tiles) > 0 and tiles[0] == tiles[-1] and len(tiles) > 1
    col = lax.broadcasted_iota(jnp.int32, (4 * BLK, 2 * BLK), 1) % BLK
    row = lax.broadcasted_iota(jnp.int32, (4 * BLK, 2 * BLK), 0)
    edge = row - (col // HALF) * BLK - core * HALF - col % HALF

    def tile(m, extent):
        rows = pl.ds(pl.multiple_of(m * BLK, BLK), BLK)
        span = pl.ds(0, extent)
        pair = two_heads(qs[rows, :])
        cot_pair = two_heads(cs[rows, :])
        logs = jnp.transpose(ls[rows, :])
        log_row = jnp.concatenate([logs[0:1], logs[HD : HD + 1]], axis=1)
        products = jnp.transpose(ps[rows, :])
        delta = jnp.concatenate(
            [
                jnp.sum(products[:HD], axis=0, keepdims=True),
                jnp.sum(products[HD:], axis=0, keepdims=True),
            ],
            axis=1,
        )
        scores = dot(ks[span, :], pair, 1, 1) * scale
        probs = jnp.exp(scores - log_row)
        if full:
            wide_row = lax.broadcasted_iota(jnp.int32, scores.shape, 0)
            wide_col = lax.broadcasted_iota(jnp.int32, scores.shape, 1) % BLK
            begin = jnp.where(
                wide_col < HALF,
                table[1 + blocks + 2 * LO + 2 * m],
                table[2 + blocks + 2 * LO + 2 * m],
            )
            allowed = wide_row <= begin * BLK + core * HALF + wide_col % HALF
            probs = jnp.where(allowed, probs, 0.0)
        else:
            last = jnp.where(edge <= (m % 2) * (2 * BLK), probs[extent - 4 * BLK :], 0.0)
            if extent > 4 * BLK:
                probs = jnp.concatenate([probs[: extent - 4 * BLK], last], axis=0)
            else:
                probs = last
        grad_probs = dot(vs[span, :], cot_pair, 1, 1)
        grad_scores = (probs * (grad_probs - delta)).astype(BF)
        dvs[span, :] += dot(probs.astype(BF), cot_pair, 1, 0)
        dks[span, :] += dot(grad_scores, pair, 1, 0)
        dqs[rows, :] = one_tile(dot(grad_scores, ks[span, :], 0, 0)) * scale

    if full:
        lax.fori_loop(0, len(tiles), lambda m, carry: (tile(m, tiles[0]), carry)[1], 0)
    else:
        for m in range(0, len(tiles), 2):
            lax.fori_loop(m, m + 2, lambda i, carry: (tile(i, tiles[m]), carry)[1], 0)
    for i in range(2 * LO):
        place = table[1 + blocks + i]
        dq[pl.ds(i * HALF, HALF), :] = dqs[
            pl.ds(pl.multiple_of(place * HALF, HALF), HALF), :
        ]
    for i in range(blocks):
        place = table[1 + i]
        rows = pl.ds(i * HALF, HALF)
        own = pl.ds(pl.multiple_of(place * BLK + core * HALF, HALF), HALF)
        other = pl.ds(pl.multiple_of(place * BLK + (1 - core) * HALF, HALF), HALF)
        dk_own[rows, :] = dks[own, :] * scale
        dv_own[rows, :] = dvs[own, :]
        sent[0, rows, :] = pltpu.roll(dks[other, :] * scale, HD, 1).astype(BF)
        sent[1, rows, :] = pltpu.roll(dvs[other, :], HD, 1).astype(BF)


def attend_back(tiles, blocks, table, q, k_own, v_own, k_other, v_other, cot, att, log_in):
    tokens = q.shape[0]
    keys = blocks * BLK
    return pl.pallas_call(
        functools.partial(attend_back_kernel, tiles, blocks),
        out_shape=(
            jax.ShapeDtypeStruct((tokens, 128), F32),
            jax.ShapeDtypeStruct((keys // 2, 128), F32),
            jax.ShapeDtypeStruct((keys // 2, 128), F32),
            jax.ShapeDtypeStruct((2, keys // 2, 128), BF),
        ),
        in_specs=[pl.BlockSpec(memory_space=pltpu.SMEM)] + full_spec(8),
        out_specs=tuple(full_spec(4)),
        scratch_shapes=[
            pltpu.VMEM((tokens, 128), BF),
            pltpu.VMEM((keys, 128), BF),
            pltpu.VMEM((keys, 128), BF),
            pltpu.VMEM((tokens, 128), BF),
            pltpu.VMEM((tokens, 128), F32),
            pltpu.VMEM((tokens, 128), F32),
            pltpu.VMEM((tokens, 128), F32),
            pltpu.VMEM((keys, 128), F32),
            pltpu.VMEM((keys, 128), F32),
        ],
        cost_estimate=pl.CostEstimate(
            flops=20 * 256 * 128 * sum(tiles),
            bytes_accessed=6000000,
            transcendentals=256 * sum(tiles),
        ),
        name="attend_back",
    )(table, q, k_own, v_own, k_other, v_other, cot, att, log_in)


def front_kernel(place, *refs):
    front_body(place, refs[:PIECES], *refs[PIECES:])


def front_body(
    place,
    pieces,
    gain,
    shift,
    qkv,
    bias_joint,
    cosine,
    sine_a,
    sine_b,
    fc1_own,
    fc1_other,
    bias1,
    normed,
    mean,
    inv,
    queries,
    keys,
    values,
    sent,
    pre,
    active,
):
    sides = sides_of(place)
    rows = [
        part.astype(F32)
        for part in piece_rows(pl.program_id(0), pieces)
    ]
    center = sum(jnp.sum(part, axis=-1, keepdims=True) for part in rows) / D
    rows = [part - center for part in rows]
    spread_ = sum(jnp.sum(part * part, axis=-1, keepdims=True) for part in rows) / D
    inv_std = lax.rsqrt(spread_ + epsilon)
    mean[...] = jnp.broadcast_to(center, mean.shape)
    inv[...] = jnp.broadcast_to(inv_std, inv.shape)
    for part, side in zip(rows, sides):
        normed[:, side] = (part * inv_std * gain[:, side] + shift[:, side]).astype(BF)
    normed16 = normed[...]
    joint = dot(normed16, qkv[...], 1, 0) + bias_joint[...]
    tables = (cosine[...], sine_a[...], sine_b[...])
    queries[...] = turn(joint[:, :BLK], *tables).astype(BF)
    turned, value = turn(joint[:, BLK : 2 * BLK], *tables), joint[:, 2 * BLK :]
    keys[...] = turned.astype(BF)
    values[...] = value.astype(BF)
    sent[0] = pltpu.roll(turned, HD, 1).astype(BF)
    sent[1] = pltpu.roll(value, HD, 1).astype(BF)
    hidden = fc1_own.shape[1]
    for part, weight in enumerate((fc1_own, fc1_other)):
        columns = slice(part * hidden, (part + 1) * hidden)
        result = dot(normed16, weight[...], 1, 0) + bias1[:, columns]
        pre[:, columns] = result
        inner = jnp.tanh(inner_coef * (result + cubic_coef * result * result * result))
        active[:, columns] = (0.5 * result * (1.0 + inner)).astype(BF)


def front(place, pieces, gain, shift, qkv, bias_joint, cosine, sine_a, sine_b, fc1_own, fc1_other, bias1):
    tokens = LO * BLK
    hidden = fc1_own.shape[1]

    def shape(columns, dtype):
        return jax.ShapeDtypeStruct((tokens, columns), dtype)

    narrow = rows_spec(BLK)
    return pl.pallas_call(
        front_kernel,
        grid=(tokens // STEP,),
        out_shape=(
            shape(D, BF),
            shape(BLK, F32),
            shape(BLK, F32),
            shape(BLK, BF),
            shape(BLK, BF),
            shape(BLK, BF),
            jax.ShapeDtypeStruct((2, tokens, BLK), BF),
            shape(2 * hidden, F32),
            shape(2 * hidden, BF),
        ),
        in_specs=[
            scalar_spec(),
            *piece_specs(),
            fixed_spec(1, D),
            fixed_spec(1, D),
            fixed_spec(D, 3 * BLK),
            fixed_spec(1, 3 * BLK),
            narrow,
            narrow,
            narrow,
            fixed_spec(D, hidden),
            fixed_spec(D, hidden),
            fixed_spec(1, 2 * hidden),
        ],
        out_specs=(
            rows_spec(D),
            narrow,
            narrow,
            narrow,
            narrow,
            narrow,
            pl.BlockSpec((2, STEP, BLK), lambda i: (0, i, 0)),
            rows_spec(2 * hidden),
            rows_spec(2 * hidden),
        ),
        cost_estimate=cost(2 * tokens * D * (384 + 2 * hidden), 12 * tokens * D // 2),
        name="front",
    )(
        place,
        *pieces,
        gain,
        shift,
        qkv,
        bias_joint,
        cosine,
        sine_a,
        sine_b,
        fc1_own,
        fc1_other,
        bias1,
    )


def store_pieces(step, index, rows, a_own, a_other, b_near, b_far):
    for s in range(2):
        (a_own, a_other)[index][s] = rows[s * BLK : s * BLK + HALF]
    for wanted, target in ((step < 2, b_near), (step >= 2, b_far)):

        @pl.when(wanted)
        def _(target=target):
            for s in range(2):
                target[s, index] = rows[s * BLK + HALF : (s + 1) * BLK]


def partial_shapes():
    return (
        jax.ShapeDtypeStruct((LO, HALF, UNIT), BF),
        jax.ShapeDtypeStruct((LO, HALF, UNIT), BF),
        jax.ShapeDtypeStruct((LO // 2, 2, HALF, UNIT), BF),
        jax.ShapeDtypeStruct((LO // 2, 2, HALF, UNIT), BF),
    )


def partial_specs():
    near = pl.BlockSpec((2, HALF, UNIT), lambda i: (i, 0, 0))
    return (
        near,
        near,
        pl.BlockSpec((2, 2, HALF, UNIT), lambda i: (jnp.minimum(i, 1), 0, 0, 0)),
        pl.BlockSpec((2, 2, HALF, UNIT), lambda i: (jnp.maximum(i - 2, 0), 0, 0, 0)),
    )


def out_rows(c, down_own, down_other):
    hidden = down_own.shape[1] - HD
    return jnp.concatenate([down_own[c, hidden:], down_other[c, hidden:]], axis=0)


def mix_kernel(place, attended, active, down_own, down_other, *partial):
    hidden = down_own.shape[1] - HD
    for index, side in enumerate((place[0], 1 - place[0])):
        parts = []
        for quarter in range(4):
            c = 4 * side + quarter
            parts.append(
                (
                    dot(active[:, :hidden], down_own[c, :hidden], 1, 0)
                    + dot(active[:, hidden:], down_other[c, :hidden], 1, 0)
                    + dot(attended[...], out_rows(c, down_own, down_other), 1, 0)
                ).astype(BF)
            )
        store_pieces(pl.program_id(0), index, jnp.concatenate(parts, axis=1), *partial)


def mix(place, attended, active, down_own, down_other):
    tokens = LO * BLK
    hidden = down_own.shape[1] - HD
    return pl.pallas_call(
        mix_kernel,
        grid=(tokens // STEP,),
        out_shape=partial_shapes(),
        in_specs=[
            scalar_spec(),
            rows_spec(BLK),
            rows_spec(2 * hidden),
            fixed_spec(LO, hidden + HD, 256),
            fixed_spec(LO, hidden + HD, 256),
        ],
        out_specs=partial_specs(),
        cost_estimate=cost(2 * tokens * D * (128 + 2 * hidden), 8000000),
        name="mix",
    )(place, attended, active, down_own, down_other)


def back_kernel(place, *refs):
    back_body(place, refs[:PIECES], *refs[PIECES:])


def back_body(
    place,
    pieces,
    pre,
    down_own,
    down_other,
    cot,
    grad_pre,
    grad_attended,
    bias_sum,
):
    @pl.when(pl.program_id(0) == 0)
    def _():
        bias_sum[...] = jnp.zeros_like(bias_sum)

    parts = piece_rows(pl.program_id(0), pieces)
    for part, side in zip(parts, sides_of(place)):
        cot[:, side] = part
    rows = cot[...]
    hidden = down_own.shape[1] - HD

    def through(weight):
        total = 0.0
        for c in range(LO):
            total = total + dot(rows[:, c * 256 : (c + 1) * 256], weight(c), 1, 1)
        return total

    grad_attended[...] = through(lambda c: out_rows(c, down_own, down_other)).astype(BF)
    for part, weight in enumerate((down_own, down_other)):
        columns = slice(part * hidden, (part + 1) * hidden)
        value = pre[:, columns]
        inner = jnp.tanh(inner_coef * (value + cubic_coef * value * value * value))
        slope = 0.5 * (1.0 + inner) + 0.5 * value * (1.0 - inner * inner) * inner_coef * (
            1.0 + 3.0 * cubic_coef * value * value
        )
        grad = through(lambda c: weight[c, :hidden]) * slope
        bias_sum[:, columns] += jnp.sum(grad, axis=0, keepdims=True)
        grad_pre[:, columns] = grad.astype(BF)


def back(place, pieces, pre, down_own, down_other):
    tokens = LO * BLK
    hidden = down_own.shape[1] - HD
    return pl.pallas_call(
        back_kernel,
        grid=(tokens // STEP,),
        out_shape=(
            jax.ShapeDtypeStruct((tokens, D), BF),
            jax.ShapeDtypeStruct((tokens, 2 * hidden), BF),
            jax.ShapeDtypeStruct((tokens, BLK), BF),
            jax.ShapeDtypeStruct((1, 2 * hidden), F32),
        ),
        in_specs=[
            scalar_spec(),
            *piece_specs(),
            rows_spec(2 * hidden),
            fixed_spec(LO, hidden + HD, 256),
            fixed_spec(LO, hidden + HD, 256),
        ],
        out_specs=(
            rows_spec(D),
            rows_spec(2 * hidden),
            rows_spec(BLK),
            fixed_spec(1, 2 * hidden),
        ),
        cost_estimate=cost(2 * tokens * D * (128 + 2 * hidden), 14000000),
        name="back",
    )(place, *pieces, pre, down_own, down_other)


def unturn_kernel(dq, dk, dv, got, cosine, sine_a, sine_b, joint, own, other, bias):
    tables = (cosine[...], -sine_a[...], -sine_b[...])
    dk_all = dk[...] + got[0].astype(F32)
    dv_all = dv[...] + got[1].astype(F32)
    for j, grads in enumerate((turn(dq[...], *tables), turn(dk_all, *tables), dv_all)):
        columns = slice(j * BLK, (j + 1) * BLK)
        bias[:, columns] = jnp.sum(grads, axis=0, keepdims=True)
        grads = grads.astype(BF)
        joint[:, columns] = grads
        own[:, j * HD : (j + 1) * HD] = grads[:, :HD]
        other[:, j * HD : (j + 1) * HD] = grads[:, HD:]


def unturn(dq, dk, dv, got, cosine, sine_a, sine_b):
    tokens = dq.shape[0]
    return pl.pallas_call(
        unturn_kernel,
        out_shape=(
            jax.ShapeDtypeStruct((tokens, 3 * BLK), BF),
            jax.ShapeDtypeStruct((tokens, 3 * HD), BF),
            jax.ShapeDtypeStruct((tokens, 3 * HD), BF),
            jax.ShapeDtypeStruct((1, 3 * BLK), F32),
        ),
        in_specs=full_spec(7),
        out_specs=tuple(full_spec(4)),
        cost_estimate=cost(0, 6000000),
        name="unturn",
    )(dq, dk, dv, got, cosine, sine_a, sine_b)


def grad_kernel(place, *refs):
    grad_body(place, refs[:PIECES], *refs[PIECES:])


def grad_body(
    place,
    pieces,
    mean,
    inv,
    gain,
    joint,
    grad_pre,
    qkv,
    fc1_own,
    fc1_other,
    a_own,
    a_other,
    b_near,
    b_far,
    sums,
    gain_sum,
    shift_sum,
):
    step = pl.program_id(0)

    @pl.when(step == 0)
    def _():
        gain_sum[...] = jnp.zeros_like(gain_sum)
        shift_sum[...] = jnp.zeros_like(shift_sum)

    hidden = fc1_own.shape[1]
    parts = piece_rows(step, pieces)
    first, second = 0.0, 0.0
    for index, (side, part) in enumerate(zip(sides_of(place), parts)):
        grads = (
            dot(joint[...], qkv[side, :], 1, 1)
            + dot(grad_pre[:, :hidden], fc1_own[side, :], 1, 1)
            + dot(grad_pre[:, hidden:], fc1_other[side, :], 1, 1)
        )
        store_pieces(step, index, grads.astype(BF), a_own, a_other, b_near, b_far)
        both = grads * ((part.astype(F32) - mean[:, :1]) * inv[:, :1])
        shift_sum[index : index + 1, :] += jnp.sum(grads, axis=0, keepdims=True)
        gain_sum[index : index + 1, :] += jnp.sum(both, axis=0, keepdims=True)
        first = first + jnp.sum(grads * gain[:, side], axis=-1, keepdims=True)
        second = second + jnp.sum(both * gain[:, side], axis=-1, keepdims=True)
    lane = lax.broadcasted_iota(jnp.int32, (STEP, BLK), 1)
    turned = jnp.transpose(jnp.where(lane < HD, first, second))
    sums[0:1, :] = turned[0:1]
    sums[1:2, :] = turned[HD : HD + 1]


def grad_units(place, pieces, mean, inv, gain, joint, grad_pre, qkv, fc1_own, fc1_other):
    tokens = LO * BLK
    hidden = fc1_own.shape[1]
    return pl.pallas_call(
        grad_kernel,
        grid=(tokens // STEP,),
        out_shape=(
            *partial_shapes(),
            jax.ShapeDtypeStruct((2, tokens), F32),
            jax.ShapeDtypeStruct((2, UNIT), F32),
            jax.ShapeDtypeStruct((2, UNIT), F32),
        ),
        in_specs=[
            scalar_spec(),
            *piece_specs(),
            rows_spec(BLK),
            rows_spec(BLK),
            fixed_spec(1, D),
            rows_spec(3 * BLK),
            rows_spec(2 * hidden),
            fixed_spec(D, 3 * BLK),
            fixed_spec(D, hidden),
            fixed_spec(D, hidden),
        ],
        out_specs=(
            *partial_specs(),
            pl.BlockSpec((2, STEP), lambda i: (0, i)),
            fixed_spec(2, UNIT),
            fixed_spec(2, UNIT),
        ),
        cost_estimate=cost(2 * tokens * D * (384 + 2 * hidden), 16000000),
        name="grad",
    )(place, *pieces, mean, inv, gain, joint, grad_pre, qkv, fc1_own, fc1_other)


def step_body(
    n_hi,
    layer_input,
    norm_gain,
    norm_shift,
    w_qkv,
    b_qkv,
    w_out,
    b_out,
    w_fc1,
    b_fc1,
    w_fc2,
    b_fc2,
    grad_output,
    placement,
    position_ids,
):
    hi, y, k = (lax.axis_index(name) for name in ("hi", "y", "k"))
    lo = lax.axis_index(LOX)
    depth = D // (n_hi * LO)
    width = w_qkv.shape[2]
    hidden = w_fc1.shape[1] // LO
    tokens = LO * BLK

    def half(values, which):
        split = values.reshape((2, 2, HALF) + values.shape[1:])
        cut = lax.dynamic_index_in_dim(split, which, 1, keepdims=False)
        return cut.reshape((BLK,) + values.shape[1:])

    def in_order(index, own, got, axis):
        return jnp.where(
            index == 0,
            jnp.concatenate([own, got], axis=axis),
            jnp.concatenate([got, own], axis=axis),
        )

    def make_unit(values):
        got = swap(half(values, 1 - k), "k")
        return in_order(k, half(values, k), got, 1)

    unit_in = make_unit(layer_input)
    pieces = gather_pieces(unit_in)
    unit_cot = make_unit(grad_output)
    pieces_cot = gather_pieces(unit_cot)
    slot_lo = [lo ^ (((s & 1) << 2) | (s & 2) | (s >> 2)) for s in range(LO)]
    place = jnp.stack([y, k] + slot_lo).astype(jnp.int32)

    def over_hi(values):
        return values[None] if n_hi == 1 else lax.all_gather(values, "hi", axis=0)

    def ordered(got, shape):
        return got if n_hi == 1 else jnp.moveaxis(got, 1, 0).reshape(shape)

    fc1_own = spread(over_hi(w_fc1).reshape(n_hi, depth, LO, hidden).transpose(2, 0, 1, 3))
    fc1_own = ordered(fc1_own, (D, hidden)).reshape(D, hidden)
    fc1_other = swap(fc1_own, "k")
    down = jnp.concatenate(
        [w_fc2.reshape(LO, hidden, depth), w_out.reshape(LO, HD, depth)], axis=1
    )
    down = spread(jnp.moveaxis(over_hi(down), 0, 1))
    if n_hi == 1:
        down_own = down.reshape(LO, hidden + HD, 256)
    else:
        down_own = down.transpose(2, 1, 0, 3).reshape(hidden + HD, LO, 256).transpose(1, 0, 2)
    down_other = swap(down_own, "k")
    if n_hi == 1:
        ids = half(position_ids, k)
        ids = jnp.stack([ids // BLK, ids % BLK]).astype(BF)
        ids = jnp.concatenate([ids, jnp.zeros((IDS - 2, BLK), BF)])
        heads_own = spread(pack_heads(w_qkv.transpose(1, 0, 2), ids))
        qkv = join_heads(heads_own, swap(heads_own, "k"))
        ids = heads_own[:, 3 * BLK : 3 * BLK + 2].astype(jnp.int32)
        ids = ids[:, 0] * BLK + ids[:, 1]
        ids = jnp.stack([lax.dynamic_index_in_dim(ids, c, 0, keepdims=False) for c in slot_lo])
    else:
        ids = half(position_ids, k)
        for name in ("zh", "zl", "x"):
            ids = jnp.stack([ids, swap(ids, name)])
        cut = over_hi(w_qkv).reshape(n_hi, depth, 3, LO, HD).transpose(3, 0, 1, 2, 4)
        heads_own = spread(cut.reshape(LO, n_hi, depth, 3 * HD))
        heads_own = ordered(heads_own, (D, 3, HD))
        qkv = jnp.concatenate([heads_own, swap(heads_own, "k")], axis=2).reshape(D, 6 * HD)

    own_head = lax.dynamic_slice_in_dim(b_qkv, lo * HD, HD, 1)
    own_bias1 = lax.dynamic_slice_in_dim(b_fc1, lo * hidden, hidden, 0)
    affine = jnp.stack([norm_gain.astype(F32), norm_shift.astype(F32)])
    small = jnp.concatenate([affine.reshape(-1), own_head.reshape(-1), own_bias1])
    small_other = swap(small, "k")
    affine = in_order(k, affine, small_other[: 2 * width].reshape(2, width), 1)
    affine = in_order(y, affine, swap(affine, "y"), 1)
    gain, shift = affine[0:1], affine[1:2]
    head_other = small_other[2 * width : 2 * width + 3 * HD].reshape(3, HD)
    bias_joint = jnp.concatenate([own_head, head_other], axis=1).reshape(1, 6 * HD)
    bias1 = jnp.concatenate([own_bias1, small_other[2 * width + 3 * HD :]])[None]

    ids = ids.reshape(tokens)
    lane = jnp.arange(BLK, dtype=jnp.int32) % HD
    frequency = 10000.0 ** (-2.0 * (lane % (ROT // 2)).astype(F32) / ROT)
    angles = ids.astype(F32)[:, None] * frequency[None, :]
    cosine = jnp.where(lane < ROT, jnp.cos(angles), 1.0)
    sine = jnp.sin(angles)
    sine_a = jnp.where(lane < ROT // 2, -sine, 0.0)
    sine_b = jnp.where((lane >= ROT // 2) & (lane < ROT), sine, 0.0)

    blocks = n_hi * 2 * LO
    by_group = placement.reshape(n_hi, LO, 2)
    in_slots = jnp.stack(
        [lax.dynamic_index_in_dim(by_group, c, 1, keepdims=False) for c in slot_lo], axis=1
    ).reshape(n_hi, 2 * LO)
    local = lax.dynamic_index_in_dim(in_slots, hi, 0, keepdims=False)
    ranks = jnp.sum((local[None, :] < local[:, None]).astype(jnp.int32), axis=1)
    sorted_local = jnp.sort(local) if n_hi > 1 else jnp.arange(2 * LO, dtype=jnp.int32)
    table = jnp.concatenate(
        [k[None].astype(jnp.int32), in_slots.reshape(-1), ranks, sorted_local]
    )
    if n_hi == 1:
        tiles = tuple(4 * BLK * (m // 2 + 1) for m in range(LO))
    else:
        tiles = (blocks * BLK,) * LO

    normed16, mean, inv, queries, keys, values, sent, pre, active = front(
        place,
        pieces,
        gain,
        shift,
        qkv,
        bias_joint,
        cosine,
        sine_a,
        sine_b,
        fc1_own,
        fc1_other,
        bias1,
    )
    other_kv = swap(sent, "k")

    def all_keys(rows):
        return rows if n_hi == 1 else lax.all_gather(rows, "hi", axis=0, tiled=True)

    key_set = tuple(all_keys(v) for v in (keys, values, other_kv[0], other_kv[1]))
    attended, log_total = attend(tiles, blocks, table, queries, *key_set)
    summed = scatter_pieces(*mix(place, attended, active, down_own, down_other))

    cot, grad_pre, grad_attended, term_bias1 = back(
        place, pieces_cot, pre, down_own, down_other
    )

    def summed_dot(left, own, other, flip):
        def product(right):
            return dot(right, left, 0, 0) if flip else dot(left, right, 0, 0)

        return product(own), swap(product(other).astype(BF), "k")

    def home(total):
        got = spread(total)
        if n_hi == 1:
            return got[:, 0]
        return lax.psum_scatter(got.astype(F32), "hi", scatter_dimension=1)

    def add(own, got):
        return (own + got.astype(F32)).astype(BF)

    def cut_columns(values):
        rows = values.shape[0]
        return values.reshape(rows, n_hi, LO, depth).transpose(2, 1, 0, 3)

    fc2_sum = add(*summed_dot(cot, active[:, :hidden], active[:, hidden:], True))
    out_sum = add(*summed_dot(cot, attended[:, :HD], attended[:, HD:], True))
    down = jnp.concatenate([cut_columns(fc2_sum), cut_columns(out_sum)], axis=2)
    if n_hi == 1:
        grad_attended, down = lax.optimization_barrier((grad_attended, down))
    down_home = home(down)
    grad_fc2 = down_home[:, :hidden].reshape(LO * hidden, depth).astype(F32)
    grad_out = down_home[:, hidden:].reshape(LO * HD, depth).astype(F32)

    dq, dk, dv, grads_sent = attend_back(
        tiles, blocks, table, queries, *key_set, grad_attended, attended, log_total
    )

    def own_keys(rows):
        if n_hi == 1:
            return rows
        return lax.psum_scatter(rows, "hi", scatter_dimension=0, tiled=True)

    got = swap(grads_sent, "k")
    if n_hi > 1:
        dk = own_keys(dk + got[0].astype(F32))
        dv = own_keys(dv + got[1].astype(F32))
        got = jnp.zeros((2,) + dk.shape, BF)
    joint, joint_own, joint_other, term_joint_bias = unturn(
        dq, dk, dv, got, cosine, sine_a, sine_b
    )
    *partial, row_sums, gain_sum, shift_sum = grad_units(
        place, pieces, mean, inv, gain, joint, grad_pre, qkv, fc1_own, fc1_other
    )
    if n_hi == 1:
        late, *partial = lax.optimization_barrier((normed16, *partial))
    else:
        late = normed16
    fc1_term, fc1_got = summed_dot(late, grad_pre[:, :hidden], grad_pre[:, hidden:], False)
    own_term, got_term = summed_dot(late, joint_own, joint_other, False)
    if n_hi == 1:
        packed = pack_grads(fc1_term, fc1_got, own_term, got_term)
        grad_fc1, grad_qkv = home_grads(spread(packed))
        grad_qkv = grad_qkv.transpose(1, 0, 2)
    else:
        fc1_sum = add(fc1_term, fc1_got).reshape(n_hi, LO, depth, hidden)
        fc1_home = home(fc1_sum.transpose(1, 0, 2, 3))
        grad_fc1 = fc1_home.transpose(1, 0, 2).reshape(depth, LO * hidden).astype(F32)
        qkv_sum = add(own_term, got_term).reshape(n_hi, LO, depth, 3 * HD)
        qkv_home = home(qkv_sum.transpose(1, 0, 2, 3)).reshape(LO, depth, 3, HD)
        grad_qkv = qkv_home.transpose(1, 2, 0, 3).reshape(depth, 3, width).astype(F32)
    grad_unit = scatter_pieces(*partial)

    heads = lax.dynamic_update_slice(
        jnp.zeros((2, 3, width), F32),
        term_joint_bias.reshape(3, 2, HD).transpose(1, 0, 2),
        (0, 0, lo * HD),
    )
    bias_sum = lax.dynamic_update_slice(
        jnp.zeros((2, LO * hidden), F32), term_bias1.reshape(2, hidden), (0, lo * hidden)
    )
    affine_sum = jnp.stack([gain_sum, shift_sum]).reshape(2, 2, 2, width).transpose(1, 2, 0, 3)

    def pick(values, index):
        return lax.dynamic_index_in_dim(values, index, 0, keepdims=False)

    row_pair = row_sums.reshape(-1)
    over_y = jnp.concatenate([affine_sum[1].reshape(-1), row_pair])
    over_y = swap(over_y, "y")
    affine_sum = affine_sum[0] + over_y[: 4 * width].reshape(2, 2, width)
    row_pair = (row_pair + over_y[4 * width :]).reshape(2, tokens)
    over_k = jnp.concatenate(
        [heads[1].reshape(-1), bias_sum[1], pick(affine_sum, 1 - k).reshape(-1)]
    )
    over_k = swap(over_k, "k") + jnp.concatenate(
        [heads[0].reshape(-1), bias_sum[0], pick(affine_sum, k).reshape(-1)]
    )
    local_bias = jnp.sum(grad_output.astype(F32), axis=0)
    flat = jnp.concatenate([over_k, local_bias])
    length = flat.shape[0]
    for name in ("x", "zl", "zh"):
        left = row_pair.shape[1] // 2
        got = swap(jnp.concatenate([flat, row_pair[:, left:].reshape(-1)]), name)
        flat = flat + got[:length]
        row_pair = row_pair[:, :left] + got[length:].reshape(2, left)
    row_own = row_pair.T / D
    if n_hi > 1:
        flat = lax.psum(flat, "hi")
    cuts = [3 * width, LO * hidden, width, width, width]
    ends = [sum(cuts[: i + 1]) for i in range(len(cuts))]
    grad_b_qkv = flat[: ends[0]].reshape(3, width)
    grad_b_fc1 = flat[ends[0] : ends[1]]
    grad_gain = flat[ends[1] : ends[2]]
    grad_shift = flat[ends[2] : ends[3]]
    grad_b_out = flat[ends[3] :]

    def to_rows(unit):
        parts = unit.reshape(BLK, 2, width)
        own = lax.dynamic_index_in_dim(parts, k, 1, keepdims=False)
        got = swap(lax.dynamic_index_in_dim(parts, 1 - k, 1, keepdims=False), "k")
        own, got = own.reshape(2, 1, HALF, width), got.reshape(2, 1, HALF, width)
        return in_order(k, own, got, 1).reshape(2 * BLK, width)

    layer_output = layer_input.astype(F32) + to_rows(summed) + b_out + b_fc2

    mean_own, inv_own = mean[:BLK, :1], inv[:BLK, :1]
    gain_own = lax.dynamic_slice_in_dim(gain, y * UNIT, UNIT, 1)
    normed_unit = (unit_in.astype(F32) - mean_own) * inv_own
    grad_x = inv_own * (
        grad_unit * gain_own - row_own[:, :1] - normed_unit * row_own[:, 1:]
    )
    grad_input = to_rows(grad_x + unit_cot.astype(F32))
    return (
        layer_output,
        grad_input,
        grad_gain,
        grad_shift,
        grad_qkv,
        grad_b_qkv,
        grad_out,
        grad_b_out,
        grad_fc1,
        grad_b_fc1,
        grad_fc2,
        grad_b_out,
    )


def on_device(n_hi, *arguments):
    return step_body(n_hi, *arguments)


def solution(mesh):
    n_hi = mesh.shape["ctx"] // LO
    inner = Mesh(mesh.devices.reshape(n_hi, 2, 2, 2, 2, 2), CTX + TP)
    in_specs = (
        P(CTX, TP),
        P(TP),
        P(TP),
        P(CTX, None, TP),
        P(None, TP),
        P(TP, CTX),
        P(TP),
        P(CTX, TP),
        P(TP),
        P(TP, CTX),
        P(TP),
        P(CTX, TP),
        P(),
        P(CTX),
    )
    out_specs = (
        P(CTX, TP),
        P(CTX, TP),
        P(TP),
        P(TP),
        P(CTX, None, TP),
        P(None, TP),
        P(TP, CTX),
        P(TP),
        P(CTX, TP),
        P(TP),
        P(TP, CTX),
        P(TP),
    )
    return jax.shard_map(
        functools.partial(on_device, n_hi),
        mesh=inner,
        in_specs=in_specs,
        out_specs=out_specs,
        check_vma=False,
    )
```

```python
import functools
import math

import jax
import jax.numpy as jnp
from jax import lax
from jax.experimental import pallas as pl
from jax.experimental.pallas import tpu as pltpu
from jax.sharding import Mesh, PartitionSpec as P


D = 2048
HD = 64
ROT = 32
BLK = 128
HALF = BLK // 2
LO = 8
UNIT = 1024
STEP = 256
IDS = 16

epsilon = 1e-05
cubic_coef = 0.044715
inner_coef = math.sqrt(2.0 / math.pi)
neg_large = -1e30
BF = jnp.bfloat16
F32 = jnp.float32
LOX = ("zh", "zl", "x")
CTX = ("hi",) + LOX
TP = ("y", "k")


def swap(values, axis):
    return lax.ppermute(values, axis, [(0, 1), (1, 0)])


def spread(pieces):
    return lax.all_to_all(pieces, LOX, 0, 0, tiled=True)


def gather_pieces(unit):
    unit = unit.reshape(2, HALF, UNIT)
    pair = jnp.stack([unit, swap(unit, "zh")])
    quad = jnp.concatenate([pair, swap(pair, "zl")])
    first, second = quad[:, 0], quad[:, 1]
    first_x = swap(first, "x")
    second_y = swap(second, "y")
    first_y = swap(first, "y")
    second_x = swap(second, "x")
    first_xy = swap(first_x, "y")
    second_yx = swap(second_y, "x")
    return first, first_x, first_y, first_xy, second, second_x, second_y, second_yx


def scatter_pieces(a_own, a_other, b_near, b_far):
    def add(left, right):
        return left.astype(F32) + right.astype(F32)

    a_own = add(a_own, swap(a_other, "y")).astype(BF)
    b_near = add(b_near, swap(b_far, "x")).astype(BF)
    a_own = add(a_own[:4], swap(a_own[4:], "x")).astype(BF)
    b_near = add(b_near[:, 0], swap(b_near[:, 1], "y")).astype(BF)
    both = jnp.stack([a_own, b_near], axis=1)
    both = add(both[:2], swap(both[2:], "zl")).astype(BF)
    return add(both[0], swap(both[1], "zh")).reshape(BLK, UNIT)


def full_spec(count):
    return [pl.BlockSpec(memory_space=pltpu.VMEM) for _ in range(count)]


def dot(left, right, left_dim, right_dim):
    return lax.dot_general(
        left, right, (((left_dim,), (right_dim,)), ((), ())), preferred_element_type=F32
    )


def cost(flops, size):
    return pl.CostEstimate(flops=flops, bytes_accessed=size, transcendentals=0)


def rows_spec(columns, step=STEP):
    return pl.BlockSpec((step, columns), lambda i: (i, 0))


def fixed_spec(*shape):
    return pl.BlockSpec(shape, lambda i: (0,) * len(shape))


def scalar_spec():
    return pl.BlockSpec(memory_space=pltpu.SMEM)


PIECES = 8


def piece_specs():
    return [pl.BlockSpec((2, HALF, UNIT), lambda i: (i % 2, 0, 0)) for _ in range(PIECES)]


def piece_rows(step, pieces):
    near = step < 2
    chosen = [jnp.where(near, pieces[i][...], pieces[i + 1][...]) for i in (0, 2, 4, 6)]
    return [
        jnp.concatenate([first[0], second[0], first[1], second[1]], axis=0)
        for first, second in ((chosen[0], chosen[2]), (chosen[1], chosen[3]))
    ]


def sides_of(place):
    y = place[0]
    return [
        pl.ds(pl.multiple_of(y * UNIT, UNIT), UNIT),
        pl.ds(pl.multiple_of((1 - y) * UNIT, UNIT), UNIT),
    ]


def pack_kernel(fc1, weight, ids, out):
    for c in range(LO):
        columns = slice(c * HD, (c + 1) * HD)
        out[c, : 2 * BLK] = fc1[:, c * 256 : (c + 1) * 256]
        tiles = [
            jnp.concatenate([weight[j, :BLK, columns], weight[j, BLK:, columns]], axis=1)
            for j in range(3)
        ]
        out[c, 2 * BLK : 3 * BLK] = jnp.concatenate(tiles[:2], axis=1)
        out[c, 3 * BLK : 3 * BLK + HALF] = jnp.concatenate(
            [tiles[2][:HALF], tiles[2][HALF:]], axis=1
        )
        out[c, 3 * BLK + HALF :] = ids[...]


def pack_first(fc1, weight, ids):
    return pl.pallas_call(
        pack_kernel,
        out_shape=jax.ShapeDtypeStruct((LO, 3 * BLK + HALF + IDS, 256), BF),
        in_specs=full_spec(3),
        out_specs=full_spec(1)[0],
        cost_estimate=cost(0, 3800000),
        name="pack",
    )(fc1, weight, ids)


def head_tile(half, c, j):
    if j < 2:
        return half[c, 2 * BLK : 3 * BLK, j * BLK : (j + 1) * BLK]
    rows = slice(3 * BLK, 3 * BLK + HALF)
    return jnp.concatenate([half[c, rows, :BLK], half[c, rows, BLK:]], axis=0)


def join_kernel(own, other, fc1_own, fc1_other, qkv):
    for c in range(LO):
        rows = pl.ds(c * 2 * BLK, 2 * BLK)
        fc1_own[rows, :] = own[c, : 2 * BLK]
        fc1_other[rows, :] = other[c, : 2 * BLK]
        for j in range(3):
            tiles = [head_tile(half, c, j) for half in (own, other)]
            for u in range(2):
                columns = slice(u * HD, (u + 1) * HD)
                rows = pl.ds(c * 2 * BLK + u * BLK, BLK)
                qkv[rows, j * BLK : (j + 1) * BLK] = jnp.concatenate(
                    [tile[:, columns] for tile in tiles], axis=1
                )


def join_first(own, other):
    return pl.pallas_call(
        join_kernel,
        out_shape=(
            jax.ShapeDtypeStruct((D, 256), BF),
            jax.ShapeDtypeStruct((D, 256), BF),
            jax.ShapeDtypeStruct((D, 3 * BLK), BF),
        ),
        in_specs=full_spec(2),
        out_specs=tuple(full_spec(3)),
        cost_estimate=cost(0, 7400000),
        name="join",
    )(own, other)


def pack_grad_kernel(fc1_own, fc1_other, own, other, out):
    for c in range(LO):
        rows = pl.ds(c * 2 * BLK, 2 * BLK)
        out[c, : 2 * BLK] = (fc1_own[rows, :] + fc1_other[rows, :].astype(F32)).astype(BF)
        tiles = []
        for j in range(3):
            columns = slice(j * HD, (j + 1) * HD)
            parts = []
            for u in range(2):
                rows = pl.ds(c * 2 * BLK + u * BLK, BLK)
                parts.append(own[rows, columns] + other[rows, columns].astype(F32))
            tiles.append(jnp.concatenate(parts, axis=1).astype(BF))
        out[c, 2 * BLK : 3 * BLK] = jnp.concatenate(tiles[:2], axis=1)
        out[c, 3 * BLK :] = jnp.concatenate([tiles[2][:HALF], tiles[2][HALF:]], axis=1)


def pack_grads(fc1_own, fc1_other, own, other):
    return pl.pallas_call(
        pack_grad_kernel,
        out_shape=jax.ShapeDtypeStruct((LO, 3 * BLK + HALF, 2 * BLK), BF),
        in_specs=full_spec(4),
        out_specs=full_spec(1)[0],
        cost_estimate=cost(0, 9000000),
        name="pack_grad",
    )(fc1_own, fc1_other, own, other)


def home_kernel(pieces, fc1, qkv):
    for c in range(LO):
        fc1[:, c * 256 : (c + 1) * 256] = pieces[c, : 2 * BLK].astype(F32)
    for c in range(0, LO, 2):
        for j in range(3):
            tiles = []
            for d in range(2):
                if j < 2:
                    tiles.append(pieces[c + d, 2 * BLK : 3 * BLK, j * BLK : (j + 1) * BLK])
                else:
                    tiles.append(
                        jnp.concatenate(
                            [pieces[c + d, 3 * BLK :, :BLK], pieces[c + d, 3 * BLK :, BLK:]],
                            axis=0,
                        )
                    )
            for u in range(2):
                columns = slice(u * HD, (u + 1) * HD)
                qkv[j, u * BLK : (u + 1) * BLK, c * HD : (c + 2) * HD] = jnp.concatenate(
                    [tile[:, columns] for tile in tiles], axis=1
                ).astype(F32)


def home_grads(pieces):
    return pl.pallas_call(
        home_kernel,
        out_shape=(
            jax.ShapeDtypeStruct((2 * BLK, LO * 256), F32),
            jax.ShapeDtypeStruct((3, 2 * BLK, LO * HD), F32),
        ),
        in_specs=full_spec(1),
        out_specs=tuple(full_spec(2)),
        cost_estimate=cost(0, 6000000),
        name="home",
    )(pieces)


def turn(values, cosine, sine_a, sine_b):
    return (
        values * cosine
        + pltpu.roll(values, 128 - ROT // 2, 1) * sine_a
        + pltpu.roll(values, ROT // 2, 1) * sine_b
    )


def sort_in(table, own, other, target, blocks):
    core = table[0]
    for i in range(blocks):
        place = table[1 + i]
        rows = pl.ds(i * HALF, HALF)
        target[pl.ds(pl.multiple_of(place * BLK + core * HALF, HALF), HALF), :] = own[rows, :]
        target[pl.ds(pl.multiple_of(place * BLK + (1 - core) * HALF, HALF), HALF), :] = other[
            rows, :
        ]


def two_heads(tile):
    lane = lax.broadcasted_iota(jnp.int32, tile.shape, 1)
    zero = jnp.zeros_like(tile)
    return jnp.concatenate(
        [jnp.where(lane < HD, tile, zero), jnp.where(lane < HD, zero, tile)], axis=0
    )


def one_tile(pair):
    rows = pair.shape[0] // 2
    lane = lax.broadcasted_iota(jnp.int32, (rows, pair.shape[1]), 1)
    return jnp.where(lane < HD, pair[:rows], pair[rows:])


def attend_kernel(
    tiles, blocks, table, q, k_own, v_own, k_other, v_other, out, log_out, qs, ks, vs, os, ls
):
    core = table[0]
    sort_in(table, k_own, k_other, ks, blocks)
    sort_in(table, v_own, v_other, vs, blocks)
    for i in range(2 * LO):
        place = table[1 + blocks + i]
        qs[pl.ds(pl.multiple_of(place * HALF, HALF), HALF), :] = q[pl.ds(i * HALF, HALF), :]
    scale = 1.0 / math.sqrt(HD)
    full = len(tiles) > 0 and tiles[0] == tiles[-1] and len(tiles) > 1
    row = lax.broadcasted_iota(jnp.int32, (2 * BLK, 4 * BLK), 0) % BLK
    col = lax.broadcasted_iota(jnp.int32, (2 * BLK, 4 * BLK), 1)
    edge = col - (row // HALF) * BLK - core * HALF - row % HALF

    def tile(m, extent):
        pair = two_heads(qs[pl.ds(pl.multiple_of(m * BLK, BLK), BLK), :])
        scores = dot(pair, ks[pl.ds(0, extent), :], 1, 1) * scale
        if full:
            wide_col = lax.broadcasted_iota(jnp.int32, scores.shape, 1)
            wide_row = lax.broadcasted_iota(jnp.int32, scores.shape, 0) % BLK
            begin = jnp.where(
                wide_row < HALF,
                table[1 + blocks + 2 * LO + 2 * m],
                table[2 + blocks + 2 * LO + 2 * m],
            )
            allowed = wide_col <= begin * BLK + core * HALF + wide_row % HALF
            scores = jnp.where(allowed, scores, neg_large)
        else:
            last = scores[:, extent - 4 * BLK :]
            last = jnp.where(edge <= (m % 2) * (2 * BLK), last, neg_large)
            if extent > 4 * BLK:
                scores = jnp.concatenate([scores[:, : extent - 4 * BLK], last], axis=1)
            else:
                scores = last
        top = jnp.max(scores, axis=-1, keepdims=True)
        weights = jnp.exp(scores - top)
        total = jnp.sum(weights, axis=-1, keepdims=True)
        probs = (weights * (1.0 / total)).astype(BF)
        mixed = dot(probs, vs[pl.ds(0, extent), :], 1, 0)
        os[pl.ds(pl.multiple_of(m * BLK, BLK), BLK), :] = one_tile(mixed)
        ls[pl.ds(pl.multiple_of(m * BLK, BLK), BLK), :] = one_tile(
            jnp.broadcast_to(top + jnp.log(total), (2 * BLK, 128))
        )

    if full:
        lax.fori_loop(0, len(tiles), lambda m, carry: (tile(m, tiles[0]), carry)[1], 0)
    else:
        for m in range(0, len(tiles), 2):
            lax.fori_loop(m, m + 2, lambda i, carry: (tile(i, tiles[m]), carry)[1], 0)
    for i in range(2 * LO):
        place = table[1 + blocks + i]
        rows = pl.ds(pl.multiple_of(place * HALF, HALF), HALF)
        out[pl.ds(i * HALF, HALF), :] = os[rows, :].astype(BF)
        log_out[pl.ds(i * HALF, HALF), :] = ls[rows, :]


def attend(tiles, blocks, table, q, k_own, v_own, k_other, v_other):
    tokens = q.shape[0]
    keys = blocks * BLK
    return pl.pallas_call(
        functools.partial(attend_kernel, tiles, blocks),
        out_shape=(
            jax.ShapeDtypeStruct((tokens, 128), BF),
            jax.ShapeDtypeStruct((tokens, 128), F32),
        ),
        in_specs=[pl.BlockSpec(memory_space=pltpu.SMEM)] + full_spec(5),
        out_specs=tuple(full_spec(2)),
        scratch_shapes=[
            pltpu.VMEM((tokens, 128), BF),
            pltpu.VMEM((keys, 128), BF),
            pltpu.VMEM((keys, 128), BF),
            pltpu.VMEM((tokens, 128), F32),
            pltpu.VMEM((tokens, 128), F32),
        ],
        cost_estimate=pl.CostEstimate(
            flops=8 * 256 * 128 * sum(tiles),
            bytes_accessed=2000000,
            transcendentals=256 * sum(tiles),
        ),
        name="attend",
    )(table, q, k_own, v_own, k_other, v_other)


def attend_back_kernel(
    tiles,
    blocks,
    table,
    q,
    k_own,
    v_own,
    k_other,
    v_other,
    cot,
    att,
    log_in,
    dq,
    dk_own,
    dv_own,
    sent,
    qs,
    ks,
    vs,
    cs,
    ps,
    ls,
    dqs,
    dks,
    dvs,
):
    core = table[0]
    sort_in(table, k_own, k_other, ks, blocks)
    sort_in(table, v_own, v_other, vs, blocks)
    for i in range(2 * LO):
        place = table[1 + blocks + i]
        rows = pl.ds(i * HALF, HALF)
        target = pl.ds(pl.multiple_of(place * HALF, HALF), HALF)
        qs[target, :] = q[rows, :]
        cs[target, :] = cot[rows, :]
        ps[target, :] = cot[rows, :].astype(F32) * att[rows, :].astype(F32)
        ls[target, :] = log_in[rows, :]
    dks[...] = jnp.zeros_like(dks)
    dvs[...] = jnp.zeros_like(dvs)
    scale = 1.0 / math.sqrt(HD)
    full = len(tiles) > 0 and tiles[0] == tiles[-1] and len(tiles) > 1
    col = lax.broadcasted_iota(jnp.int32, (4 * BLK, 2 * BLK), 1) % BLK
    row = lax.broadcasted_iota(jnp.int32, (4 * BLK, 2 * BLK), 0)
    edge = row - (col // HALF) * BLK - core * HALF - col % HALF

    def tile(m, extent):
        rows = pl.ds(pl.multiple_of(m * BLK, BLK), BLK)
        span = pl.ds(0, extent)
        pair = two_heads(qs[rows, :])
        cot_pair = two_heads(cs[rows, :])
        logs = jnp.transpose(ls[rows, :])
        log_row = jnp.concatenate([logs[0:1], logs[HD : HD + 1]], axis=1)
        products = jnp.transpose(ps[rows, :])
        delta = jnp.concatenate(
            [
                jnp.sum(products[:HD], axis=0, keepdims=True),
                jnp.sum(products[HD:], axis=0, keepdims=True),
            ],
            axis=1,
        )
        scores = dot(ks[span, :], pair, 1, 1) * scale
        probs = jnp.exp(scores - log_row)
        if full:
            wide_row = lax.broadcasted_iota(jnp.int32, scores.shape, 0)
            wide_col = lax.broadcasted_iota(jnp.int32, scores.shape, 1) % BLK
            begin = jnp.where(
                wide_col < HALF,
                table[1 + blocks + 2 * LO + 2 * m],
                table[2 + blocks + 2 * LO + 2 * m],
            )
            allowed = wide_row <= begin * BLK + core * HALF + wide_col % HALF
            probs = jnp.where(allowed, probs, 0.0)
        else:
            last = jnp.where(edge <= (m % 2) * (2 * BLK), probs[extent - 4 * BLK :], 0.0)
            if extent > 4 * BLK:
                probs = jnp.concatenate([probs[: extent - 4 * BLK], last], axis=0)
            else:
                probs = last
        grad_probs = dot(vs[span, :], cot_pair, 1, 1)
        grad_scores = (probs * (grad_probs - delta)).astype(BF)
        dvs[span, :] += dot(probs.astype(BF), cot_pair, 1, 0)
        dks[span, :] += dot(grad_scores, pair, 1, 0)
        dqs[rows, :] = one_tile(dot(grad_scores, ks[span, :], 0, 0)) * scale

    if full:
        lax.fori_loop(0, len(tiles), lambda m, carry: (tile(m, tiles[0]), carry)[1], 0)
    else:
        for m in range(0, len(tiles), 2):
            lax.fori_loop(m, m + 2, lambda i, carry: (tile(i, tiles[m]), carry)[1], 0)
    for i in range(2 * LO):
        place = table[1 + blocks + i]
        dq[pl.ds(i * HALF, HALF), :] = dqs[
            pl.ds(pl.multiple_of(place * HALF, HALF), HALF), :
        ]
    for i in range(blocks):
        place = table[1 + i]
        rows = pl.ds(i * HALF, HALF)
        own = pl.ds(pl.multiple_of(place * BLK + core * HALF, HALF), HALF)
        other = pl.ds(pl.multiple_of(place * BLK + (1 - core) * HALF, HALF), HALF)
        dk_own[rows, :] = dks[own, :] * scale
        dv_own[rows, :] = dvs[own, :]
        sent[0, rows, :] = pltpu.roll(dks[other, :] * scale, HD, 1).astype(BF)
        sent[1, rows, :] = pltpu.roll(dvs[other, :], HD, 1).astype(BF)


def attend_back(tiles, blocks, table, q, k_own, v_own, k_other, v_other, cot, att, log_in):
    tokens = q.shape[0]
    keys = blocks * BLK
    return pl.pallas_call(
        functools.partial(attend_back_kernel, tiles, blocks),
        out_shape=(
            jax.ShapeDtypeStruct((tokens, 128), F32),
            jax.ShapeDtypeStruct((keys // 2, 128), F32),
            jax.ShapeDtypeStruct((keys // 2, 128), F32),
            jax.ShapeDtypeStruct((2, keys // 2, 128), BF),
        ),
        in_specs=[pl.BlockSpec(memory_space=pltpu.SMEM)] + full_spec(8),
        out_specs=tuple(full_spec(4)),
        scratch_shapes=[
            pltpu.VMEM((tokens, 128), BF),
            pltpu.VMEM((keys, 128), BF),
            pltpu.VMEM((keys, 128), BF),
            pltpu.VMEM((tokens, 128), BF),
            pltpu.VMEM((tokens, 128), F32),
            pltpu.VMEM((tokens, 128), F32),
            pltpu.VMEM((tokens, 128), F32),
            pltpu.VMEM((keys, 128), F32),
            pltpu.VMEM((keys, 128), F32),
        ],
        cost_estimate=pl.CostEstimate(
            flops=20 * 256 * 128 * sum(tiles),
            bytes_accessed=6000000,
            transcendentals=256 * sum(tiles),
        ),
        name="attend_back",
    )(table, q, k_own, v_own, k_other, v_other, cot, att, log_in)


def front_kernel(place, *refs):
    front_body(place, refs[:PIECES], *refs[PIECES:])


def front_body(
    place,
    pieces,
    gain,
    shift,
    qkv,
    bias_joint,
    cosine,
    sine_a,
    sine_b,
    fc1_own,
    fc1_other,
    bias1,
    normed,
    mean,
    inv,
    queries,
    keys,
    values,
    sent,
    pre,
    active,
):
    sides = sides_of(place)
    rows = [
        part.astype(F32)
        for part in piece_rows(pl.program_id(0), pieces)
    ]
    center = sum(jnp.sum(part, axis=-1, keepdims=True) for part in rows) / D
    rows = [part - center for part in rows]
    spread_ = sum(jnp.sum(part * part, axis=-1, keepdims=True) for part in rows) / D
    inv_std = lax.rsqrt(spread_ + epsilon)
    mean[...] = jnp.broadcast_to(center, mean.shape)
    inv[...] = jnp.broadcast_to(inv_std, inv.shape)
    for part, side in zip(rows, sides):
        normed[:, side] = (part * inv_std * gain[:, side] + shift[:, side]).astype(BF)
    normed16 = normed[...]
    joint = dot(normed16, qkv[...], 1, 0) + bias_joint[...]
    tables = (cosine[...], sine_a[...], sine_b[...])
    queries[...] = turn(joint[:, :BLK], *tables).astype(BF)
    turned, value = turn(joint[:, BLK : 2 * BLK], *tables), joint[:, 2 * BLK :]
    keys[...] = turned.astype(BF)
    values[...] = value.astype(BF)
    sent[0] = pltpu.roll(turned, HD, 1).astype(BF)
    sent[1] = pltpu.roll(value, HD, 1).astype(BF)
    hidden = fc1_own.shape[1]
    for part, weight in enumerate((fc1_own, fc1_other)):
        columns = slice(part * hidden, (part + 1) * hidden)
        result = dot(normed16, weight[...], 1, 0) + bias1[:, columns]
        pre[:, columns] = result
        inner = jnp.tanh(inner_coef * (result + cubic_coef * result * result * result))
        active[:, columns] = (0.5 * result * (1.0 + inner)).astype(BF)


def front(place, pieces, gain, shift, qkv, bias_joint, cosine, sine_a, sine_b, fc1_own, fc1_other, bias1):
    tokens = LO * BLK
    hidden = fc1_own.shape[1]

    def shape(columns, dtype):
        return jax.ShapeDtypeStruct((tokens, columns), dtype)

    narrow = rows_spec(BLK)
    return pl.pallas_call(
        front_kernel,
        grid=(tokens // STEP,),
        out_shape=(
            shape(D, BF),
            shape(BLK, F32),
            shape(BLK, F32),
            shape(BLK, BF),
            shape(BLK, BF),
            shape(BLK, BF),
            jax.ShapeDtypeStruct((2, tokens, BLK), BF),
            shape(2 * hidden, F32),
            shape(2 * hidden, BF),
        ),
        in_specs=[
            scalar_spec(),
            *piece_specs(),
            fixed_spec(1, D),
            fixed_spec(1, D),
            fixed_spec(D, 3 * BLK),
            fixed_spec(1, 3 * BLK),
            narrow,
            narrow,
            narrow,
            fixed_spec(D, hidden),
            fixed_spec(D, hidden),
            fixed_spec(1, 2 * hidden),
        ],
        out_specs=(
            rows_spec(D),
            narrow,
            narrow,
            narrow,
            narrow,
            narrow,
            pl.BlockSpec((2, STEP, BLK), lambda i: (0, i, 0)),
            rows_spec(2 * hidden),
            rows_spec(2 * hidden),
        ),
        cost_estimate=cost(2 * tokens * D * (384 + 2 * hidden), 12 * tokens * D // 2),
        name="front",
    )(
        place,
        *pieces,
        gain,
        shift,
        qkv,
        bias_joint,
        cosine,
        sine_a,
        sine_b,
        fc1_own,
        fc1_other,
        bias1,
    )


def store_pieces(step, index, rows, a_own, a_other, b_near, b_far):
    for s in range(2):
        (a_own, a_other)[index][s] = rows[s * BLK : s * BLK + HALF]
    for wanted, target in ((step < 2, b_near), (step >= 2, b_far)):

        @pl.when(wanted)
        def _(target=target):
            for s in range(2):
                target[s, index] = rows[s * BLK + HALF : (s + 1) * BLK]


def partial_shapes():
    return (
        jax.ShapeDtypeStruct((LO, HALF, UNIT), BF),
        jax.ShapeDtypeStruct((LO, HALF, UNIT), BF),
        jax.ShapeDtypeStruct((LO // 2, 2, HALF, UNIT), BF),
        jax.ShapeDtypeStruct((LO // 2, 2, HALF, UNIT), BF),
    )


def partial_specs():
    near = pl.BlockSpec((2, HALF, UNIT), lambda i: (i, 0, 0))
    return (
        near,
        near,
        pl.BlockSpec((2, 2, HALF, UNIT), lambda i: (jnp.minimum(i, 1), 0, 0, 0)),
        pl.BlockSpec((2, 2, HALF, UNIT), lambda i: (jnp.maximum(i - 2, 0), 0, 0, 0)),
    )


def mix_kernel(place, attended, active, out2, fc2_own, fc2_other, *partial):
    hidden = fc2_own.shape[1]
    for index, side in enumerate((place[0], 1 - place[0])):
        parts = []
        for quarter in range(4):
            c = 4 * side + quarter
            parts.append(
                (
                    dot(active[:, :hidden], fc2_own[c], 1, 0)
                    + dot(active[:, hidden:], fc2_other[c], 1, 0)
                    + dot(attended[...], out2[c], 1, 0)
                ).astype(BF)
            )
        store_pieces(pl.program_id(0), index, jnp.concatenate(parts, axis=1), *partial)


def mix(place, attended, active, out2, fc2_own, fc2_other):
    tokens = LO * BLK
    hidden = fc2_own.shape[1]
    return pl.pallas_call(
        mix_kernel,
        grid=(tokens // STEP,),
        out_shape=partial_shapes(),
        in_specs=[
            scalar_spec(),
            rows_spec(BLK),
            rows_spec(2 * hidden),
            fixed_spec(LO, BLK, 256),
            fixed_spec(LO, hidden, 256),
            fixed_spec(LO, hidden, 256),
        ],
        out_specs=partial_specs(),
        cost_estimate=cost(2 * tokens * D * (128 + 2 * hidden), 8000000),
        name="mix",
    )(place, attended, active, out2, fc2_own, fc2_other)


def back_kernel(place, *refs):
    back_body(place, refs[:PIECES], *refs[PIECES:])


def back_body(
    place,
    pieces,
    pre,
    out2,
    fc2_own,
    fc2_other,
    cot,
    grad_pre,
    grad_attended,
    bias_sum,
):
    @pl.when(pl.program_id(0) == 0)
    def _():
        bias_sum[...] = jnp.zeros_like(bias_sum)

    parts = piece_rows(pl.program_id(0), pieces)
    for part, side in zip(parts, sides_of(place)):
        cot[:, side] = part
    rows = cot[...]
    hidden = fc2_own.shape[1]

    def through(weight):
        total = 0.0
        for c in range(LO):
            total = total + dot(rows[:, c * 256 : (c + 1) * 256], weight[c], 1, 1)
        return total

    grad_attended[...] = through(out2).astype(BF)
    for part, weight in enumerate((fc2_own, fc2_other)):
        columns = slice(part * hidden, (part + 1) * hidden)
        value = pre[:, columns]
        inner = jnp.tanh(inner_coef * (value + cubic_coef * value * value * value))
        slope = 0.5 * (1.0 + inner) + 0.5 * value * (1.0 - inner * inner) * inner_coef * (
            1.0 + 3.0 * cubic_coef * value * value
        )
        grad = through(weight) * slope
        bias_sum[:, columns] += jnp.sum(grad, axis=0, keepdims=True)
        grad_pre[:, columns] = grad.astype(BF)


def back(place, pieces, pre, out2, fc2_own, fc2_other):
    tokens = LO * BLK
    hidden = fc2_own.shape[1]
    return pl.pallas_call(
        back_kernel,
        grid=(tokens // STEP,),
        out_shape=(
            jax.ShapeDtypeStruct((tokens, D), BF),
            jax.ShapeDtypeStruct((tokens, 2 * hidden), BF),
            jax.ShapeDtypeStruct((tokens, BLK), BF),
            jax.ShapeDtypeStruct((1, 2 * hidden), F32),
        ),
        in_specs=[
            scalar_spec(),
            *piece_specs(),
            rows_spec(2 * hidden),
            fixed_spec(LO, BLK, 256),
            fixed_spec(LO, hidden, 256),
            fixed_spec(LO, hidden, 256),
        ],
        out_specs=(
            rows_spec(D),
            rows_spec(2 * hidden),
            rows_spec(BLK),
            fixed_spec(1, 2 * hidden),
        ),
        cost_estimate=cost(2 * tokens * D * (128 + 2 * hidden), 14000000),
        name="back",
    )(place, *pieces, pre, out2, fc2_own, fc2_other)


def unturn_kernel(dq, dk, dv, got, cosine, sine_a, sine_b, joint, own, other, bias):
    tables = (cosine[...], -sine_a[...], -sine_b[...])
    dk_all = dk[...] + got[0].astype(F32)
    dv_all = dv[...] + got[1].astype(F32)
    for j, grads in enumerate((turn(dq[...], *tables), turn(dk_all, *tables), dv_all)):
        columns = slice(j * BLK, (j + 1) * BLK)
        bias[:, columns] = jnp.sum(grads, axis=0, keepdims=True)
        grads = grads.astype(BF)
        joint[:, columns] = grads
        own[:, j * HD : (j + 1) * HD] = grads[:, :HD]
        other[:, j * HD : (j + 1) * HD] = grads[:, HD:]


def unturn(dq, dk, dv, got, cosine, sine_a, sine_b):
    tokens = dq.shape[0]
    return pl.pallas_call(
        unturn_kernel,
        out_shape=(
            jax.ShapeDtypeStruct((tokens, 3 * BLK), BF),
            jax.ShapeDtypeStruct((tokens, 3 * HD), BF),
            jax.ShapeDtypeStruct((tokens, 3 * HD), BF),
            jax.ShapeDtypeStruct((1, 3 * BLK), F32),
        ),
        in_specs=full_spec(7),
        out_specs=tuple(full_spec(4)),
        cost_estimate=cost(0, 6000000),
        name="unturn",
    )(dq, dk, dv, got, cosine, sine_a, sine_b)


def grad_kernel(place, *refs):
    grad_body(place, refs[:PIECES], *refs[PIECES:])


def grad_body(
    place,
    pieces,
    mean,
    inv,
    gain,
    joint,
    grad_pre,
    qkv,
    fc1_own,
    fc1_other,
    a_own,
    a_other,
    b_near,
    b_far,
    sums,
    gain_sum,
    shift_sum,
):
    step = pl.program_id(0)

    @pl.when(step == 0)
    def _():
        gain_sum[...] = jnp.zeros_like(gain_sum)
        shift_sum[...] = jnp.zeros_like(shift_sum)

    hidden = fc1_own.shape[1]
    parts = piece_rows(step, pieces)
    first, second = 0.0, 0.0
    for index, (side, part) in enumerate(zip(sides_of(place), parts)):
        grads = (
            dot(joint[...], qkv[side, :], 1, 1)
            + dot(grad_pre[:, :hidden], fc1_own[side, :], 1, 1)
            + dot(grad_pre[:, hidden:], fc1_other[side, :], 1, 1)
        )
        store_pieces(step, index, grads.astype(BF), a_own, a_other, b_near, b_far)
        both = grads * ((part.astype(F32) - mean[:, :1]) * inv[:, :1])
        shift_sum[index : index + 1, :] += jnp.sum(grads, axis=0, keepdims=True)
        gain_sum[index : index + 1, :] += jnp.sum(both, axis=0, keepdims=True)
        first = first + jnp.sum(grads * gain[:, side], axis=-1, keepdims=True)
        second = second + jnp.sum(both * gain[:, side], axis=-1, keepdims=True)
    lane = lax.broadcasted_iota(jnp.int32, (STEP, BLK), 1)
    turned = jnp.transpose(jnp.where(lane < HD, first, second))
    sums[0:1, :] = turned[0:1]
    sums[1:2, :] = turned[HD : HD + 1]


def grad_units(place, pieces, mean, inv, gain, joint, grad_pre, qkv, fc1_own, fc1_other):
    tokens = LO * BLK
    hidden = fc1_own.shape[1]
    return pl.pallas_call(
        grad_kernel,
        grid=(tokens // STEP,),
        out_shape=(
            *partial_shapes(),
            jax.ShapeDtypeStruct((2, tokens), F32),
            jax.ShapeDtypeStruct((2, UNIT), F32),
            jax.ShapeDtypeStruct((2, UNIT), F32),
        ),
        in_specs=[
            scalar_spec(),
            *piece_specs(),
            rows_spec(BLK),
            rows_spec(BLK),
            fixed_spec(1, D),
            rows_spec(3 * BLK),
            rows_spec(2 * hidden),
            fixed_spec(D, 3 * BLK),
            fixed_spec(D, hidden),
            fixed_spec(D, hidden),
        ],
        out_specs=(
            *partial_specs(),
            pl.BlockSpec((2, STEP), lambda i: (0, i)),
            fixed_spec(2, UNIT),
            fixed_spec(2, UNIT),
        ),
        cost_estimate=cost(2 * tokens * D * (384 + 2 * hidden), 16000000),
        name="grad",
    )(place, *pieces, mean, inv, gain, joint, grad_pre, qkv, fc1_own, fc1_other)


def step_body(
    n_hi,
    layer_input,
    norm_gain,
    norm_shift,
    w_qkv,
    b_qkv,
    w_out,
    b_out,
    w_fc1,
    b_fc1,
    w_fc2,
    b_fc2,
    grad_output,
    placement,
    position_ids,
):
    hi, y, k = (lax.axis_index(name) for name in ("hi", "y", "k"))
    lo = lax.axis_index(LOX)
    depth = D // (n_hi * LO)
    width = w_qkv.shape[2]
    hidden = w_fc1.shape[1] // LO
    tokens = LO * BLK

    def half(values, which):
        split = values.reshape((2, 2, HALF) + values.shape[1:])
        cut = lax.dynamic_index_in_dim(split, which, 1, keepdims=False)
        return cut.reshape((BLK,) + values.shape[1:])

    def in_order(index, own, got, axis):
        return jnp.where(
            index == 0,
            jnp.concatenate([own, got], axis=axis),
            jnp.concatenate([got, own], axis=axis),
        )

    def make_unit(values):
        got = swap(half(values, 1 - k), "k")
        return in_order(k, half(values, k), got, 1)

    unit_in = make_unit(layer_input)
    pieces = gather_pieces(unit_in)
    unit_cot = make_unit(grad_output)
    pieces_cot = gather_pieces(unit_cot)
    slot_lo = [lo ^ (((s & 1) << 2) | (s & 2) | (s >> 2)) for s in range(LO)]
    place = jnp.stack([y, k] + slot_lo).astype(jnp.int32)

    def over_hi(values):
        return values[None] if n_hi == 1 else lax.all_gather(values, "hi", axis=0)

    def ordered(got, shape):
        return got if n_hi == 1 else jnp.moveaxis(got, 1, 0).reshape(shape)

    down = jnp.concatenate(
        [w_fc2.reshape(LO, hidden, depth), w_out.reshape(LO, HD, depth)], axis=1
    )
    down = spread(jnp.moveaxis(over_hi(down), 0, 1))
    if n_hi == 1:
        down_own = down.reshape(LO, hidden + HD, 256)
    else:
        down_own = down.transpose(2, 1, 0, 3).reshape(hidden + HD, LO, 256).transpose(1, 0, 2)
    down_other = swap(down_own, "k")
    fc2_own, fc2_other = down_own[:, :hidden], down_other[:, :hidden]
    out2 = jnp.concatenate([down_own[:, hidden:], down_other[:, hidden:]], axis=1)
    if n_hi == 1:
        ids = half(position_ids, k)
        ids = jnp.stack([ids // BLK, ids % BLK]).astype(BF)
        ids = jnp.pad(ids, ((0, IDS - 2), (0, BLK)))
        first_own = spread(pack_first(w_fc1, w_qkv.transpose(1, 0, 2), ids))
        fc1_own, fc1_other, qkv = join_first(first_own, swap(first_own, "k"))
        ids = first_own[:, 3 * BLK + HALF : 3 * BLK + HALF + 2, :BLK].astype(jnp.int32)
        ids = ids[:, 0] * BLK + ids[:, 1]
        ids = jnp.stack([lax.dynamic_index_in_dim(ids, c, 0, keepdims=False) for c in slot_lo])
    else:
        fc1_own = spread(over_hi(w_fc1).reshape(n_hi, depth, LO, hidden).transpose(2, 0, 1, 3))
        fc1_own = ordered(fc1_own, (D, hidden)).reshape(D, hidden)
        fc1_other = swap(fc1_own, "k")
        ids = half(position_ids, k)
        for name in ("zh", "zl", "x"):
            ids = jnp.stack([ids, swap(ids, name)])
        cut = over_hi(w_qkv).reshape(n_hi, depth, 3, LO, HD).transpose(3, 0, 1, 2, 4)
        heads_own = spread(cut.reshape(LO, n_hi, depth, 3 * HD))
        heads_own = ordered(heads_own, (D, 3, HD))
        qkv = jnp.concatenate([heads_own, swap(heads_own, "k")], axis=2).reshape(D, 6 * HD)

    own_head = lax.dynamic_slice_in_dim(b_qkv, lo * HD, HD, 1)
    own_bias1 = lax.dynamic_slice_in_dim(b_fc1, lo * hidden, hidden, 0)
    affine = jnp.stack([norm_gain.astype(F32), norm_shift.astype(F32)])
    small = jnp.concatenate([affine.reshape(-1), own_head.reshape(-1), own_bias1])
    small_other = swap(small, "k")
    affine = in_order(k, affine, small_other[: 2 * width].reshape(2, width), 1)
    affine = in_order(y, affine, swap(affine, "y"), 1)
    gain, shift = affine[0:1], affine[1:2]
    head_other = small_other[2 * width : 2 * width + 3 * HD].reshape(3, HD)
    bias_joint = jnp.concatenate([own_head, head_other], axis=1).reshape(1, 6 * HD)
    bias1 = jnp.concatenate([own_bias1, small_other[2 * width + 3 * HD :]])[None]

    ids = ids.reshape(tokens)
    lane = jnp.arange(BLK, dtype=jnp.int32) % HD
    frequency = 10000.0 ** (-2.0 * (lane % (ROT // 2)).astype(F32) / ROT)
    angles = ids.astype(F32)[:, None] * frequency[None, :]
    cosine = jnp.where(lane < ROT, jnp.cos(angles), 1.0)
    sine = jnp.sin(angles)
    sine_a = jnp.where(lane < ROT // 2, -sine, 0.0)
    sine_b = jnp.where((lane >= ROT // 2) & (lane < ROT), sine, 0.0)

    blocks = n_hi * 2 * LO
    by_group = placement.reshape(n_hi, LO, 2)
    in_slots = jnp.stack(
        [lax.dynamic_index_in_dim(by_group, c, 1, keepdims=False) for c in slot_lo], axis=1
    ).reshape(n_hi, 2 * LO)
    local = lax.dynamic_index_in_dim(in_slots, hi, 0, keepdims=False)
    ranks = jnp.sum((local[None, :] < local[:, None]).astype(jnp.int32), axis=1)
    sorted_local = jnp.sort(local) if n_hi > 1 else jnp.arange(2 * LO, dtype=jnp.int32)
    table = jnp.concatenate(
        [k[None].astype(jnp.int32), in_slots.reshape(-1), ranks, sorted_local]
    )
    if n_hi == 1:
        tiles = tuple(4 * BLK * (m // 2 + 1) for m in range(LO))
    else:
        tiles = (blocks * BLK,) * LO

    normed16, mean, inv, queries, keys, values, sent, pre, active = front(
        place,
        pieces,
        gain,
        shift,
        qkv,
        bias_joint,
        cosine,
        sine_a,
        sine_b,
        fc1_own,
        fc1_other,
        bias1,
    )
    other_kv = swap(sent, "k")

    def all_keys(rows):
        return rows if n_hi == 1 else lax.all_gather(rows, "hi", axis=0, tiled=True)

    key_set = tuple(all_keys(v) for v in (keys, values, other_kv[0], other_kv[1]))
    attended, log_total = attend(tiles, blocks, table, queries, *key_set)
    summed = scatter_pieces(*mix(place, attended, active, out2, fc2_own, fc2_other))

    cot, grad_pre, grad_attended, term_bias1 = back(
        place, pieces_cot, pre, out2, fc2_own, fc2_other
    )

    def summed_dot(left, own, other, flip):
        def product(right):
            return dot(right, left, 0, 0) if flip else dot(left, right, 0, 0)

        return product(own), swap(product(other).astype(BF), "k")

    def home(total):
        got = spread(total)
        if n_hi == 1:
            return got[:, 0]
        return lax.psum_scatter(got.astype(F32), "hi", scatter_dimension=1)

    def add(own, got):
        return (own + got.astype(F32)).astype(BF)

    def cut_columns(values):
        rows = values.shape[0]
        return values.reshape(rows, n_hi, LO, depth).transpose(2, 1, 0, 3)

    fc2_sum = add(*summed_dot(cot, active[:, :hidden], active[:, hidden:], True))
    out_sum = add(*summed_dot(cot, attended[:, :HD], attended[:, HD:], True))
    down = jnp.concatenate([cut_columns(fc2_sum), cut_columns(out_sum)], axis=2)
    fc1_term, fc1_got = summed_dot(normed16, grad_pre[:, :hidden], grad_pre[:, hidden:], False)
    if n_hi == 1:
        grad_attended, down, fc1_term, fc1_got = lax.optimization_barrier(
            (grad_attended, down, fc1_term, fc1_got)
        )
    down_home = home(down)
    grad_fc2 = down_home[:, :hidden].reshape(LO * hidden, depth).astype(F32)
    grad_out = down_home[:, hidden:].reshape(LO * HD, depth).astype(F32)

    dq, dk, dv, grads_sent = attend_back(
        tiles, blocks, table, queries, *key_set, grad_attended, attended, log_total
    )

    def own_keys(rows):
        if n_hi == 1:
            return rows
        return lax.psum_scatter(rows, "hi", scatter_dimension=0, tiled=True)

    got = swap(grads_sent, "k")
    if n_hi > 1:
        dk = own_keys(dk + got[0].astype(F32))
        dv = own_keys(dv + got[1].astype(F32))
        got = jnp.zeros((2,) + dk.shape, BF)
    joint, joint_own, joint_other, term_joint_bias = unturn(
        dq, dk, dv, got, cosine, sine_a, sine_b
    )
    own_term, got_term = summed_dot(normed16, joint_own, joint_other, False)
    if n_hi == 1:
        packed = pack_grads(fc1_term, fc1_got, own_term, got_term)
        packed, joint = lax.optimization_barrier((packed, joint))
        grad_fc1, grad_qkv = home_grads(spread(packed))
        grad_qkv = grad_qkv.transpose(1, 0, 2)
    else:
        fc1_sum = add(fc1_term, fc1_got).reshape(n_hi, LO, depth, hidden)
        fc1_home = home(fc1_sum.transpose(1, 0, 2, 3))
        grad_fc1 = fc1_home.transpose(1, 0, 2).reshape(depth, LO * hidden).astype(F32)
        qkv_sum = add(own_term, got_term).reshape(n_hi, LO, depth, 3 * HD)
        qkv_home = home(qkv_sum.transpose(1, 0, 2, 3)).reshape(LO, depth, 3, HD)
        grad_qkv = qkv_home.transpose(1, 2, 0, 3).reshape(depth, 3, width).astype(F32)
    *partial, row_sums, gain_sum, shift_sum = grad_units(
        place, pieces, mean, inv, gain, joint, grad_pre, qkv, fc1_own, fc1_other
    )
    grad_unit = scatter_pieces(*partial)

    heads = lax.dynamic_update_slice(
        jnp.zeros((2, 3, width), F32),
        term_joint_bias.reshape(3, 2, HD).transpose(1, 0, 2),
        (0, 0, lo * HD),
    )
    bias_sum = lax.dynamic_update_slice(
        jnp.zeros((2, LO * hidden), F32), term_bias1.reshape(2, hidden), (0, lo * hidden)
    )
    affine_sum = jnp.stack([gain_sum, shift_sum]).reshape(2, 2, 2, width).transpose(1, 2, 0, 3)

    def pick(values, index):
        return lax.dynamic_index_in_dim(values, index, 0, keepdims=False)

    row_pair = row_sums.reshape(-1)
    over_y = jnp.concatenate([affine_sum[1].reshape(-1), row_pair])
    over_y = swap(over_y, "y")
    affine_sum = affine_sum[0] + over_y[: 4 * width].reshape(2, 2, width)
    row_pair = (row_pair + over_y[4 * width :]).reshape(2, tokens)
    over_k = jnp.concatenate(
        [heads[1].reshape(-1), bias_sum[1], pick(affine_sum, 1 - k).reshape(-1)]
    )
    over_k = swap(over_k, "k") + jnp.concatenate(
        [heads[0].reshape(-1), bias_sum[0], pick(affine_sum, k).reshape(-1)]
    )
    local_bias = jnp.sum(grad_output.astype(F32), axis=0)
    flat = jnp.concatenate([over_k, local_bias])
    length = flat.shape[0]
    for name in ("x", "zl", "zh"):
        left = row_pair.shape[1] // 2
        got = swap(jnp.concatenate([flat, row_pair[:, left:].reshape(-1)]), name)
        flat = flat + got[:length]
        row_pair = row_pair[:, :left] + got[length:].reshape(2, left)
    row_own = row_pair.T / D
    if n_hi > 1:
        flat = lax.psum(flat, "hi")
    cuts = [3 * width, LO * hidden, width, width, width]
    ends = [sum(cuts[: i + 1]) for i in range(len(cuts))]
    grad_b_qkv = flat[: ends[0]].reshape(3, width)
    grad_b_fc1 = flat[ends[0] : ends[1]]
    grad_gain = flat[ends[1] : ends[2]]
    grad_shift = flat[ends[2] : ends[3]]
    grad_b_out = flat[ends[3] :]

    def to_rows(unit):
        parts = unit.reshape(BLK, 2, width)
        own = lax.dynamic_index_in_dim(parts, k, 1, keepdims=False)
        got = swap(lax.dynamic_index_in_dim(parts, 1 - k, 1, keepdims=False), "k")
        own, got = own.reshape(2, 1, HALF, width), got.reshape(2, 1, HALF, width)
        return in_order(k, own, got, 1).reshape(2 * BLK, width)

    layer_output = layer_input.astype(F32) + to_rows(summed) + b_out + b_fc2

    mean_own, inv_own = mean[:BLK, :1], inv[:BLK, :1]
    gain_own = lax.dynamic_slice_in_dim(gain, y * UNIT, UNIT, 1)
    normed_unit = (unit_in.astype(F32) - mean_own) * inv_own
    grad_x = inv_own * (
        grad_unit * gain_own - row_own[:, :1] - normed_unit * row_own[:, 1:]
    )
    grad_input = to_rows(grad_x + unit_cot.astype(F32))
    return (
        layer_output,
        grad_input,
        grad_gain,
        grad_shift,
        grad_qkv,
        grad_b_qkv,
        grad_out,
        grad_b_out,
        grad_fc1,
        grad_b_fc1,
        grad_fc2,
        grad_b_out,
    )


def on_device(n_hi, *arguments):
    return step_body(n_hi, *arguments)


def solution(mesh):
    n_hi = mesh.shape["ctx"] // LO
    inner = Mesh(mesh.devices.reshape(n_hi, 2, 2, 2, 2, 2), CTX + TP)
    in_specs = (
        P(CTX, TP),
        P(TP),
        P(TP),
        P(CTX, None, TP),
        P(None, TP),
        P(TP, CTX),
        P(TP),
        P(CTX, TP),
        P(TP),
        P(TP, CTX),
        P(TP),
        P(CTX, TP),
        P(),
        P(CTX),
    )
    out_specs = (
        P(CTX, TP),
        P(CTX, TP),
        P(TP),
        P(TP),
        P(CTX, None, TP),
        P(None, TP),
        P(TP, CTX),
        P(TP),
        P(CTX, TP),
        P(TP),
        P(TP, CTX),
        P(TP),
    )
    return jax.shard_map(
        functools.partial(on_device, n_hi),
        mesh=inner,
        in_specs=in_specs,
        out_specs=out_specs,
        check_vma=False,
    )
```
